128 devices in a mesh: gx: 16 (over z, y_lo, core), gy: 8 (over x, y_hi).
Axes of the slice: x: 4, y: 4 (y_hi: 2, y_lo: 2; y = y_hi * 2 + y_lo), z: 4, core: 2. Of those that a mesh axis runs over, the one named last changes fastest.
Arguments:
- velocity: float32 [3, 4096, 1024], P(None, 'gx', 'gy'), may hold values from 0.4 to 1.6
- adjoint_seed: float32 [3, 4096, 1024], P(None, 'gx', 'gy'), may hold values from -6 to 6
- courant: float32 [3, 4096, 1024], P(None, 'gx', 'gy'), may hold values from 0.1 to 0.45
- viscosity: float32 [3, 4096, 1024], P(None, 'gx', 'gy'), may hold values from 0.02 to 0.1
- turbine_tile: int32 [512, 1], P(('gx', 'gy')), may hold values from 0 to 127; in each aligned block of 512 rows (0 to 511, 512 to 1023, ...) at most 12 rows name the same one
- turbine_offset: int32 [512, 2], P(('gx', 'gy')), may hold values from 0 to 64
- thrust: float32 [512], P(('gx', 'gy')), may hold values from 0.5 to 2
- disk_width: float32 [512], P(('gx', 'gy')), may hold values from 8 to 16
Outputs:
- adjoint_start: float32 [3, 4096, 1024], P(None, 'gx', 'gy')
- thrust_grad: float32 [512], P(('gx', 'gy'))
The draws below stay inside these ranges and needn't reach their ends.
Inputs may be any that keep to these rules, and one draw needn't show every extreme that they name: `turbine_tile`: each turbine's tile is the index along gx times the number of devices of gy plus the index along gy of the device whose cells hold its footprint. No tile holds more than 12 turbines, and some tile holds exactly 12.
All inputs are finite; a program needn't handle non-finite values.
Results may differ from the reference program's by a relative error of at most 0.00002.
Values sent between devices are 32-bit elements; how exact they have to be, the bound alone decides.
A program may use at most 128 MiB of HBM per device.

```python
import math
import jax
import jax.numpy as jnp
import numpy as np
from jax import lax

LEV = 3
CX = 256
CY = 128
STEPS = 8
FP = 64
MOST = 12
NX = 4096
NY = 1024
TURBINES = 512
N_GY = 8
DEVICES = 128


def plant(result, key, least, top_value):
    spot = [jax.random.randint(jax.random.fold_in(key, axis), (), 0, length) for axis, length in enumerate(result.shape)]
    widest = result.shape.index(max(result.shape))
    neighbour = spot[:widest] + [(spot[widest] + 1) % result.shape[widest]] + spot[widest + 1:]
    return result.at[tuple(spot)].set(least).at[tuple(neighbour)].set(top_value)


def block_levels(rng, dims, shards, least, largest):
    def one(axis_at, parts):
        steps = jax.random.uniform(jax.random.fold_in(jax.random.fold_in(rng, 6), axis_at), (parts,), jnp.float32, least / len(shards), largest / len(shards))
        return jnp.repeat(jnp.exp(steps), dims[axis_at] // parts).reshape((-1,) + (1,) * (len(dims) - axis_at - 1))

    gain = one(*shards[0])
    for cut in shards[1:]:
        gain = gain * one(*cut)
    return gain


def routed_block(key, own, number, rows, amount, top, most, lean):
    order = jax.random.permutation(key, amount)
    crowded, ordinary = portions_of(amount, rows * top, most, lean, True), portions_of(amount, rows * top, most, lean, False)
    places = jnp.arange(amount)

    def named(lengths, offset_by):
        used = int((lengths > 0).sum())
        fixed = max(1, used // 4)
        passed = fixed + (places - fixed + offset_by * (used - fixed)) % max(1, amount - fixed)
        return jnp.zeros((amount,), jnp.int32).at[order[jnp.where(places < fixed, places, passed)]].set(jnp.asarray(lengths, jnp.int32))

    lengths = jnp.where(number % 4 == 0, named(crowded, number // 4), named(ordinary, number - number // 4 - 1))
    mixed = jax.random.permutation(jax.random.fold_in(own, 3), amount)
    donor, sink = mixed[0:amount // 2 * 2:2], mixed[1:amount // 2 * 2:2]
    margin = jnp.minimum(lengths[donor] - 1, most - lengths[sink]) // 2
    margin = jnp.where((donor == order[0]) | (sink == order[0]) | (lengths[sink] == 0), 0, jnp.maximum(margin, 0))
    passed = jax.random.randint(jax.random.fold_in(own, 4), (amount // 2,), 0, 1 << 20) % (margin + 1)
    lengths = lengths.at[donor].add(-passed).at[sink].add(passed)
    items = jnp.searchsorted(jnp.cumsum(lengths), jnp.arange(rows * top), side="right").astype(jnp.int32)
    table = items.reshape(top, rows).T
    table = table[jax.random.permutation(jax.random.fold_in(own, 1), rows)]
    offset_by = jax.random.randint(jax.random.fold_in(own, 2), (rows, 1), 0, top)
    return jnp.take_along_axis(table, (jnp.arange(top)[None, :] + offset_by) % top, axis=1)


def portions_of(amount, total, limit, skew, full):
    portions = [(1 << 20) // math.isqrt(standing ** skew) + 1 for standing in range(1, amount + 1)]
    largest = limit if full else min(limit, max(-(-total // amount), total * portions[0] // sum(portions)))
    least = 1 if total - largest >= amount - 1 else 0
    counts, rest = [largest] + [least] * (amount - 1), total - largest - least * (amount - 1)
    while rest > 0:
        movable = [i for i in range(1, amount) if counts[i] < largest] or [i for i in range(1, amount) if counts[i] < limit]
        whole, budget = sum([portions[i] for i in movable]), rest
        for i in movable:
            extra = min(limit - counts[i], max(1, budget * portions[i] // whole), rest)
            counts[i] = counts[i] + extra
            rest = rest - extra
    return np.array(counts)


def gaussian(stream_key, shape, width, reach, cuts=(), kind=jnp.bfloat16):
    drawn = jax.random.normal(stream_key, shape, jnp.float32) * width
    if len(cuts) > 0:
        drawn = block_levels(stream_key, shape, cuts, -0.22, 0.18) * drawn
    return jnp.clip(drawn, min=-reach, max=reach).astype(kind)


def setup_inputs(seed: int = 0) -> dict:
    key_of = jax.random.split(jax.random.key(seed), 9)
    velocity = jnp.clip(0.4 + 1.2 * jax.random.uniform(key_of[0], (LEV, NX, NY), jnp.float32) ** block_levels(key_of[0], (LEV, NX, NY), ((1, 16), (2, 8)), -0.2, 0.2), 0.4, 1.6)
    adjoint_seed = gaussian(key_of[1], (LEV, NX, NY), 1.0, 6.0, ((1, 16), (2, 8)), jnp.float32)
    courant = jnp.clip(0.1 + 0.35 * jax.random.uniform(key_of[2], (LEV, NX, NY), jnp.float32) ** block_levels(key_of[2], (LEV, NX, NY), ((1, 16), (2, 8)), -0.2, 0.2), 0.1, 0.45)
    viscosity = jnp.clip(0.02 + 0.08 * jax.random.uniform(key_of[3], (LEV, NX, NY), jnp.float32) ** block_levels(key_of[3], (LEV, NX, NY), ((1, 16), (2, 8)), -0.2, 0.2), 0.02, 0.1)
    turbine_tile_keys = jax.random.split(jax.random.fold_in(key_of[4], 1), TURBINES // TURBINES)
    turbine_tile_turns = jax.random.permutation(jax.random.fold_in(key_of[4], 3), TURBINES // TURBINES)
    turbine_tile = jax.vmap(lambda own, number: routed_block(jax.random.fold_in(key_of[4], 2), own, number, TURBINES, DEVICES, 1, MOST, 2))(turbine_tile_keys, turbine_tile_turns).reshape((TURBINES, 1))
    turbine_offset = plant(jax.random.randint(key_of[5], (TURBINES, 2), 0, min(CX, CY) - FP + 1), jax.random.fold_in(key_of[5], 1), 0, min(CX, CY) - FP).astype(jnp.int32)
    thrust = jnp.clip(jnp.exp(math.log(2.0) - 1.3862944 * jax.random.uniform(key_of[6], (TURBINES,), jnp.float32) ** block_levels(key_of[6], (TURBINES,), ((0, 128),), -0.2, 0.2)), 0.5, 2.0)
    disk_width = jnp.clip(jnp.exp(math.log(16.0) - 0.6931472 * jax.random.uniform(key_of[7], (TURBINES,), jnp.float32) ** block_levels(key_of[7], (TURBINES,), ((0, 128),), -0.2, 0.2)), 8.0, 16.0)
    return dict(velocity=velocity, adjoint_seed=adjoint_seed, courant=courant, viscosity=viscosity, turbine_tile=turbine_tile, turbine_offset=turbine_offset, thrust=thrust, disk_width=disk_width)


VERTICAL_MIX = 0.05
DRAG_SCALE = 0.01

def drag_law(state):
    return state * jnp.sqrt(state * state + 1.0)

def drag_slope(state):
    square_one = state * state + 1.0
    return (square_one + state * state) / jnp.sqrt(square_one)

def vertical(center):
    zero_row = jnp.zeros_like(center[:1])
    from_above = jnp.concatenate([center[1:] - center[:-1], zero_row], axis=0)
    from_below = jnp.concatenate([zero_row, center[:-1] - center[1:]], axis=0)
    return from_above + from_below

def advance(padded, advect, diffuse, drag_coef):
    center = padded[:, 1:-1, 1:-1]
    upwind = padded[:, :-2, 1:-1]
    downwind = padded[:, 2:, 1:-1]
    left_cell = padded[:, 1:-1, :-2]
    right_cell = padded[:, 1:-1, 2:]
    return center + advect * (upwind - center) + diffuse * (downwind + upwind + right_cell + left_cell - 4.0 * center) + VERTICAL_MIX * vertical(center) - drag_coef * drag_law(center)

def retreat(padded, advect_ext, diffuse_ext, drag_coef, state):
    flux_adv = advect_ext * padded
    flux_dif = diffuse_ext * padded
    center = padded[:, 1:-1, 1:-1]
    return center - flux_adv[:, 1:-1, 1:-1] - 4.0 * flux_dif[:, 1:-1, 1:-1] + flux_adv[:, 2:, 1:-1] + (flux_dif[:, 2:, 1:-1] + flux_dif[:, :-2, 1:-1] + flux_dif[:, 1:-1, 2:] + flux_dif[:, 1:-1, :-2]) + VERTICAL_MIX * vertical(center) - drag_coef * drag_slope(state) * center

def footprint(disk_width):
    cell_pos = jnp.arange(FP, dtype=jnp.float32) - (FP - 1) / 2.0
    profile = jnp.exp(-(cell_pos[None, :] * cell_pos[None, :]) / (2.0 * disk_width[:, None] * disk_width[:, None]))
    level_pos = jnp.arange(LEV, dtype=jnp.float32) - (LEV - 1) / 2.0
    level_gain = DRAG_SCALE * jnp.exp(-0.5 * level_pos * level_pos)
    return level_gain[None, :, None, None] * profile[:, None, :, None] * profile[:, None, None, :]

def wrap_pad(array):
    return jnp.pad(array, ((0, 0), (1, 1), (1, 1)), mode='wrap')

def reference(velocity, adjoint_seed, courant, viscosity, turbine_tile, turbine_offset, thrust, disk_width):
    tile_ids = turbine_tile[:, 0]
    row_start = (tile_ids // N_GY * CX + turbine_offset[:, 0]).astype(jnp.int32)
    col_start = (tile_ids % N_GY * CY + turbine_offset[:, 1]).astype(jnp.int32)
    kernels = footprint(disk_width)

    def add_turbine(turbine, field_now):
        corner = (jnp.int32(0), row_start[turbine], col_start[turbine])
        block_vals = lax.dynamic_slice(field_now, corner, (LEV, FP, FP))
        return lax.dynamic_update_slice(field_now, block_vals + thrust[turbine] * kernels[turbine], corner)
    drag_field = lax.fori_loop(0, TURBINES, add_turbine, jnp.zeros((LEV, NX, NY), jnp.float32))
    states = []
    state = velocity
    for step_index in range(STEPS):
        states.append(state)
        if step_index + 1 < STEPS:
            state = advance(wrap_pad(state), courant, viscosity, drag_field)
    advect_ext = wrap_pad(courant)
    diffuse_ext = wrap_pad(viscosity)
    adjoint = adjoint_seed
    sensitivity = jnp.zeros((LEV, NX, NY), jnp.float32)
    for step_index in reversed(range(STEPS)):
        sensitivity = sensitivity - adjoint * drag_law(states[step_index])
        adjoint = retreat(wrap_pad(adjoint), advect_ext, diffuse_ext, drag_field, states[step_index])

    def turbine_total(turbine):
        corner = (jnp.int32(0), row_start[turbine], col_start[turbine])
        block_vals = lax.dynamic_slice(sensitivity, corner, (LEV, FP, FP))
        return jnp.sum(kernels[turbine] * block_vals)
    totals = lax.map(turbine_total, jnp.arange(TURBINES, dtype=jnp.int32))
    return (adjoint, thrust * totals)
```

```python
import jax
import jax.numpy as jnp
from jax import lax
from jax.sharding import PartitionSpec as P

LEV = 3
STEPS = 8
FP = 64
MARGIN = 2 * (STEPS - 1)

VERTICAL_MIX = 0.05
DRAG_SCALE = 0.01
HIGHEST = lax.Precision.HIGHEST


def exchange(block, width):
    for axis, dim in (("gx", 1), ("gy", 2)):
        count = lax.axis_size(axis)
        forward = [(i, (i + 1) % count) for i in range(count)]
        backward = [((i + 1) % count, i) for i in range(count)]
        low = lax.ppermute(
            lax.slice_in_dim(block, block.shape[dim] - width, None, axis=dim), axis, forward
        )
        high = lax.ppermute(lax.slice_in_dim(block, 0, width, axis=dim), axis, backward)
        block = jnp.concatenate([low, block, high], axis=dim)
    return block


def drag_law(state):
    return state * jnp.sqrt(state * state + 1.0)


def drag_slope(state):
    square_one = state * state + 1.0
    return (square_one + state * state) / jnp.sqrt(square_one)


def vertical(center):
    zero_row = jnp.zeros_like(center[:1])
    from_above = jnp.concatenate([center[1:] - center[:-1], zero_row], axis=0)
    from_below = jnp.concatenate([zero_row, center[:-1] - center[1:]], axis=0)
    return from_above + from_below


def advance(padded, advect, diffuse, drag_coef):
    center = padded[:, 1:-1, 1:-1]
    upwind = padded[:, :-2, 1:-1]
    downwind = padded[:, 2:, 1:-1]
    left_cell = padded[:, 1:-1, :-2]
    right_cell = padded[:, 1:-1, 2:]
    return (
        center
        + advect * (upwind - center)
        + diffuse * (downwind + upwind + right_cell + left_cell - 4.0 * center)
        + VERTICAL_MIX * vertical(center)
        - drag_coef * drag_law(center)
    )


def retreat(padded, advect_ext, diffuse_ext, drag_coef, state):
    flux_adv = advect_ext * padded
    flux_dif = diffuse_ext * padded
    center = padded[:, 1:-1, 1:-1]
    return (
        center
        - flux_adv[:, 1:-1, 1:-1]
        - 4.0 * flux_dif[:, 1:-1, 1:-1]
        + flux_adv[:, 2:, 1:-1]
        + (
            flux_dif[:, 2:, 1:-1]
            + flux_dif[:, :-2, 1:-1]
            + flux_dif[:, 1:-1, 2:]
            + flux_dif[:, 1:-1, :-2]
        )
        + VERTICAL_MIX * vertical(center)
        - drag_coef * drag_slope(state) * center
    )


def trim(array, margin, wanted):
    excess = margin - wanted
    if excess == 0:
        return array
    return array[:, excess:-excess, excess:-excess]


def profiles(first, starts, widths, period, length):
    pos = (first + jnp.arange(length, dtype=jnp.int32)[None, :] - starts[:, None]) % period
    cell_pos = pos.astype(jnp.float32) - (FP - 1) / 2.0
    profile = jnp.exp(-(cell_pos * cell_pos) / (2.0 * widths[:, None] * widths[:, None]))
    return jnp.where(pos < FP, profile, 0.0)


def level_gain():
    level_pos = jnp.arange(LEV, dtype=jnp.float32) - (LEV - 1) / 2.0
    return DRAG_SCALE * jnp.exp(-0.5 * level_pos * level_pos)


def shards(
    velocity, adjoint_seed, courant, viscosity, turbine_tile, turbine_offset, thrust, disk_width
):
    levels, rows, cols = velocity.shape
    n_gx = lax.axis_size("gx")
    n_gy = lax.axis_size("gy")
    m = MARGIN
    info = jnp.concatenate(
        [
            turbine_tile.astype(jnp.float32),
            turbine_offset.astype(jnp.float32),
            thrust[:, None],
            disk_width[:, None],
        ],
        axis=1,
    )
    info = lax.all_gather(info, ("gx", "gy"), axis=0, tiled=True)
    tiles = info[:, 0].astype(jnp.int32)
    row_start = tiles // n_gy * rows + info[:, 1].astype(jnp.int32)
    col_start = tiles % n_gy * cols + info[:, 2].astype(jnp.int32)
    thrusts = info[:, 3]
    widths = info[:, 4]
    gx = lax.axis_index("gx")
    gy = lax.axis_index("gy")
    prof_r = profiles(gx * rows - m, row_start, widths, n_gx * rows, rows + 2 * m)
    prof_c = profiles(gy * cols - m, col_start, widths, n_gy * cols, cols + 2 * m)
    gain = level_gain()
    plane = jnp.einsum("kr,kc->rc", thrusts[:, None] * prof_r, prof_c, precision=HIGHEST)
    drag = gain[:, None, None] * plane[None]

    ext = exchange(jnp.concatenate([velocity, courant, viscosity, adjoint_seed], axis=0), m)
    advect_all = ext[levels : 2 * levels]
    diffuse_all = ext[2 * levels : 3 * levels]

    state = ext[:levels]
    margin = m
    states = [(state, margin)]
    for _ in range(STEPS - 1):
        margin = margin - 1
        state = advance(
            state, trim(advect_all, m, margin), trim(diffuse_all, m, margin), trim(drag, m, margin)
        )
        states.append((state, margin))

    adjoint = trim(ext[3 * levels :], m, STEPS)
    sensitivity = jnp.zeros_like(velocity)
    for step_index in reversed(range(STEPS)):
        stored, stored_margin = states[step_index]
        sensitivity = sensitivity - trim(adjoint, step_index + 1, 0) * drag_law(
            trim(stored, stored_margin, 0)
        )
        adjoint = retreat(
            adjoint,
            trim(advect_all, m, step_index + 1),
            trim(diffuse_all, m, step_index + 1),
            trim(drag, m, step_index),
            trim(stored, stored_margin, step_index),
        )

    weighted = jnp.einsum("l,lrc->rc", gain, sensitivity, precision=HIGHEST)
    own_r = prof_r[:, m : m + rows]
    own_c = prof_c[:, m : m + cols]
    across = jnp.einsum("rc,kc->kr", weighted, own_c, precision=HIGHEST)
    totals = jnp.sum(own_r * across, axis=1)
    values = thrusts * totals
    grad = lax.psum_scatter(values, ("gx", "gy"), scatter_dimension=0, tiled=True)
    return adjoint, grad


def solution(mesh):
    placed = (
        P(None, "gx", "gy"),
        P(None, "gx", "gy"),
        P(None, "gx", "gy"),
        P(None, "gx", "gy"),
        P(("gx", "gy"), None),
        P(("gx", "gy"), None),
        P(("gx", "gy")),
        P(("gx", "gy")),
    )
    return jax.shard_map(
        shards,
        mesh=mesh,
        in_specs=placed,
        out_specs=(P(None, "gx", "gy"), P(("gx", "gy"))),
        check_vma=False,
    )
```

```python
import functools

import jax
import jax.numpy as jnp
from jax import lax
from jax.experimental import pallas as pl
from jax.experimental.pallas import tpu as pltpu
from jax.sharding import PartitionSpec as P

LEV = 3
STEPS = 8
FP = 64
MARGIN = 2 * (STEPS - 1)

VERTICAL_MIX = 0.05
DRAG_SCALE = 0.01
HIGHEST = lax.Precision.HIGHEST


MESH_ID = pl.DeviceIdType.MESH


def fan_kernel(n_gy, n_dev, gather, src_ref, out_ref, slots, send_sem, recv_sem, local_sem):
    gx = lax.axis_index("gx")
    gy = lax.axis_index("gy")
    me = gx * n_gy + gy
    own = src_ref if gather else src_ref.at[me]
    local = pltpu.make_async_copy(own, slots.at[me], local_sem)
    local.start()
    for step in range(1, n_dev):
        target = lax.rem(me + step, n_dev)
        block = src_ref if gather else src_ref.at[target]
        pltpu.make_async_remote_copy(
            block,
            slots.at[me],
            send_sem,
            recv_sem,
            device_id=(target // n_gy, target % n_gy),
            device_id_type=MESH_ID,
        ).start()
    local.wait()
    first = lax.rem(me + 1, n_dev)
    rest = pl.ds(0, n_dev - 1)
    every = pltpu.make_async_remote_copy(
        slots.at[rest],
        slots.at[rest],
        send_sem,
        recv_sem,
        device_id=(first // n_gy, first % n_gy),
        device_id_type=MESH_ID,
    )
    every.wait_send()
    every.wait_recv()
    if gather:
        out_ref[...] = slots[...]
    else:
        out_ref[...] = jnp.sum(slots[...], axis=0)


def fan(block, gather):
    n_gy = lax.axis_size("gy")
    n_dev = lax.axis_size("gx") * n_gy
    tile = block.shape[-2:]
    out_shape = (n_dev,) + tile if gather else tile
    return pl.pallas_call(
        functools.partial(fan_kernel, n_gy, n_dev, gather),
        out_shape=jax.ShapeDtypeStruct(out_shape, jnp.float32),
        in_specs=[pl.BlockSpec(memory_space=pltpu.VMEM)],
        out_specs=pl.BlockSpec(memory_space=pltpu.VMEM),
        scratch_shapes=[
            pltpu.VMEM((n_dev,) + tile, jnp.float32),
            pltpu.SemaphoreType.DMA,
            pltpu.SemaphoreType.DMA,
            pltpu.SemaphoreType.DMA,
        ],
        compiler_params=pltpu.CompilerParams(has_side_effects=True),
    )(block)


def exchange(block, width):
    for axis, dim in (("gx", 1), ("gy", 2)):
        count = lax.axis_size(axis)
        forward = [(i, (i + 1) % count) for i in range(count)]
        backward = [((i + 1) % count, i) for i in range(count)]
        low = lax.ppermute(
            lax.slice_in_dim(block, block.shape[dim] - width, None, axis=dim), axis, forward
        )
        high = lax.ppermute(lax.slice_in_dim(block, 0, width, axis=dim), axis, backward)
        block = jnp.concatenate([low, block, high], axis=dim)
    return block


def drag_law(state):
    return state * jnp.sqrt(state * state + 1.0)


def drag_slope(state):
    square_one = state * state + 1.0
    return (square_one + state * state) / jnp.sqrt(square_one)


def vertical(center):
    zero_row = jnp.zeros_like(center[:1])
    from_above = jnp.concatenate([center[1:] - center[:-1], zero_row], axis=0)
    from_below = jnp.concatenate([zero_row, center[:-1] - center[1:]], axis=0)
    return from_above + from_below


def advance(padded, advect, diffuse, drag_coef):
    center = padded[:, 1:-1, 1:-1]
    upwind = padded[:, :-2, 1:-1]
    downwind = padded[:, 2:, 1:-1]
    left_cell = padded[:, 1:-1, :-2]
    right_cell = padded[:, 1:-1, 2:]
    return (
        center
        + advect * (upwind - center)
        + diffuse * (downwind + upwind + right_cell + left_cell - 4.0 * center)
        + VERTICAL_MIX * vertical(center)
        - drag_coef * drag_law(center)
    )


def retreat(padded, advect_ext, diffuse_ext, drag_coef, state):
    flux_adv = advect_ext * padded
    flux_dif = diffuse_ext * padded
    center = padded[:, 1:-1, 1:-1]
    return (
        center
        - flux_adv[:, 1:-1, 1:-1]
        - 4.0 * flux_dif[:, 1:-1, 1:-1]
        + flux_adv[:, 2:, 1:-1]
        + (
            flux_dif[:, 2:, 1:-1]
            + flux_dif[:, :-2, 1:-1]
            + flux_dif[:, 1:-1, 2:]
            + flux_dif[:, 1:-1, :-2]
        )
        + VERTICAL_MIX * vertical(center)
        - drag_coef * drag_slope(state) * center
    )


def trim(array, margin, wanted):
    excess = margin - wanted
    if excess == 0:
        return array
    return array[:, excess:-excess, excess:-excess]


def profiles(first, starts, widths, period, length):
    pos = (first + jnp.arange(length, dtype=jnp.int32)[None, :] - starts[:, None]) % period
    cell_pos = pos.astype(jnp.float32) - (FP - 1) / 2.0
    profile = jnp.exp(-(cell_pos * cell_pos) / (2.0 * widths[:, None] * widths[:, None]))
    return jnp.where(pos < FP, profile, 0.0)


def level_gain():
    level_pos = jnp.arange(LEV, dtype=jnp.float32) - (LEV - 1) / 2.0
    return DRAG_SCALE * jnp.exp(-0.5 * level_pos * level_pos)


def shards(
    velocity, adjoint_seed, courant, viscosity, turbine_tile, turbine_offset, thrust, disk_width
):
    levels, rows, cols = velocity.shape
    n_gx = lax.axis_size("gx")
    n_gy = lax.axis_size("gy")
    m = MARGIN
    info = jnp.concatenate(
        [
            turbine_tile.astype(jnp.float32),
            turbine_offset.astype(jnp.float32),
            thrust[:, None],
            disk_width[:, None],
        ],
        axis=1,
    )
    per = info.shape[0]
    packed = jnp.zeros((8, 128), jnp.float32).at[0, : info.size].set(info.reshape(-1))
    info = fan(packed, True)[:, 0, : info.size].reshape(-1, info.shape[1])
    tiles = info[:, 0].astype(jnp.int32)
    row_start = tiles // n_gy * rows + info[:, 1].astype(jnp.int32)
    col_start = tiles % n_gy * cols + info[:, 2].astype(jnp.int32)
    thrusts = info[:, 3]
    widths = info[:, 4]
    gx = lax.axis_index("gx")
    gy = lax.axis_index("gy")
    prof_r = profiles(gx * rows - m, row_start, widths, n_gx * rows, rows + 2 * m)
    prof_c = profiles(gy * cols - m, col_start, widths, n_gy * cols, cols + 2 * m)
    gain = level_gain()
    plane = jnp.einsum("kr,kc->rc", thrusts[:, None] * prof_r, prof_c, precision=HIGHEST)
    drag = gain[:, None, None] * plane[None]

    ext = exchange(jnp.concatenate([velocity, courant, viscosity, adjoint_seed], axis=0), m)
    advect_all = ext[levels : 2 * levels]
    diffuse_all = ext[2 * levels : 3 * levels]

    state = ext[:levels]
    margin = m
    states = [(state, margin)]
    for _ in range(STEPS - 1):
        margin = margin - 1
        state = advance(
            state, trim(advect_all, m, margin), trim(diffuse_all, m, margin), trim(drag, m, margin)
        )
        states.append((state, margin))

    adjoint = trim(ext[3 * levels :], m, STEPS)
    sensitivity = jnp.zeros_like(velocity)
    for step_index in reversed(range(STEPS)):
        stored, stored_margin = states[step_index]
        sensitivity = sensitivity - trim(adjoint, step_index + 1, 0) * drag_law(
            trim(stored, stored_margin, 0)
        )
        adjoint = retreat(
            adjoint,
            trim(advect_all, m, step_index + 1),
            trim(diffuse_all, m, step_index + 1),
            trim(drag, m, step_index),
            trim(stored, stored_margin, step_index),
        )

    weighted = jnp.einsum("l,lrc->rc", gain, sensitivity, precision=HIGHEST)
    own_r = prof_r[:, m : m + rows]
    own_c = prof_c[:, m : m + cols]
    across = jnp.einsum("rc,kc->kr", weighted, own_c, precision=HIGHEST)
    totals = jnp.sum(own_r * across, axis=1)
    values = thrusts * totals
    spread = jnp.zeros((values.shape[0] // per, 8, 128), jnp.float32)
    spread = spread.at[:, 0, :per].set(values.reshape(-1, per))
    grad = fan(spread, False)[0, :per]
    return adjoint, grad


def solution(mesh):
    placed = (
        P(None, "gx", "gy"),
        P(None, "gx", "gy"),
        P(None, "gx", "gy"),
        P(None, "gx", "gy"),
        P(("gx", "gy"), None),
        P(("gx", "gy"), None),
        P(("gx", "gy")),
        P(("gx", "gy")),
    )
    return jax.shard_map(
        shards,
        mesh=mesh,
        in_specs=placed,
        out_specs=(P(None, "gx", "gy"), P(("gx", "gy"))),
        check_vma=False,
    )
```

```python
import functools

import jax
import jax.numpy as jnp
from jax import lax
from jax.experimental import pallas as pl
from jax.experimental.pallas import tpu as pltpu
from jax.sharding import PartitionSpec as P

LEV = 3
STEPS = 8
FP = 64
MARGIN = 2 * (STEPS - 1)

VERTICAL_MIX = 0.05
DRAG_SCALE = 0.01
HIGHEST = lax.Precision.HIGHEST


MESH_ID = pl.DeviceIdType.MESH


HALO_MOVES = ((1, 0), (-1, 0), (0, 1), (0, -1), (1, 1), (1, -1), (-1, 1), (-1, -1))


def spread_rows(n_gy, n_dev, me, src_of, slots, send_sem, recv_sem):
    for step in range(1, n_dev):
        target = lax.rem(me + step, n_dev)
        pltpu.make_async_remote_copy(
            src_of(target),
            slots.at[pl.ds(me, 1)],
            send_sem,
            recv_sem,
            device_id=(target // n_gy, target % n_gy),
            device_id_type=MESH_ID,
        ).start()
    first = lax.rem(me + 1, n_dev)
    rest = pl.ds(0, n_dev - 1)
    return pltpu.make_async_remote_copy(
        slots.at[rest],
        slots.at[rest],
        send_sem,
        recv_sem,
        device_id=(first // n_gy, first % n_gy),
        device_id_type=MESH_ID,
    )


def open_kernel(n_gx, n_gy, *refs):
    n_dev = n_gx * n_gy
    n_halo = len(HALO_MOVES)
    info_ref = refs[0]
    pieces = refs[1 : 1 + n_halo]
    gathered = refs[1 + n_halo]
    landed = refs[2 + n_halo : 2 + 2 * n_halo]
    slots, send_sem, recv_sem, local_sem, halo_send, halo_recv = refs[2 + 2 * n_halo :]
    gx = lax.axis_index("gx")
    gy = lax.axis_index("gy")
    me = gx * n_gy + gy
    local = pltpu.make_async_copy(info_ref, slots.at[pl.ds(me, 1)], local_sem)
    local.start()
    halo = []
    for index, (dx, dy) in enumerate(HALO_MOVES):
        copy = pltpu.make_async_remote_copy(
            pieces[index],
            landed[index],
            halo_send.at[index],
            halo_recv.at[index],
            device_id=(lax.rem(gx + dx + n_gx, n_gx), lax.rem(gy + dy + n_gy, n_gy)),
            device_id_type=MESH_ID,
        )
        copy.start()
        halo.append(copy)
    every = spread_rows(n_gy, n_dev, me, lambda target: info_ref, slots, send_sem, recv_sem)
    local.wait()
    for copy in halo:
        copy.wait()
    every.wait_send()
    every.wait_recv()
    gathered[...] = slots[...]


def open_exchange(info_row, pieces):
    n_gx = lax.axis_size("gx")
    n_gy = lax.axis_size("gy")
    n_dev = n_gx * n_gy
    vmem = pl.BlockSpec(memory_space=pltpu.VMEM)
    out_shape = [jax.ShapeDtypeStruct((n_dev, info_row.shape[1]), jnp.float32)] + [
        jax.ShapeDtypeStruct(piece.shape, piece.dtype) for piece in pieces
    ]
    return pl.pallas_call(
        functools.partial(open_kernel, n_gx, n_gy),
        out_shape=out_shape,
        in_specs=[vmem] * (1 + len(pieces)),
        out_specs=[vmem] * len(out_shape),
        scratch_shapes=[
            pltpu.VMEM((n_dev, info_row.shape[1]), jnp.float32),
            pltpu.SemaphoreType.DMA,
            pltpu.SemaphoreType.DMA,
            pltpu.SemaphoreType.DMA,
            pltpu.SemaphoreType.DMA((len(pieces),)),
            pltpu.SemaphoreType.DMA((len(pieces),)),
        ],
        compiler_params=pltpu.CompilerParams(has_side_effects=True),
    )(info_row, *pieces)


def close_kernel(n_gy, n_dev, src_ref, out_ref, slots, send_sem, recv_sem, local_sem):
    gx = lax.axis_index("gx")
    gy = lax.axis_index("gy")
    me = gx * n_gy + gy
    local = pltpu.make_async_copy(src_ref.at[pl.ds(me, 1)], slots.at[pl.ds(me, 1)], local_sem)
    local.start()
    every = spread_rows(
        n_gy, n_dev, me, lambda target: src_ref.at[pl.ds(target, 1)], slots, send_sem, recv_sem
    )
    local.wait()
    every.wait_send()
    every.wait_recv()
    out_ref[...] = jnp.sum(slots[...], axis=0, keepdims=True)


def close_scatter(rows):
    n_gy = lax.axis_size("gy")
    n_dev = lax.axis_size("gx") * n_gy
    vmem = pl.BlockSpec(memory_space=pltpu.VMEM)
    return pl.pallas_call(
        functools.partial(close_kernel, n_gy, n_dev),
        out_shape=jax.ShapeDtypeStruct((1, rows.shape[1]), jnp.float32),
        in_specs=[vmem],
        out_specs=vmem,
        scratch_shapes=[
            pltpu.VMEM(rows.shape, jnp.float32),
            pltpu.SemaphoreType.DMA,
            pltpu.SemaphoreType.DMA,
            pltpu.SemaphoreType.DMA,
        ],
        compiler_params=pltpu.CompilerParams(has_side_effects=True),
    )(rows)


def halo_pieces(block, m):
    last_r, first_r = block[:, -m:, :], block[:, :m, :]
    return (
        last_r,
        first_r,
        block[:, :, -m:],
        block[:, :, :m],
        last_r[:, :, -m:],
        last_r[:, :, :m],
        first_r[:, :, -m:],
        first_r[:, :, :m],
    )


def assemble(block, landed):
    row_low, row_high, col_low, col_high, c_ll, c_lh, c_hl, c_hh = landed
    top = jnp.concatenate([c_ll, row_low, c_lh], axis=2)
    middle = jnp.concatenate([col_low, block, col_high], axis=2)
    bottom = jnp.concatenate([c_hl, row_high, c_hh], axis=2)
    return jnp.concatenate([top, middle, bottom], axis=1)


def drag_law(state):
    return state * jnp.sqrt(state * state + 1.0)


def drag_slope(state):
    square_one = state * state + 1.0
    return (square_one + state * state) / jnp.sqrt(square_one)


def vertical(center):
    zero_row = jnp.zeros_like(center[:1])
    from_above = jnp.concatenate([center[1:] - center[:-1], zero_row], axis=0)
    from_below = jnp.concatenate([zero_row, center[:-1] - center[1:]], axis=0)
    return from_above + from_below


def advance(padded, advect, diffuse, drag_coef):
    center = padded[:, 1:-1, 1:-1]
    upwind = padded[:, :-2, 1:-1]
    downwind = padded[:, 2:, 1:-1]
    left_cell = padded[:, 1:-1, :-2]
    right_cell = padded[:, 1:-1, 2:]
    return (
        center
        + advect * (upwind - center)
        + diffuse * (downwind + upwind + right_cell + left_cell - 4.0 * center)
        + VERTICAL_MIX * vertical(center)
        - drag_coef * drag_law(center)
    )


def retreat(padded, advect_ext, diffuse_ext, drag_coef, state):
    flux_adv = advect_ext * padded
    flux_dif = diffuse_ext * padded
    center = padded[:, 1:-1, 1:-1]
    return (
        center
        - flux_adv[:, 1:-1, 1:-1]
        - 4.0 * flux_dif[:, 1:-1, 1:-1]
        + flux_adv[:, 2:, 1:-1]
        + (
            flux_dif[:, 2:, 1:-1]
            + flux_dif[:, :-2, 1:-1]
            + flux_dif[:, 1:-1, 2:]
            + flux_dif[:, 1:-1, :-2]
        )
        + VERTICAL_MIX * vertical(center)
        - drag_coef * drag_slope(state) * center
    )


def trim(array, margin, wanted):
    excess = margin - wanted
    if excess == 0:
        return array
    return array[:, excess:-excess, excess:-excess]


def profiles(first, starts, widths, period, length):
    pos = (first + jnp.arange(length, dtype=jnp.int32)[None, :] - starts[:, None]) % period
    cell_pos = pos.astype(jnp.float32) - (FP - 1) / 2.0
    profile = jnp.exp(-(cell_pos * cell_pos) / (2.0 * widths[:, None] * widths[:, None]))
    return jnp.where(pos < FP, profile, 0.0)


def level_gain():
    level_pos = jnp.arange(LEV, dtype=jnp.float32) - (LEV - 1) / 2.0
    return DRAG_SCALE * jnp.exp(-0.5 * level_pos * level_pos)


def shards(
    velocity, adjoint_seed, courant, viscosity, turbine_tile, turbine_offset, thrust, disk_width
):
    levels, rows, cols = velocity.shape
    n_gx = lax.axis_size("gx")
    n_gy = lax.axis_size("gy")
    m = MARGIN
    info = jnp.concatenate(
        [
            turbine_tile.astype(jnp.float32),
            turbine_offset.astype(jnp.float32),
            thrust[:, None],
            disk_width[:, None],
        ],
        axis=1,
    )
    per = info.shape[0]
    info_row = jnp.zeros((1, 128), jnp.float32).at[0, : info.size].set(info.reshape(-1))
    stack = jnp.concatenate([velocity, courant, viscosity, adjoint_seed], axis=0)
    opened = open_exchange(info_row, halo_pieces(stack, m))
    info = opened[0][:, : info.size].reshape(-1, info.shape[1])
    ext = assemble(stack, opened[1:])
    tiles = info[:, 0].astype(jnp.int32)
    row_start = tiles // n_gy * rows + info[:, 1].astype(jnp.int32)
    col_start = tiles % n_gy * cols + info[:, 2].astype(jnp.int32)
    thrusts = info[:, 3]
    widths = info[:, 4]
    gx = lax.axis_index("gx")
    gy = lax.axis_index("gy")
    prof_r = profiles(gx * rows - m, row_start, widths, n_gx * rows, rows + 2 * m)
    prof_c = profiles(gy * cols - m, col_start, widths, n_gy * cols, cols + 2 * m)
    gain = level_gain()
    plane = jnp.einsum("kr,kc->rc", thrusts[:, None] * prof_r, prof_c, precision=HIGHEST)
    drag = gain[:, None, None] * plane[None]

    advect_all = ext[levels : 2 * levels]
    diffuse_all = ext[2 * levels : 3 * levels]

    state = ext[:levels]
    margin = m
    states = [(state, margin)]
    for _ in range(STEPS - 1):
        margin = margin - 1
        state = advance(
            state, trim(advect_all, m, margin), trim(diffuse_all, m, margin), trim(drag, m, margin)
        )
        states.append((state, margin))

    adjoint = trim(ext[3 * levels :], m, STEPS)
    sensitivity = jnp.zeros_like(velocity)
    for step_index in reversed(range(STEPS)):
        stored, stored_margin = states[step_index]
        sensitivity = sensitivity - trim(adjoint, step_index + 1, 0) * drag_law(
            trim(stored, stored_margin, 0)
        )
        adjoint = retreat(
            adjoint,
            trim(advect_all, m, step_index + 1),
            trim(diffuse_all, m, step_index + 1),
            trim(drag, m, step_index),
            trim(stored, stored_margin, step_index),
        )

    weighted = jnp.einsum("l,lrc->rc", gain, sensitivity, precision=HIGHEST)
    own_r = prof_r[:, m : m + rows]
    own_c = prof_c[:, m : m + cols]
    across = jnp.einsum("rc,kc->kr", weighted, own_c, precision=HIGHEST)
    totals = jnp.sum(own_r * across, axis=1)
    values = thrusts * totals
    spread = jnp.zeros((values.shape[0] // per, 128), jnp.float32)
    spread = spread.at[:, :per].set(values.reshape(-1, per))
    grad = close_scatter(spread)[0, :per]
    return adjoint, grad


def solution(mesh):
    placed = (
        P(None, "gx", "gy"),
        P(None, "gx", "gy"),
        P(None, "gx", "gy"),
        P(None, "gx", "gy"),
        P(("gx", "gy"), None),
        P(("gx", "gy"), None),
        P(("gx", "gy")),
        P(("gx", "gy")),
    )
    return jax.shard_map(
        shards,
        mesh=mesh,
        in_specs=placed,
        out_specs=(P(None, "gx", "gy"), P(("gx", "gy"))),
        check_vma=False,
    )
```

```python
import functools

import jax
import jax.numpy as jnp
from jax import lax
from jax.experimental import pallas as pl
from jax.experimental.pallas import tpu as pltpu
from jax.sharding import PartitionSpec as P

LEV = 3
STEPS = 8
FP = 64
MARGIN = 2 * (STEPS - 1)

VERTICAL_MIX = 0.05
DRAG_SCALE = 0.01
HIGHEST = lax.Precision.HIGHEST


MESH_ID = pl.DeviceIdType.MESH


HALO_MOVES = ((1, 0), (-1, 0), (0, 1), (0, -1), (1, 1), (1, -1), (-1, 1), (-1, -1))


def spread_rows(n_gy, n_dev, me, src_of, slots, send_sem, recv_sem):
    for step in range(1, n_dev):
        target = lax.rem(me + step, n_dev)
        pltpu.make_async_remote_copy(
            src_of(target),
            slots.at[pl.ds(me, 1)],
            send_sem,
            recv_sem,
            device_id=(target // n_gy, target % n_gy),
            device_id_type=MESH_ID,
        ).start()
    first = lax.rem(me + 1, n_dev)
    rest = pl.ds(0, n_dev - 1)
    return pltpu.make_async_remote_copy(
        slots.at[rest],
        slots.at[rest],
        send_sem,
        recv_sem,
        device_id=(first // n_gy, first % n_gy),
        device_id_type=MESH_ID,
    )


def open_kernel(n_gx, n_gy, *refs):
    n_dev = n_gx * n_gy
    n_halo = len(HALO_MOVES)
    info_ref = refs[0]
    pieces = refs[1 : 1 + n_halo]
    gathered = refs[1 + n_halo]
    landed = refs[2 + n_halo : 2 + 2 * n_halo]
    slots, send_sem, recv_sem, local_sem, halo_send, halo_recv = refs[2 + 2 * n_halo :]
    gx = lax.axis_index("gx")
    gy = lax.axis_index("gy")
    me = gx * n_gy + gy
    local = pltpu.make_async_copy(info_ref, slots.at[pl.ds(me, 1)], local_sem)
    local.start()
    halo = []
    for index, (dx, dy) in enumerate(HALO_MOVES):
        copy = pltpu.make_async_remote_copy(
            pieces[index],
            landed[index],
            halo_send.at[index],
            halo_recv.at[index],
            device_id=(lax.rem(gx + dx + n_gx, n_gx), lax.rem(gy + dy + n_gy, n_gy)),
            device_id_type=MESH_ID,
        )
        copy.start()
        halo.append(copy)
    every = spread_rows(n_gy, n_dev, me, lambda target: info_ref, slots, send_sem, recv_sem)
    local.wait()
    for copy in halo:
        copy.wait()
    every.wait_send()
    every.wait_recv()
    gathered[...] = slots[...]


def open_exchange(info_row, pieces):
    n_gx = lax.axis_size("gx")
    n_gy = lax.axis_size("gy")
    n_dev = n_gx * n_gy
    vmem = pl.BlockSpec(memory_space=pltpu.VMEM)
    out_shape = [jax.ShapeDtypeStruct((n_dev, info_row.shape[1]), jnp.float32)] + [
        jax.ShapeDtypeStruct(piece.shape, piece.dtype) for piece in pieces
    ]
    return pl.pallas_call(
        functools.partial(open_kernel, n_gx, n_gy),
        out_shape=out_shape,
        in_specs=[vmem] * (1 + len(pieces)),
        out_specs=[vmem] * len(out_shape),
        scratch_shapes=[
            pltpu.VMEM((n_dev, info_row.shape[1]), jnp.float32),
            pltpu.SemaphoreType.DMA,
            pltpu.SemaphoreType.DMA,
            pltpu.SemaphoreType.DMA,
            pltpu.SemaphoreType.DMA((len(pieces),)),
            pltpu.SemaphoreType.DMA((len(pieces),)),
        ],
        compiler_params=pltpu.CompilerParams(has_side_effects=True),
    )(info_row, *pieces)


def close_kernel(n_gy, n_dev, src_ref, out_ref, slots, send_sem, recv_sem, local_sem):
    gx = lax.axis_index("gx")
    gy = lax.axis_index("gy")
    me = gx * n_gy + gy
    local = pltpu.make_async_copy(src_ref.at[pl.ds(me, 1)], slots.at[pl.ds(me, 1)], local_sem)
    local.start()
    every = spread_rows(
        n_gy, n_dev, me, lambda target: src_ref.at[pl.ds(target, 1)], slots, send_sem, recv_sem
    )
    local.wait()
    every.wait_send()
    every.wait_recv()
    out_ref[...] = jnp.sum(slots[...], axis=0, keepdims=True)


def close_scatter(rows):
    n_gy = lax.axis_size("gy")
    n_dev = lax.axis_size("gx") * n_gy
    vmem = pl.BlockSpec(memory_space=pltpu.VMEM)
    return pl.pallas_call(
        functools.partial(close_kernel, n_gy, n_dev),
        out_shape=jax.ShapeDtypeStruct((1, rows.shape[1]), jnp.float32),
        in_specs=[vmem],
        out_specs=vmem,
        scratch_shapes=[
            pltpu.VMEM(rows.shape, jnp.float32),
            pltpu.SemaphoreType.DMA,
            pltpu.SemaphoreType.DMA,
            pltpu.SemaphoreType.DMA,
        ],
        compiler_params=pltpu.CompilerParams(has_side_effects=True),
    )(rows)


def halo_pieces(block, m):
    depth = block.shape[0]
    last_r, first_r = block[:, -m:, :], block[:, :m, :]
    last_c = jnp.swapaxes(block[:, :, -m:], 1, 2)
    first_c = jnp.swapaxes(block[:, :, :m], 1, 2)
    pieces = (
        last_r,
        first_r,
        last_c,
        first_c,
        last_r[:, :, -m:],
        last_r[:, :, :m],
        first_r[:, :, -m:],
        first_r[:, :, :m],
    )
    return tuple(piece.reshape(depth * m, piece.shape[2]) for piece in pieces)


def assemble(block, landed, m):
    depth = block.shape[0]
    row_low, row_high, col_low, col_high, c_ll, c_lh, c_hl, c_hh = (
        piece.reshape(depth, m, piece.shape[1]) for piece in landed
    )
    col_low = jnp.swapaxes(col_low, 1, 2)
    col_high = jnp.swapaxes(col_high, 1, 2)
    top = jnp.concatenate([c_ll, row_low, c_lh], axis=2)
    middle = jnp.concatenate([col_low, block, col_high], axis=2)
    bottom = jnp.concatenate([c_hl, row_high, c_hh], axis=2)
    return jnp.concatenate([top, middle, bottom], axis=1)


def drag_law(state):
    return state * jnp.sqrt(state * state + 1.0)


def drag_slope(state):
    square_one = state * state + 1.0
    return (square_one + state * state) / jnp.sqrt(square_one)


def vertical(center):
    zero_row = jnp.zeros_like(center[:1])
    from_above = jnp.concatenate([center[1:] - center[:-1], zero_row], axis=0)
    from_below = jnp.concatenate([zero_row, center[:-1] - center[1:]], axis=0)
    return from_above + from_below


def advance(padded, advect, diffuse, drag_coef):
    center = padded[:, 1:-1, 1:-1]
    upwind = padded[:, :-2, 1:-1]
    downwind = padded[:, 2:, 1:-1]
    left_cell = padded[:, 1:-1, :-2]
    right_cell = padded[:, 1:-1, 2:]
    return (
        center
        + advect * (upwind - center)
        + diffuse * (downwind + upwind + right_cell + left_cell - 4.0 * center)
        + VERTICAL_MIX * vertical(center)
        - drag_coef * drag_law(center)
    )


def retreat(padded, advect_ext, diffuse_ext, drag_coef, state):
    flux_adv = advect_ext * padded
    flux_dif = diffuse_ext * padded
    center = padded[:, 1:-1, 1:-1]
    return (
        center
        - flux_adv[:, 1:-1, 1:-1]
        - 4.0 * flux_dif[:, 1:-1, 1:-1]
        + flux_adv[:, 2:, 1:-1]
        + (
            flux_dif[:, 2:, 1:-1]
            + flux_dif[:, :-2, 1:-1]
            + flux_dif[:, 1:-1, 2:]
            + flux_dif[:, 1:-1, :-2]
        )
        + VERTICAL_MIX * vertical(center)
        - drag_coef * drag_slope(state) * center
    )


def trim(array, margin, wanted):
    excess = margin - wanted
    if excess == 0:
        return array
    return array[:, excess:-excess, excess:-excess]


def profiles(first, starts, widths, period, length):
    pos = (first + jnp.arange(length, dtype=jnp.int32)[None, :] - starts[:, None]) % period
    cell_pos = pos.astype(jnp.float32) - (FP - 1) / 2.0
    profile = jnp.exp(-(cell_pos * cell_pos) / (2.0 * widths[:, None] * widths[:, None]))
    return jnp.where(pos < FP, profile, 0.0)


def level_gain():
    level_pos = jnp.arange(LEV, dtype=jnp.float32) - (LEV - 1) / 2.0
    return DRAG_SCALE * jnp.exp(-0.5 * level_pos * level_pos)


def shards(
    velocity, adjoint_seed, courant, viscosity, turbine_tile, turbine_offset, thrust, disk_width
):
    levels, rows, cols = velocity.shape
    n_gx = lax.axis_size("gx")
    n_gy = lax.axis_size("gy")
    m = MARGIN
    info = jnp.concatenate(
        [
            turbine_tile.astype(jnp.float32),
            turbine_offset.astype(jnp.float32),
            thrust[:, None],
            disk_width[:, None],
        ],
        axis=1,
    )
    per = info.shape[0]
    info_row = jnp.zeros((1, 128), jnp.float32).at[0, : info.size].set(info.reshape(-1))
    stack = jnp.concatenate([velocity, courant, viscosity, adjoint_seed], axis=0)
    opened = open_exchange(info_row, halo_pieces(stack, m))
    info = opened[0][:, : info.size].reshape(-1, info.shape[1])
    ext = assemble(stack, opened[1:], m)
    tiles = info[:, 0].astype(jnp.int32)
    row_start = tiles // n_gy * rows + info[:, 1].astype(jnp.int32)
    col_start = tiles % n_gy * cols + info[:, 2].astype(jnp.int32)
    thrusts = info[:, 3]
    widths = info[:, 4]
    gx = lax.axis_index("gx")
    gy = lax.axis_index("gy")
    prof_r = profiles(gx * rows - m, row_start, widths, n_gx * rows, rows + 2 * m)
    prof_c = profiles(gy * cols - m, col_start, widths, n_gy * cols, cols + 2 * m)
    gain = level_gain()
    plane = jnp.einsum("kr,kc->rc", thrusts[:, None] * prof_r, prof_c, precision=HIGHEST)
    drag = gain[:, None, None] * plane[None]

    advect_all = ext[levels : 2 * levels]
    diffuse_all = ext[2 * levels : 3 * levels]

    state = ext[:levels]
    margin = m
    states = [(state, margin)]
    for _ in range(STEPS - 1):
        margin = margin - 1
        state = advance(
            state, trim(advect_all, m, margin), trim(diffuse_all, m, margin), trim(drag, m, margin)
        )
        states.append((state, margin))

    adjoint = trim(ext[3 * levels :], m, STEPS)
    sensitivity = jnp.zeros_like(velocity)
    for step_index in reversed(range(STEPS)):
        stored, stored_margin = states[step_index]
        sensitivity = sensitivity - trim(adjoint, step_index + 1, 0) * drag_law(
            trim(stored, stored_margin, 0)
        )
        adjoint = retreat(
            adjoint,
            trim(advect_all, m, step_index + 1),
            trim(diffuse_all, m, step_index + 1),
            trim(drag, m, step_index),
            trim(stored, stored_margin, step_index),
        )

    weighted = jnp.einsum("l,lrc->rc", gain, sensitivity, precision=HIGHEST)
    own_r = prof_r[:, m : m + rows]
    own_c = prof_c[:, m : m + cols]
    across = jnp.einsum("rc,kc->kr", weighted, own_c, precision=HIGHEST)
    totals = jnp.sum(own_r * across, axis=1)
    values = thrusts * totals
    spread = jnp.zeros((values.shape[0] // per, 128), jnp.float32)
    spread = spread.at[:, :per].set(values.reshape(-1, per))
    grad = close_scatter(spread)[0, :per]
    return adjoint, grad


def solution(mesh):
    placed = (
        P(None, "gx", "gy"),
        P(None, "gx", "gy"),
        P(None, "gx", "gy"),
        P(None, "gx", "gy"),
        P(("gx", "gy"), None),
        P(("gx", "gy"), None),
        P(("gx", "gy")),
        P(("gx", "gy")),
    )
    return jax.shard_map(
        shards,
        mesh=mesh,
        in_specs=placed,
        out_specs=(P(None, "gx", "gy"), P(("gx", "gy"))),
        check_vma=False,
    )
```

```python
import functools

import jax
import jax.numpy as jnp
from jax import lax
from jax.experimental import pallas as pl
from jax.experimental.pallas import tpu as pltpu
from jax.sharding import PartitionSpec as P

LEV = 3
STEPS = 8
FP = 64
MARGIN = 2 * (STEPS - 1)

VERTICAL_MIX = 0.05
DRAG_SCALE = 0.01
HIGHEST = lax.Precision.HIGHEST


MESH_ID = pl.DeviceIdType.MESH


HALO_MOVES = ((1, 0), (-1, 0), (0, 1), (0, -1), (1, 1), (1, -1), (-1, 1), (-1, -1))


def enter(n_gy, n_dev, me):
    barrier = pltpu.get_barrier_semaphore()
    for step in range(1, n_dev):
        target = lax.rem(me + step, n_dev)
        pl.semaphore_signal(
            barrier, inc=1, device_id=(target // n_gy, target % n_gy), device_id_type=MESH_ID
        )
    pl.semaphore_wait(barrier, n_dev - 1)


def spread_rows(n_gy, n_dev, me, src_of, slots, send_sem, recv_sem):
    for step in range(1, n_dev):
        target = lax.rem(me + step, n_dev)
        pltpu.make_async_remote_copy(
            src_of(target),
            slots.at[pl.ds(me, 1)],
            send_sem,
            recv_sem,
            device_id=(target // n_gy, target % n_gy),
            device_id_type=MESH_ID,
        ).start()
    first = lax.rem(me + 1, n_dev)
    rest = pl.ds(0, n_dev - 1)
    return pltpu.make_async_remote_copy(
        slots.at[rest],
        slots.at[rest],
        send_sem,
        recv_sem,
        device_id=(first // n_gy, first % n_gy),
        device_id_type=MESH_ID,
    )


def open_kernel(n_gx, n_gy, *refs):
    n_dev = n_gx * n_gy
    n_halo = len(HALO_MOVES)
    info_ref = refs[0]
    pieces = refs[1 : 1 + n_halo]
    gathered = refs[1 + n_halo]
    landed = refs[2 + n_halo : 2 + 2 * n_halo]
    slots, send_sem, recv_sem, local_sem, halo_send, halo_recv = refs[2 + 2 * n_halo :]
    gx = lax.axis_index("gx")
    gy = lax.axis_index("gy")
    me = gx * n_gy + gy
    enter(n_gy, n_dev, me)
    local = pltpu.make_async_copy(info_ref, slots.at[pl.ds(me, 1)], local_sem)
    local.start()
    halo = []
    for index, (dx, dy) in enumerate(HALO_MOVES):
        copy = pltpu.make_async_remote_copy(
            pieces[index],
            landed[index],
            halo_send.at[index],
            halo_recv.at[index],
            device_id=(lax.rem(gx + dx + n_gx, n_gx), lax.rem(gy + dy + n_gy, n_gy)),
            device_id_type=MESH_ID,
        )
        copy.start()
        halo.append(copy)
    every = spread_rows(n_gy, n_dev, me, lambda target: info_ref, slots, send_sem, recv_sem)
    local.wait()
    for copy in halo:
        copy.wait()
    every.wait_send()
    every.wait_recv()
    gathered[...] = slots[...]


def open_exchange(info_row, pieces):
    n_gx = lax.axis_size("gx")
    n_gy = lax.axis_size("gy")
    n_dev = n_gx * n_gy
    vmem = pl.BlockSpec(memory_space=pltpu.VMEM)
    out_shape = [jax.ShapeDtypeStruct((n_dev, info_row.shape[1]), jnp.float32)] + [
        jax.ShapeDtypeStruct(piece.shape, piece.dtype) for piece in pieces
    ]
    return pl.pallas_call(
        functools.partial(open_kernel, n_gx, n_gy),
        out_shape=out_shape,
        in_specs=[vmem] * (1 + len(pieces)),
        out_specs=[vmem] * len(out_shape),
        scratch_shapes=[
            pltpu.VMEM((n_dev, info_row.shape[1]), jnp.float32),
            pltpu.SemaphoreType.DMA,
            pltpu.SemaphoreType.DMA,
            pltpu.SemaphoreType.DMA,
            pltpu.SemaphoreType.DMA((len(pieces),)),
            pltpu.SemaphoreType.DMA((len(pieces),)),
        ],
        compiler_params=pltpu.CompilerParams(has_side_effects=True, collective_id=0),
    )(info_row, *pieces)


def close_kernel(n_gy, n_dev, src_ref, out_ref, slots, send_sem, recv_sem, local_sem):
    gx = lax.axis_index("gx")
    gy = lax.axis_index("gy")
    me = gx * n_gy + gy
    enter(n_gy, n_dev, me)
    local = pltpu.make_async_copy(src_ref.at[pl.ds(me, 1)], slots.at[pl.ds(me, 1)], local_sem)
    local.start()
    every = spread_rows(
        n_gy, n_dev, me, lambda target: src_ref.at[pl.ds(target, 1)], slots, send_sem, recv_sem
    )
    local.wait()
    every.wait_send()
    every.wait_recv()
    out_ref[...] = jnp.sum(slots[...], axis=0, keepdims=True)


def close_scatter(rows):
    n_gy = lax.axis_size("gy")
    n_dev = lax.axis_size("gx") * n_gy
    vmem = pl.BlockSpec(memory_space=pltpu.VMEM)
    return pl.pallas_call(
        functools.partial(close_kernel, n_gy, n_dev),
        out_shape=jax.ShapeDtypeStruct((1, rows.shape[1]), jnp.float32),
        in_specs=[vmem],
        out_specs=vmem,
        scratch_shapes=[
            pltpu.VMEM(rows.shape, jnp.float32),
            pltpu.SemaphoreType.DMA,
            pltpu.SemaphoreType.DMA,
            pltpu.SemaphoreType.DMA,
        ],
        compiler_params=pltpu.CompilerParams(has_side_effects=True, collective_id=1),
    )(rows)


def halo_pieces(block, m):
    depth = block.shape[0]
    last_r, first_r = block[:, -m:, :], block[:, :m, :]
    last_c = jnp.swapaxes(block[:, :, -m:], 1, 2)
    first_c = jnp.swapaxes(block[:, :, :m], 1, 2)
    pieces = (
        last_r,
        first_r,
        last_c,
        first_c,
        last_r[:, :, -m:],
        last_r[:, :, :m],
        first_r[:, :, -m:],
        first_r[:, :, :m],
    )
    return tuple(piece.reshape(depth * m, piece.shape[2]) for piece in pieces)


def assemble(block, landed, m):
    depth = block.shape[0]
    row_low, row_high, col_low, col_high, c_ll, c_lh, c_hl, c_hh = (
        piece.reshape(depth, m, piece.shape[1]) for piece in landed
    )
    col_low = jnp.swapaxes(col_low, 1, 2)
    col_high = jnp.swapaxes(col_high, 1, 2)
    top = jnp.concatenate([c_ll, row_low, c_lh], axis=2)
    middle = jnp.concatenate([col_low, block, col_high], axis=2)
    bottom = jnp.concatenate([c_hl, row_high, c_hh], axis=2)
    return jnp.concatenate([top, middle, bottom], axis=1)


def drag_law(state):
    return state * jnp.sqrt(state * state + 1.0)


def drag_slope(state):
    square_one = state * state + 1.0
    return (square_one + state * state) / jnp.sqrt(square_one)


def vertical(center):
    zero_row = jnp.zeros_like(center[:1])
    from_above = jnp.concatenate([center[1:] - center[:-1], zero_row], axis=0)
    from_below = jnp.concatenate([zero_row, center[:-1] - center[1:]], axis=0)
    return from_above + from_below


def advance(padded, advect, diffuse, drag_coef):
    center = padded[:, 1:-1, 1:-1]
    upwind = padded[:, :-2, 1:-1]
    downwind = padded[:, 2:, 1:-1]
    left_cell = padded[:, 1:-1, :-2]
    right_cell = padded[:, 1:-1, 2:]
    return (
        center
        + advect * (upwind - center)
        + diffuse * (downwind + upwind + right_cell + left_cell - 4.0 * center)
        + VERTICAL_MIX * vertical(center)
        - drag_coef * drag_law(center)
    )


def retreat(padded, advect_ext, diffuse_ext, drag_coef, state):
    flux_adv = advect_ext * padded
    flux_dif = diffuse_ext * padded
    center = padded[:, 1:-1, 1:-1]
    return (
        center
        - flux_adv[:, 1:-1, 1:-1]
        - 4.0 * flux_dif[:, 1:-1, 1:-1]
        + flux_adv[:, 2:, 1:-1]
        + (
            flux_dif[:, 2:, 1:-1]
            + flux_dif[:, :-2, 1:-1]
            + flux_dif[:, 1:-1, 2:]
            + flux_dif[:, 1:-1, :-2]
        )
        + VERTICAL_MIX * vertical(center)
        - drag_coef * drag_slope(state) * center
    )


def trim(array, margin, wanted):
    excess = margin - wanted
    if excess == 0:
        return array
    return array[:, excess:-excess, excess:-excess]


def profiles(first, starts, widths, period, length):
    pos = (first + jnp.arange(length, dtype=jnp.int32) - starts[..., None]) % period
    cell_pos = pos.astype(jnp.float32) - (FP - 1) / 2.0
    profile = jnp.exp(-(cell_pos * cell_pos) / (2.0 * widths[..., None] * widths[..., None]))
    return jnp.where(pos < FP, profile, 0.0)


def level_gain():
    level_pos = jnp.arange(LEV, dtype=jnp.float32) - (LEV - 1) / 2.0
    return DRAG_SCALE * jnp.exp(-0.5 * level_pos * level_pos)


def shards(
    velocity, adjoint_seed, courant, viscosity, turbine_tile, turbine_offset, thrust, disk_width
):
    levels, rows, cols = velocity.shape
    n_gx = lax.axis_size("gx")
    n_gy = lax.axis_size("gy")
    m = MARGIN
    per = thrust.shape[0]
    fields = (
        turbine_tile[:, 0].astype(jnp.float32),
        turbine_offset[:, 0].astype(jnp.float32),
        turbine_offset[:, 1].astype(jnp.float32),
        thrust,
        disk_width,
    )
    info_row = jnp.pad(jnp.concatenate(fields)[None, :], ((0, 0), (0, 128 - len(fields) * per)))
    stack = jnp.concatenate([velocity, courant, viscosity, adjoint_seed], axis=0)
    opened = open_exchange(info_row, halo_pieces(stack, m))
    info = opened[0]
    ext = assemble(stack, opened[1:], m)
    tiles = info[:, 0:per].astype(jnp.int32)
    row_start = tiles // n_gy * rows + info[:, per : 2 * per].astype(jnp.int32)
    col_start = tiles % n_gy * cols + info[:, 2 * per : 3 * per].astype(jnp.int32)
    thrusts = info[:, 3 * per : 4 * per]
    widths = info[:, 4 * per : 5 * per]
    gx = lax.axis_index("gx")
    gy = lax.axis_index("gy")
    prof_r = profiles(gx * rows - m, row_start, widths, n_gx * rows, rows + 2 * m)
    prof_c = profiles(gy * cols - m, col_start, widths, n_gy * cols, cols + 2 * m)
    gain = level_gain()
    plane = jnp.einsum("dkr,dkc->rc", thrusts[..., None] * prof_r, prof_c, precision=HIGHEST)
    drag = gain[:, None, None] * plane[None]

    advect_all = ext[levels : 2 * levels]
    diffuse_all = ext[2 * levels : 3 * levels]

    state = ext[:levels]
    margin = m
    states = [(state, margin)]
    for _ in range(STEPS - 1):
        margin = margin - 1
        state = advance(
            state, trim(advect_all, m, margin), trim(diffuse_all, m, margin), trim(drag, m, margin)
        )
        states.append((state, margin))

    adjoint = trim(ext[3 * levels :], m, STEPS)
    sensitivity = jnp.zeros_like(velocity)
    for step_index in reversed(range(STEPS)):
        stored, stored_margin = states[step_index]
        sensitivity = sensitivity - trim(adjoint, step_index + 1, 0) * drag_law(
            trim(stored, stored_margin, 0)
        )
        adjoint = retreat(
            adjoint,
            trim(advect_all, m, step_index + 1),
            trim(diffuse_all, m, step_index + 1),
            trim(drag, m, step_index),
            trim(stored, stored_margin, step_index),
        )

    weighted = jnp.einsum("l,lrc->rc", gain, sensitivity, precision=HIGHEST)
    own_r = prof_r[..., m : m + rows]
    own_c = prof_c[..., m : m + cols]
    across = jnp.einsum("rc,dkc->dkr", weighted, own_c, precision=HIGHEST)
    totals = jnp.sum(own_r * across, axis=2)
    values = thrusts * totals
    spread = jnp.pad(values, ((0, 0), (0, 128 - per)))
    grad = close_scatter(spread)[0, :per]
    return adjoint, grad


def solution(mesh):
    placed = (
        P(None, "gx", "gy"),
        P(None, "gx", "gy"),
        P(None, "gx", "gy"),
        P(None, "gx", "gy"),
        P(("gx", "gy"), None),
        P(("gx", "gy"), None),
        P(("gx", "gy")),
        P(("gx", "gy")),
    )
    return jax.shard_map(
        shards,
        mesh=mesh,
        in_specs=placed,
        out_specs=(P(None, "gx", "gy"), P(("gx", "gy"))),
        check_vma=False,
    )
```

```python
import functools

import jax
import jax.numpy as jnp
from jax import lax
from jax.experimental import pallas as pl
from jax.experimental.pallas import tpu as pltpu
from jax.sharding import PartitionSpec as P

LEV = 3
STEPS = 8
FP = 64
MARGIN = 2 * (STEPS - 1)

VERTICAL_MIX = 0.05
DRAG_SCALE = 0.01
HIGHEST = lax.Precision.HIGHEST


MESH_ID = pl.DeviceIdType.MESH


HALO_MOVES = ((1, 0), (-1, 0), (0, 1), (0, -1), (1, 1), (1, -1), (-1, 1), (-1, -1))


def enter(n_gy, n_dev, me):
    barrier = pltpu.get_barrier_semaphore()
    for step in range(1, n_dev):
        target = lax.rem(me + step, n_dev)
        pl.semaphore_signal(
            barrier, inc=1, device_id=(target // n_gy, target % n_gy), device_id_type=MESH_ID
        )
    pl.semaphore_wait(barrier, n_dev - 1)


def spread_rows(n_gy, n_dev, me, src_of, slots, send_sem, recv_sem):
    for step in range(1, n_dev):
        target = lax.rem(me + step, n_dev)
        pltpu.make_async_remote_copy(
            src_of(target),
            slots.at[pl.ds(me, 1)],
            send_sem,
            recv_sem,
            device_id=(target // n_gy, target % n_gy),
            device_id_type=MESH_ID,
        ).start()
    first = lax.rem(me + 1, n_dev)
    rest = pl.ds(0, n_dev - 1)
    return pltpu.make_async_remote_copy(
        slots.at[rest],
        slots.at[rest],
        send_sem,
        recv_sem,
        device_id=(first // n_gy, first % n_gy),
        device_id_type=MESH_ID,
    )


def open_kernel(n_gx, n_gy, *refs):
    n_dev = n_gx * n_gy
    n_halo = len(HALO_MOVES)
    info_ref = refs[0]
    pieces = refs[1 : 1 + n_halo]
    gathered = refs[1 + n_halo]
    landed = refs[2 + n_halo : 2 + 2 * n_halo]
    slots, send_sem, recv_sem, local_sem, halo_send, halo_recv = refs[2 + 2 * n_halo :]
    gx = lax.axis_index("gx")
    gy = lax.axis_index("gy")
    me = gx * n_gy + gy
    enter(n_gy, n_dev, me)
    local = pltpu.make_async_copy(info_ref, slots.at[pl.ds(me, 1)], local_sem)
    local.start()
    halo = []
    for index, (dx, dy) in enumerate(HALO_MOVES):
        copy = pltpu.make_async_remote_copy(
            pieces[index],
            landed[index],
            halo_send.at[index],
            halo_recv.at[index],
            device_id=(lax.rem(gx + dx + n_gx, n_gx), lax.rem(gy + dy + n_gy, n_gy)),
            device_id_type=MESH_ID,
        )
        copy.start()
        halo.append(copy)
    every = spread_rows(n_gy, n_dev, me, lambda target: info_ref, slots, send_sem, recv_sem)
    local.wait()
    for copy in halo:
        copy.wait()
    every.wait_send()
    every.wait_recv()
    gathered[...] = slots[...]


def open_exchange(info_row, pieces):
    n_gx = lax.axis_size("gx")
    n_gy = lax.axis_size("gy")
    n_dev = n_gx * n_gy
    vmem = pl.BlockSpec(memory_space=pltpu.VMEM)
    out_shape = [jax.ShapeDtypeStruct((n_dev, info_row.shape[1]), jnp.float32)] + [
        jax.ShapeDtypeStruct(piece.shape, piece.dtype) for piece in pieces
    ]
    return pl.pallas_call(
        functools.partial(open_kernel, n_gx, n_gy),
        out_shape=out_shape,
        in_specs=[vmem] * (1 + len(pieces)),
        out_specs=[vmem] * len(out_shape),
        scratch_shapes=[
            pltpu.VMEM((n_dev, info_row.shape[1]), jnp.float32),
            pltpu.SemaphoreType.DMA,
            pltpu.SemaphoreType.DMA,
            pltpu.SemaphoreType.DMA,
            pltpu.SemaphoreType.DMA((len(pieces),)),
            pltpu.SemaphoreType.DMA((len(pieces),)),
        ],
        compiler_params=pltpu.CompilerParams(has_side_effects=True, collective_id=0),
    )(info_row, *pieces)


def close_kernel(n_gy, n_dev, src_ref, out_ref, slots, send_sem, recv_sem, local_sem):
    gx = lax.axis_index("gx")
    gy = lax.axis_index("gy")
    me = gx * n_gy + gy
    enter(n_gy, n_dev, me)
    local = pltpu.make_async_copy(src_ref.at[pl.ds(me, 1)], slots.at[pl.ds(me, 1)], local_sem)
    local.start()
    every = spread_rows(
        n_gy, n_dev, me, lambda target: src_ref.at[pl.ds(target, 1)], slots, send_sem, recv_sem
    )
    local.wait()
    every.wait_send()
    every.wait_recv()
    out_ref[...] = jnp.sum(slots[...], axis=0, keepdims=True)


def close_scatter(rows):
    n_gy = lax.axis_size("gy")
    n_dev = lax.axis_size("gx") * n_gy
    vmem = pl.BlockSpec(memory_space=pltpu.VMEM)
    return pl.pallas_call(
        functools.partial(close_kernel, n_gy, n_dev),
        out_shape=jax.ShapeDtypeStruct((1, rows.shape[1]), jnp.float32),
        in_specs=[vmem],
        out_specs=vmem,
        scratch_shapes=[
            pltpu.VMEM(rows.shape, jnp.float32),
            pltpu.SemaphoreType.DMA,
            pltpu.SemaphoreType.DMA,
            pltpu.SemaphoreType.DMA,
        ],
        compiler_params=pltpu.CompilerParams(has_side_effects=True, collective_id=1),
    )(rows)


def halo_pieces(block, m):
    depth = block.shape[0]
    last_r, first_r = block[:, -m:, :], block[:, :m, :]
    last_c = jnp.swapaxes(block[:, :, -m:], 1, 2)
    first_c = jnp.swapaxes(block[:, :, :m], 1, 2)
    pieces = (
        last_r,
        first_r,
        last_c,
        first_c,
        last_r[:, :, -m:],
        last_r[:, :, :m],
        first_r[:, :, -m:],
        first_r[:, :, :m],
    )
    return tuple(piece.reshape(depth * m, piece.shape[2]) for piece in pieces)


def assemble(block, landed, m, size_r, size_c):
    depth, rows, cols = block.shape
    row_low, row_high, col_low, col_high, c_ll, c_lh, c_hl, c_hh = (
        piece.reshape(depth, m, piece.shape[1]) for piece in landed
    )
    col_low = jnp.swapaxes(col_low, 1, 2)
    col_high = jnp.swapaxes(col_high, 1, 2)
    gap_c = size_c - cols - 2 * m
    gap_r = size_r - rows - 2 * m

    def band(left, middle, right):
        fill = jnp.zeros(left.shape[:2] + (gap_c,), jnp.float32)
        return jnp.concatenate([left, middle, fill, right], axis=2)

    fill = jnp.zeros((depth, gap_r, size_c), jnp.float32)
    return jnp.concatenate(
        [
            band(block, col_high, col_low),
            band(row_high, c_hh, c_hl),
            fill,
            band(row_low, c_lh, c_ll),
        ],
        axis=1,
    )


def stencil_kernel(levels, steps, ext_ref, drag_ref, lam_out, sens_out, states, lams):
    size_r, size_c = ext_ref.shape[1:]

    def west(x):
        return pltpu.roll(x, 1, 0)

    def east(x):
        return pltpu.roll(x, size_r - 1, 0)

    def south(x):
        return pltpu.roll(x, 1, 1)

    def north(x):
        return pltpu.roll(x, size_c - 1, 1)

    def vertical(plane, level, center):
        mix = None
        if level + 1 < levels:
            mix = plane(level + 1) - center
        if level > 0:
            below = plane(level - 1) - center
            mix = below if mix is None else mix + below
        return mix

    for level in range(levels):
        states[0, level] = ext_ref[level]

    def forward(n, carry):
        for level in range(levels):
            center = states[n, level]
            upwind = west(center)
            advect = ext_ref[levels + level]
            diffuse = ext_ref[2 * levels + level]
            states[n + 1, level] = (
                center
                + advect * (upwind - center)
                + diffuse * (east(center) + upwind + north(center) + south(center) - 4.0 * center)
                + VERTICAL_MIX * vertical(lambda l: states[n, l], level, center)
                - drag_ref[level] * (center * jnp.sqrt(center * center + 1.0))
            )
        return carry

    lax.fori_loop(0, steps - 1, forward, 0)
    for level in range(levels):
        lams[0, level] = ext_ref[3 * levels + level]
        sens_out[level] = jnp.zeros(sens_out.shape[1:], jnp.float32)

    def backward(i, carry):
        n = steps - 1 - i
        now = i % 2
        for level in range(levels):
            adjoint = lams[now, level]
            state = states[n, level]
            sens_out[level] = sens_out[level] - adjoint * (state * jnp.sqrt(state * state + 1.0))
            flux_adv = ext_ref[levels + level] * adjoint
            flux_dif = ext_ref[2 * levels + level] * adjoint
            square_one = state * state + 1.0
            slope = (square_one + state * state) / jnp.sqrt(square_one)
            lams[1 - now, level] = (
                adjoint
                - flux_adv
                - 4.0 * flux_dif
                + east(flux_adv)
                + (east(flux_dif) + west(flux_dif) + north(flux_dif) + south(flux_dif))
                + VERTICAL_MIX * vertical(lambda l: lams[now, l], level, adjoint)
                - drag_ref[level] * slope * adjoint
            )
        return carry

    lax.fori_loop(0, steps, backward, 0)
    for level in range(levels):
        lam_out[level] = lams[steps % 2, level]


def stencil(ext, drag, levels):
    size_r, size_c = ext.shape[1:]
    vmem = pl.BlockSpec(memory_space=pltpu.VMEM)
    plane = jax.ShapeDtypeStruct((levels, size_r, size_c), jnp.float32)
    cells = levels * size_r * size_c
    return pl.pallas_call(
        functools.partial(stencil_kernel, levels, STEPS),
        out_shape=[plane, plane],
        in_specs=[vmem, vmem],
        out_specs=[vmem, vmem],
        scratch_shapes=[
            pltpu.VMEM((STEPS, levels, size_r, size_c), jnp.float32),
            pltpu.VMEM((2, levels, size_r, size_c), jnp.float32),
        ],
        compiler_params=pltpu.CompilerParams(vmem_limit_bytes=48 * 1024 * 1024),
        cost_estimate=pl.CostEstimate(
            flops=60 * STEPS * cells, transcendentals=3 * STEPS * cells, bytes_accessed=28 * cells
        ),
    )(ext, drag)


def drag_law(state):
    return state * jnp.sqrt(state * state + 1.0)


def drag_slope(state):
    square_one = state * state + 1.0
    return (square_one + state * state) / jnp.sqrt(square_one)


def vertical(center):
    zero_row = jnp.zeros_like(center[:1])
    from_above = jnp.concatenate([center[1:] - center[:-1], zero_row], axis=0)
    from_below = jnp.concatenate([zero_row, center[:-1] - center[1:]], axis=0)
    return from_above + from_below


def advance(padded, advect, diffuse, drag_coef):
    center = padded[:, 1:-1, 1:-1]
    upwind = padded[:, :-2, 1:-1]
    downwind = padded[:, 2:, 1:-1]
    left_cell = padded[:, 1:-1, :-2]
    right_cell = padded[:, 1:-1, 2:]
    return (
        center
        + advect * (upwind - center)
        + diffuse * (downwind + upwind + right_cell + left_cell - 4.0 * center)
        + VERTICAL_MIX * vertical(center)
        - drag_coef * drag_law(center)
    )


def retreat(padded, advect_ext, diffuse_ext, drag_coef, state):
    flux_adv = advect_ext * padded
    flux_dif = diffuse_ext * padded
    center = padded[:, 1:-1, 1:-1]
    return (
        center
        - flux_adv[:, 1:-1, 1:-1]
        - 4.0 * flux_dif[:, 1:-1, 1:-1]
        + flux_adv[:, 2:, 1:-1]
        + (
            flux_dif[:, 2:, 1:-1]
            + flux_dif[:, :-2, 1:-1]
            + flux_dif[:, 1:-1, 2:]
            + flux_dif[:, 1:-1, :-2]
        )
        + VERTICAL_MIX * vertical(center)
        - drag_coef * drag_slope(state) * center
    )


def trim(array, margin, wanted):
    excess = margin - wanted
    if excess == 0:
        return array
    return array[:, excess:-excess, excess:-excess]


def profiles(first, starts, widths, period, length, inner):
    cells = jnp.arange(length, dtype=jnp.int32)
    cells = jnp.where(cells < inner, cells, cells - length)
    pos = (first + cells - starts[..., None]) % period
    cell_pos = pos.astype(jnp.float32) - (FP - 1) / 2.0
    profile = jnp.exp(-(cell_pos * cell_pos) / (2.0 * widths[..., None] * widths[..., None]))
    return jnp.where(pos < FP, profile, 0.0)


def level_gain():
    level_pos = jnp.arange(LEV, dtype=jnp.float32) - (LEV - 1) / 2.0
    return DRAG_SCALE * jnp.exp(-0.5 * level_pos * level_pos)


def shards(
    velocity, adjoint_seed, courant, viscosity, turbine_tile, turbine_offset, thrust, disk_width
):
    levels, rows, cols = velocity.shape
    n_gx = lax.axis_size("gx")
    n_gy = lax.axis_size("gy")
    m = MARGIN
    per = thrust.shape[0]
    fields = (
        turbine_tile[:, 0].astype(jnp.float32),
        turbine_offset[:, 0].astype(jnp.float32),
        turbine_offset[:, 1].astype(jnp.float32),
        thrust,
        disk_width,
    )
    info_row = jnp.pad(jnp.concatenate(fields)[None, :], ((0, 0), (0, 128 - len(fields) * per)))
    stack = jnp.concatenate([velocity, courant, viscosity, adjoint_seed], axis=0)
    opened = open_exchange(info_row, halo_pieces(stack, m))
    info = opened[0]
    tiles = info[:, 0:per].astype(jnp.int32)
    row_start = tiles // n_gy * rows + info[:, per : 2 * per].astype(jnp.int32)
    col_start = tiles % n_gy * cols + info[:, 2 * per : 3 * per].astype(jnp.int32)
    thrusts = info[:, 3 * per : 4 * per]
    widths = info[:, 4 * per : 5 * per]
    gx = lax.axis_index("gx")
    gy = lax.axis_index("gy")
    size_r = -(-(rows + 2 * m) // 8) * 8
    size_c = -(-(cols + 2 * m) // 128) * 128
    inner_r = rows + (size_r - rows) // 2
    inner_c = cols + (size_c - cols) // 2
    prof_r = profiles(gx * rows, row_start, widths, n_gx * rows, size_r, inner_r)
    prof_c = profiles(gy * cols, col_start, widths, n_gy * cols, size_c, inner_c)
    gain = level_gain()
    plane = jnp.einsum("dkr,dkc->rc", thrusts[..., None] * prof_r, prof_c, precision=HIGHEST)
    drag = gain[:, None, None] * plane[None]
    ext = assemble(stack, opened[1:], m, size_r, size_c)
    adjoint_full, sens_full = stencil(ext, drag, levels)
    adjoint = adjoint_full[:, :rows, :cols]
    sensitivity = sens_full[:, :rows, :cols]

    weighted = jnp.einsum("l,lrc->rc", gain, sensitivity, precision=HIGHEST)
    own_r = prof_r[..., :rows]
    own_c = prof_c[..., :cols]
    across = jnp.einsum("rc,dkc->dkr", weighted, own_c, precision=HIGHEST)
    totals = jnp.sum(own_r * across, axis=2)
    values = thrusts * totals
    spread = jnp.pad(values, ((0, 0), (0, 128 - per)))
    grad = close_scatter(spread)[0, :per]
    return adjoint, grad


def solution(mesh):
    placed = (
        P(None, "gx", "gy"),
        P(None, "gx", "gy"),
        P(None, "gx", "gy"),
        P(None, "gx", "gy"),
        P(("gx", "gy"), None),
        P(("gx", "gy"), None),
        P(("gx", "gy")),
        P(("gx", "gy")),
    )
    return jax.shard_map(
        shards,
        mesh=mesh,
        in_specs=placed,
        out_specs=(P(None, "gx", "gy"), P(("gx", "gy"))),
        check_vma=False,
    )
```

```python
import functools

import jax
import jax.numpy as jnp
from jax import lax
from jax.experimental import pallas as pl
from jax.experimental.pallas import tpu as pltpu
from jax.sharding import PartitionSpec as P

LEV = 3
STEPS = 8
FP = 64
MARGIN = 2 * STEPS

VERTICAL_MIX = 0.05
DRAG_SCALE = 0.01
HIGHEST = lax.Precision.HIGHEST


MESH_ID = pl.DeviceIdType.MESH


HALO_MOVES = ((1, 0), (-1, 0), (0, 1), (0, -1), (1, 1), (1, -1), (-1, 1), (-1, -1))


def enter(n_gy, n_dev, me):
    barrier = pltpu.get_barrier_semaphore()
    for step in range(1, n_dev):
        target = lax.rem(me + step, n_dev)
        pl.semaphore_signal(
            barrier, inc=1, device_id=(target // n_gy, target % n_gy), device_id_type=MESH_ID
        )
    pl.semaphore_wait(barrier, n_dev - 1)


def spread_rows(n_gy, n_dev, me, src_of, slots, send_sem, recv_sem):
    for step in range(1, n_dev):
        target = lax.rem(me + step, n_dev)
        pltpu.make_async_remote_copy(
            src_of(target),
            slots.at[pl.ds(me, 1)],
            send_sem,
            recv_sem,
            device_id=(target // n_gy, target % n_gy),
            device_id_type=MESH_ID,
        ).start()
    first = lax.rem(me + 1, n_dev)
    rest = pl.ds(0, n_dev - 1)
    return pltpu.make_async_remote_copy(
        slots.at[rest],
        slots.at[rest],
        send_sem,
        recv_sem,
        device_id=(first // n_gy, first % n_gy),
        device_id_type=MESH_ID,
    )


def open_kernel(n_gx, n_gy, *refs):
    n_dev = n_gx * n_gy
    n_halo = len(HALO_MOVES)
    info_ref = refs[0]
    pieces = refs[1 : 1 + n_halo]
    gathered = refs[1 + n_halo]
    landed = refs[2 + n_halo : 2 + 2 * n_halo]
    slots, send_sem, recv_sem, local_sem, halo_send, halo_recv = refs[2 + 2 * n_halo :]
    gx = lax.axis_index("gx")
    gy = lax.axis_index("gy")
    me = gx * n_gy + gy
    enter(n_gy, n_dev, me)
    local = pltpu.make_async_copy(info_ref, slots.at[pl.ds(me, 1)], local_sem)
    local.start()
    halo = []
    for index, (dx, dy) in enumerate(HALO_MOVES):
        copy = pltpu.make_async_remote_copy(
            pieces[index],
            landed[index],
            halo_send.at[index],
            halo_recv.at[index],
            device_id=(lax.rem(gx + dx + n_gx, n_gx), lax.rem(gy + dy + n_gy, n_gy)),
            device_id_type=MESH_ID,
        )
        copy.start()
        halo.append(copy)
    every = spread_rows(n_gy, n_dev, me, lambda target: info_ref, slots, send_sem, recv_sem)
    local.wait()
    for copy in halo:
        copy.wait()
    every.wait_send()
    every.wait_recv()
    gathered[...] = slots[...]


def open_exchange(info_row, pieces):
    n_gx = lax.axis_size("gx")
    n_gy = lax.axis_size("gy")
    n_dev = n_gx * n_gy
    vmem = pl.BlockSpec(memory_space=pltpu.VMEM)
    out_shape = [jax.ShapeDtypeStruct((n_dev, info_row.shape[1]), jnp.float32)] + [
        jax.ShapeDtypeStruct(piece.shape, piece.dtype) for piece in pieces
    ]
    return pl.pallas_call(
        functools.partial(open_kernel, n_gx, n_gy),
        out_shape=out_shape,
        in_specs=[vmem] * (1 + len(pieces)),
        out_specs=[vmem] * len(out_shape),
        scratch_shapes=[
            pltpu.VMEM((n_dev, info_row.shape[1]), jnp.float32),
            pltpu.SemaphoreType.DMA,
            pltpu.SemaphoreType.DMA,
            pltpu.SemaphoreType.DMA,
            pltpu.SemaphoreType.DMA((len(pieces),)),
            pltpu.SemaphoreType.DMA((len(pieces),)),
        ],
        compiler_params=pltpu.CompilerParams(has_side_effects=True, collective_id=0),
    )(info_row, *pieces)


def close_kernel(n_gy, n_dev, src_ref, out_ref, slots, send_sem, recv_sem, local_sem):
    gx = lax.axis_index("gx")
    gy = lax.axis_index("gy")
    me = gx * n_gy + gy
    enter(n_gy, n_dev, me)
    local = pltpu.make_async_copy(src_ref.at[pl.ds(me, 1)], slots.at[pl.ds(me, 1)], local_sem)
    local.start()
    every = spread_rows(
        n_gy, n_dev, me, lambda target: src_ref.at[pl.ds(target, 1)], slots, send_sem, recv_sem
    )
    local.wait()
    every.wait_send()
    every.wait_recv()
    out_ref[...] = jnp.sum(slots[...], axis=0, keepdims=True)


def close_scatter(rows):
    n_gy = lax.axis_size("gy")
    n_dev = lax.axis_size("gx") * n_gy
    vmem = pl.BlockSpec(memory_space=pltpu.VMEM)
    return pl.pallas_call(
        functools.partial(close_kernel, n_gy, n_dev),
        out_shape=jax.ShapeDtypeStruct((1, rows.shape[1]), jnp.float32),
        in_specs=[vmem],
        out_specs=vmem,
        scratch_shapes=[
            pltpu.VMEM(rows.shape, jnp.float32),
            pltpu.SemaphoreType.DMA,
            pltpu.SemaphoreType.DMA,
            pltpu.SemaphoreType.DMA,
        ],
        compiler_params=pltpu.CompilerParams(has_side_effects=True, collective_id=1),
    )(rows)


def halo_pieces(block, m):
    last_r, first_r = block[:, -m:, :], block[:, :m, :]
    return (
        last_r,
        first_r,
        jnp.swapaxes(block[:, :, -m:], 1, 2),
        jnp.swapaxes(block[:, :, :m], 1, 2),
        last_r[:, :, -m:],
        last_r[:, :, :m],
        first_r[:, :, -m:],
        first_r[:, :, :m],
    )


def assemble(block, landed, m, size_r, size_c):
    depth, rows, cols = block.shape
    row_low, row_high, col_low, col_high, c_ll, c_lh, c_hl, c_hh = landed
    col_low = jnp.swapaxes(col_low, 1, 2)
    col_high = jnp.swapaxes(col_high, 1, 2)
    gap_c = size_c - cols - 2 * m
    gap_r = size_r - rows - 2 * m

    def band(left, middle, right):
        fill = jnp.zeros(left.shape[:2] + (gap_c,), jnp.float32)
        return jnp.concatenate([left, middle, fill, right], axis=2)

    parts = [band(block, col_high, col_low), band(row_high, c_hh, c_hl)]
    if gap_r:
        parts.append(jnp.zeros((depth, gap_r, size_c), jnp.float32))
    parts.append(band(row_low, c_lh, c_ll))
    return jnp.concatenate(parts, axis=1)


def stencil_kernel(levels, steps, ext_ref, drag_ref, lam_out, sens_out, states, lams):
    size_r, size_c = ext_ref.shape[1:]

    def west(x):
        return pltpu.roll(x, 1, 0)

    def east(x):
        return pltpu.roll(x, size_r - 1, 0)

    def south(x):
        return pltpu.roll(x, 1, 1)

    def north(x):
        return pltpu.roll(x, size_c - 1, 1)

    def vertical(plane, level, center):
        mix = None
        if level + 1 < levels:
            mix = plane(level + 1) - center
        if level > 0:
            below = plane(level - 1) - center
            mix = below if mix is None else mix + below
        return mix

    for level in range(levels):
        states[0, level] = ext_ref[level]

    def forward(n, carry):
        for level in range(levels):
            center = states[n, level]
            upwind = west(center)
            advect = ext_ref[levels + level]
            diffuse = ext_ref[2 * levels + level]
            states[n + 1, level] = (
                center
                + advect * (upwind - center)
                + diffuse * (east(center) + upwind + north(center) + south(center) - 4.0 * center)
                + VERTICAL_MIX * vertical(lambda l: states[n, l], level, center)
                - drag_ref[level] * (center * jnp.sqrt(center * center + 1.0))
            )
        return carry

    lax.fori_loop(0, steps - 1, forward, 0)
    for level in range(levels):
        lams[0, level] = ext_ref[3 * levels + level]
        sens_out[level] = jnp.zeros(sens_out.shape[1:], jnp.float32)

    def backward(i, carry):
        n = steps - 1 - i
        now = i % 2
        for level in range(levels):
            adjoint = lams[now, level]
            state = states[n, level]
            sens_out[level] = sens_out[level] - adjoint * (state * jnp.sqrt(state * state + 1.0))
            flux_adv = ext_ref[levels + level] * adjoint
            flux_dif = ext_ref[2 * levels + level] * adjoint
            square_one = state * state + 1.0
            slope = (square_one + state * state) / jnp.sqrt(square_one)
            lams[1 - now, level] = (
                adjoint
                - flux_adv
                - 4.0 * flux_dif
                + east(flux_adv)
                + (east(flux_dif) + west(flux_dif) + north(flux_dif) + south(flux_dif))
                + VERTICAL_MIX * vertical(lambda l: lams[now, l], level, adjoint)
                - drag_ref[level] * slope * adjoint
            )
        return carry

    lax.fori_loop(0, steps, backward, 0)
    for level in range(levels):
        lam_out[level] = lams[steps % 2, level]


def stencil(ext, drag, levels):
    size_r, size_c = ext.shape[1:]
    vmem = pl.BlockSpec(memory_space=pltpu.VMEM)
    plane = jax.ShapeDtypeStruct((levels, size_r, size_c), jnp.float32)
    cells = levels * size_r * size_c
    return pl.pallas_call(
        functools.partial(stencil_kernel, levels, STEPS),
        out_shape=[plane, plane],
        in_specs=[vmem, vmem],
        out_specs=[vmem, vmem],
        scratch_shapes=[
            pltpu.VMEM((STEPS, levels, size_r, size_c), jnp.float32),
            pltpu.VMEM((2, levels, size_r, size_c), jnp.float32),
        ],
        compiler_params=pltpu.CompilerParams(vmem_limit_bytes=48 * 1024 * 1024),
        cost_estimate=pl.CostEstimate(
            flops=60 * STEPS * cells, transcendentals=3 * STEPS * cells, bytes_accessed=28 * cells
        ),
    )(ext, drag)


def drag_law(state):
    return state * jnp.sqrt(state * state + 1.0)


def drag_slope(state):
    square_one = state * state + 1.0
    return (square_one + state * state) / jnp.sqrt(square_one)


def vertical(center):
    zero_row = jnp.zeros_like(center[:1])
    from_above = jnp.concatenate([center[1:] - center[:-1], zero_row], axis=0)
    from_below = jnp.concatenate([zero_row, center[:-1] - center[1:]], axis=0)
    return from_above + from_below


def advance(padded, advect, diffuse, drag_coef):
    center = padded[:, 1:-1, 1:-1]
    upwind = padded[:, :-2, 1:-1]
    downwind = padded[:, 2:, 1:-1]
    left_cell = padded[:, 1:-1, :-2]
    right_cell = padded[:, 1:-1, 2:]
    return (
        center
        + advect * (upwind - center)
        + diffuse * (downwind + upwind + right_cell + left_cell - 4.0 * center)
        + VERTICAL_MIX * vertical(center)
        - drag_coef * drag_law(center)
    )


def retreat(padded, advect_ext, diffuse_ext, drag_coef, state):
    flux_adv = advect_ext * padded
    flux_dif = diffuse_ext * padded
    center = padded[:, 1:-1, 1:-1]
    return (
        center
        - flux_adv[:, 1:-1, 1:-1]
        - 4.0 * flux_dif[:, 1:-1, 1:-1]
        + flux_adv[:, 2:, 1:-1]
        + (
            flux_dif[:, 2:, 1:-1]
            + flux_dif[:, :-2, 1:-1]
            + flux_dif[:, 1:-1, 2:]
            + flux_dif[:, 1:-1, :-2]
        )
        + VERTICAL_MIX * vertical(center)
        - drag_coef * drag_slope(state) * center
    )


def trim(array, margin, wanted):
    excess = margin - wanted
    if excess == 0:
        return array
    return array[:, excess:-excess, excess:-excess]


def profiles(first, starts, widths, period, length, inner):
    cells = jnp.arange(length, dtype=jnp.int32)
    cells = jnp.where(cells < inner, cells, cells - length)
    pos = (first + cells - starts[..., None]) % period
    cell_pos = pos.astype(jnp.float32) - (FP - 1) / 2.0
    profile = jnp.exp(-(cell_pos * cell_pos) / (2.0 * widths[..., None] * widths[..., None]))
    return jnp.where(pos < FP, profile, 0.0)


def level_gain():
    level_pos = jnp.arange(LEV, dtype=jnp.float32) - (LEV - 1) / 2.0
    return DRAG_SCALE * jnp.exp(-0.5 * level_pos * level_pos)


def shards(
    velocity, adjoint_seed, courant, viscosity, turbine_tile, turbine_offset, thrust, disk_width
):
    levels, rows, cols = velocity.shape
    n_gx = lax.axis_size("gx")
    n_gy = lax.axis_size("gy")
    m = MARGIN
    per = thrust.shape[0]
    fields = (
        turbine_tile[:, 0].astype(jnp.float32),
        turbine_offset[:, 0].astype(jnp.float32),
        turbine_offset[:, 1].astype(jnp.float32),
        thrust,
        disk_width,
    )
    info_row = jnp.pad(jnp.concatenate(fields)[None, :], ((0, 0), (0, 128 - len(fields) * per)))
    stack = jnp.concatenate([velocity, courant, viscosity, adjoint_seed], axis=0)
    opened = open_exchange(info_row, halo_pieces(stack, m))
    info = opened[0]
    tiles = info[:, 0:per].astype(jnp.int32)
    row_start = tiles // n_gy * rows + info[:, per : 2 * per].astype(jnp.int32)
    col_start = tiles % n_gy * cols + info[:, 2 * per : 3 * per].astype(jnp.int32)
    thrusts = info[:, 3 * per : 4 * per]
    widths = info[:, 4 * per : 5 * per]
    gx = lax.axis_index("gx")
    gy = lax.axis_index("gy")
    size_r = -(-(rows + 2 * m) // 8) * 8
    size_c = -(-(cols + 2 * m) // 128) * 128
    inner_r = rows + (size_r - rows) // 2
    inner_c = cols + (size_c - cols) // 2
    prof_r = profiles(gx * rows, row_start, widths, n_gx * rows, size_r, inner_r)
    prof_c = profiles(gy * cols, col_start, widths, n_gy * cols, size_c, inner_c)
    gain = level_gain()
    plane = jnp.einsum("dkr,dkc->rc", thrusts[..., None] * prof_r, prof_c, precision=HIGHEST)
    drag = gain[:, None, None] * plane[None]
    ext = assemble(stack, opened[1:], m, size_r, size_c)
    adjoint_full, sens_full = stencil(ext, drag, levels)
    adjoint = adjoint_full[:, :rows, :cols]
    sensitivity = sens_full[:, :rows, :cols]

    weighted = jnp.einsum("l,lrc->rc", gain, sensitivity, precision=HIGHEST)
    own_r = prof_r[..., :rows]
    own_c = prof_c[..., :cols]
    across = jnp.einsum("rc,dkc->dkr", weighted, own_c, precision=HIGHEST)
    totals = jnp.sum(own_r * across, axis=2)
    values = thrusts * totals
    spread = jnp.pad(values, ((0, 0), (0, 128 - per)))
    grad = close_scatter(spread)[0, :per]
    return adjoint, grad


def solution(mesh):
    placed = (
        P(None, "gx", "gy"),
        P(None, "gx", "gy"),
        P(None, "gx", "gy"),
        P(None, "gx", "gy"),
        P(("gx", "gy"), None),
        P(("gx", "gy"), None),
        P(("gx", "gy")),
        P(("gx", "gy")),
    )
    return jax.shard_map(
        shards,
        mesh=mesh,
        in_specs=placed,
        out_specs=(P(None, "gx", "gy"), P(("gx", "gy"))),
        check_vma=False,
    )
```

```python
import functools

import jax
import jax.numpy as jnp
from jax import lax
from jax.experimental import pallas as pl
from jax.experimental.pallas import tpu as pltpu
from jax.sharding import PartitionSpec as P

LEV = 3
STEPS = 8
FP = 64
MARGIN = 2 * STEPS

VERTICAL_MIX = 0.05
DRAG_SCALE = 0.01
HIGHEST = lax.Precision.HIGHEST


MESH_ID = pl.DeviceIdType.MESH


HALO_MOVES = ((1, 0), (-1, 0), (0, 1), (0, -1), (1, 1), (1, -1), (-1, 1), (-1, -1))


def enter(n_gy, n_dev, me):
    barrier = pltpu.get_barrier_semaphore()
    for step in range(1, n_dev):
        target = lax.rem(me + step, n_dev)
        pl.semaphore_signal(
            barrier, inc=1, device_id=(target // n_gy, target % n_gy), device_id_type=MESH_ID
        )
    pl.semaphore_wait(barrier, n_dev - 1)


def spread_rows(n_gy, n_dev, me, src_of, slots, send_sem, recv_sem):
    for step in range(1, n_dev):
        target = lax.rem(me + step, n_dev)
        pltpu.make_async_remote_copy(
            src_of(target),
            slots.at[pl.ds(me, 1)],
            send_sem,
            recv_sem,
            device_id=(target // n_gy, target % n_gy),
            device_id_type=MESH_ID,
        ).start()
    first = lax.rem(me + 1, n_dev)
    rest = pl.ds(0, n_dev - 1)
    return pltpu.make_async_remote_copy(
        slots.at[rest],
        slots.at[rest],
        send_sem,
        recv_sem,
        device_id=(first // n_gy, first % n_gy),
        device_id_type=MESH_ID,
    )


def open_kernel(n_gx, n_gy, *refs):
    n_dev = n_gx * n_gy
    n_halo = len(HALO_MOVES)
    info_ref = refs[0]
    pieces = refs[1 : 1 + n_halo]
    gathered = refs[1 + n_halo]
    landed = refs[2 + n_halo : 2 + 2 * n_halo]
    slots, send_sem, recv_sem, local_sem, halo_send, halo_recv = refs[2 + 2 * n_halo :]
    gx = lax.axis_index("gx")
    gy = lax.axis_index("gy")
    me = gx * n_gy + gy
    enter(n_gy, n_dev, me)
    local = pltpu.make_async_copy(info_ref, slots.at[pl.ds(me, 1)], local_sem)
    local.start()
    halo = []
    for index, (dx, dy) in enumerate(HALO_MOVES):
        copy = pltpu.make_async_remote_copy(
            pieces[index],
            landed[index],
            halo_send.at[index],
            halo_recv.at[index],
            device_id=(lax.rem(gx + dx + n_gx, n_gx), lax.rem(gy + dy + n_gy, n_gy)),
            device_id_type=MESH_ID,
        )
        copy.start()
        halo.append(copy)
    every = spread_rows(n_gy, n_dev, me, lambda target: info_ref, slots, send_sem, recv_sem)
    local.wait()
    for copy in halo:
        copy.wait()
    every.wait_send()
    every.wait_recv()
    gathered[...] = slots[...]


def open_exchange(info_row, pieces):
    n_gx = lax.axis_size("gx")
    n_gy = lax.axis_size("gy")
    n_dev = n_gx * n_gy
    vmem = pl.BlockSpec(memory_space=pltpu.VMEM)
    out_shape = [jax.ShapeDtypeStruct((n_dev, info_row.shape[1]), jnp.float32)] + [
        jax.ShapeDtypeStruct(piece.shape, piece.dtype) for piece in pieces
    ]
    return pl.pallas_call(
        functools.partial(open_kernel, n_gx, n_gy),
        out_shape=out_shape,
        in_specs=[vmem] * (1 + len(pieces)),
        out_specs=[vmem] * len(out_shape),
        scratch_shapes=[
            pltpu.VMEM((n_dev, info_row.shape[1]), jnp.float32),
            pltpu.SemaphoreType.DMA,
            pltpu.SemaphoreType.DMA,
            pltpu.SemaphoreType.DMA,
            pltpu.SemaphoreType.DMA((len(pieces),)),
            pltpu.SemaphoreType.DMA((len(pieces),)),
        ],
        compiler_params=pltpu.CompilerParams(has_side_effects=True, collective_id=0),
    )(info_row, *pieces)


def close_kernel(n_gy, n_dev, src_ref, out_ref, slots, send_sem, recv_sem, local_sem):
    gx = lax.axis_index("gx")
    gy = lax.axis_index("gy")
    me = gx * n_gy + gy
    enter(n_gy, n_dev, me)
    local = pltpu.make_async_copy(src_ref.at[pl.ds(me, 1)], slots.at[pl.ds(me, 1)], local_sem)
    local.start()
    every = spread_rows(
        n_gy, n_dev, me, lambda target: src_ref.at[pl.ds(target, 1)], slots, send_sem, recv_sem
    )
    local.wait()
    every.wait_send()
    every.wait_recv()
    out_ref[...] = jnp.sum(slots[...], axis=0, keepdims=True)


def close_scatter(rows):
    n_gy = lax.axis_size("gy")
    n_dev = lax.axis_size("gx") * n_gy
    vmem = pl.BlockSpec(memory_space=pltpu.VMEM)
    return pl.pallas_call(
        functools.partial(close_kernel, n_gy, n_dev),
        out_shape=jax.ShapeDtypeStruct((1, rows.shape[1]), jnp.float32),
        in_specs=[vmem],
        out_specs=vmem,
        scratch_shapes=[
            pltpu.VMEM(rows.shape, jnp.float32),
            pltpu.SemaphoreType.DMA,
            pltpu.SemaphoreType.DMA,
            pltpu.SemaphoreType.DMA,
        ],
        compiler_params=pltpu.CompilerParams(has_side_effects=True, collective_id=1),
    )(rows)


def halo_pieces(block, m):
    last_r, first_r = block[:, -m:, :], block[:, :m, :]
    return (
        last_r,
        first_r,
        jnp.swapaxes(block[:, :, -m:], 1, 2),
        jnp.swapaxes(block[:, :, :m], 1, 2),
        last_r[:, :, -m:],
        last_r[:, :, :m],
        first_r[:, :, -m:],
        first_r[:, :, :m],
    )


def column_band(landed, m, size_r, size_c, cols):
    row_low, row_high, col_low, col_high, c_ll, c_lh, c_hl, c_hh = landed
    depth = col_low.shape[0]
    width = size_c - cols
    span = -(-size_r // 128) * 128

    def edge(column, high_corner, low_corner):
        fill = jnp.zeros((depth, m, span - size_r), jnp.float32)
        return jnp.concatenate(
            [column, jnp.swapaxes(high_corner, 1, 2), jnp.swapaxes(low_corner, 1, 2), fill],
            axis=2,
        )

    fill = jnp.zeros((depth, width - 2 * m, span), jnp.float32)
    return jnp.concatenate([edge(col_high, c_hh, c_lh), fill, edge(col_low, c_hl, c_ll)], axis=1)


def stencil_kernel(
    levels, steps, block_ref, high_ref, low_ref, band_ref, drag_ref, lam_out, sens_out,
    ext_ref, states, lams,
):
    size_r, size_c = ext_ref.shape[1:]
    rows, cols = block_ref.shape[1:]
    m = high_ref.shape[1]
    for depth in range(ext_ref.shape[0]):
        ext_ref[depth, :rows, :cols] = block_ref[depth]
        ext_ref[depth, rows : rows + m, :cols] = high_ref[depth]
        ext_ref[depth, size_r - m :, :cols] = low_ref[depth]
        ext_ref[depth, :, cols:] = band_ref[depth].T[:size_r]

    def west(x):
        return pltpu.roll(x, 1, 0)

    def east(x):
        return pltpu.roll(x, size_r - 1, 0)

    def south(x):
        return pltpu.roll(x, 1, 1)

    def north(x):
        return pltpu.roll(x, size_c - 1, 1)

    def vertical(plane, level, center):
        mix = None
        if level + 1 < levels:
            mix = plane(level + 1) - center
        if level > 0:
            below = plane(level - 1) - center
            mix = below if mix is None else mix + below
        return mix

    for level in range(levels):
        states[0, level] = ext_ref[level]

    def forward(n, carry):
        for level in range(levels):
            center = states[n, level]
            upwind = west(center)
            advect = ext_ref[levels + level]
            diffuse = ext_ref[2 * levels + level]
            states[n + 1, level] = (
                center
                + advect * (upwind - center)
                + diffuse * (east(center) + upwind + north(center) + south(center) - 4.0 * center)
                + VERTICAL_MIX * vertical(lambda l: states[n, l], level, center)
                - drag_ref[level] * (center * jnp.sqrt(center * center + 1.0))
            )
        return carry

    lax.fori_loop(0, steps - 1, forward, 0)
    for level in range(levels):
        lams[0, level] = ext_ref[3 * levels + level]
        sens_out[level] = jnp.zeros(sens_out.shape[1:], jnp.float32)

    def backward(i, carry):
        n = steps - 1 - i
        now = i % 2
        for level in range(levels):
            adjoint = lams[now, level]
            state = states[n, level]
            sens_out[level] = sens_out[level] - adjoint * (state * jnp.sqrt(state * state + 1.0))
            flux_adv = ext_ref[levels + level] * adjoint
            flux_dif = ext_ref[2 * levels + level] * adjoint
            square_one = state * state + 1.0
            slope = (square_one + state * state) / jnp.sqrt(square_one)
            lams[1 - now, level] = (
                adjoint
                - flux_adv
                - 4.0 * flux_dif
                + east(flux_adv)
                + (east(flux_dif) + west(flux_dif) + north(flux_dif) + south(flux_dif))
                + VERTICAL_MIX * vertical(lambda l: lams[now, l], level, adjoint)
                - drag_ref[level] * slope * adjoint
            )
        return carry

    lax.fori_loop(0, steps, backward, 0)
    for level in range(levels):
        lam_out[level] = lams[steps % 2, level]


def stencil(block, landed, band, drag, levels):
    size_r, size_c = drag.shape[1:]
    depth = block.shape[0]
    vmem = pl.BlockSpec(memory_space=pltpu.VMEM)
    plane = jax.ShapeDtypeStruct((levels, size_r, size_c), jnp.float32)
    cells = levels * size_r * size_c
    return pl.pallas_call(
        functools.partial(stencil_kernel, levels, STEPS),
        out_shape=[plane, plane],
        in_specs=[vmem] * 5,
        out_specs=[vmem, vmem],
        scratch_shapes=[
            pltpu.VMEM((depth, size_r, size_c), jnp.float32),
            pltpu.VMEM((STEPS, levels, size_r, size_c), jnp.float32),
            pltpu.VMEM((2, levels, size_r, size_c), jnp.float32),
        ],
        compiler_params=pltpu.CompilerParams(vmem_limit_bytes=48 * 1024 * 1024),
        cost_estimate=pl.CostEstimate(
            flops=60 * STEPS * cells, transcendentals=3 * STEPS * cells, bytes_accessed=28 * cells
        ),
    )(block, landed[1], landed[0], band, drag)


def drag_law(state):
    return state * jnp.sqrt(state * state + 1.0)


def drag_slope(state):
    square_one = state * state + 1.0
    return (square_one + state * state) / jnp.sqrt(square_one)


def vertical(center):
    zero_row = jnp.zeros_like(center[:1])
    from_above = jnp.concatenate([center[1:] - center[:-1], zero_row], axis=0)
    from_below = jnp.concatenate([zero_row, center[:-1] - center[1:]], axis=0)
    return from_above + from_below


def advance(padded, advect, diffuse, drag_coef):
    center = padded[:, 1:-1, 1:-1]
    upwind = padded[:, :-2, 1:-1]
    downwind = padded[:, 2:, 1:-1]
    left_cell = padded[:, 1:-1, :-2]
    right_cell = padded[:, 1:-1, 2:]
    return (
        center
        + advect * (upwind - center)
        + diffuse * (downwind + upwind + right_cell + left_cell - 4.0 * center)
        + VERTICAL_MIX * vertical(center)
        - drag_coef * drag_law(center)
    )


def retreat(padded, advect_ext, diffuse_ext, drag_coef, state):
    flux_adv = advect_ext * padded
    flux_dif = diffuse_ext * padded
    center = padded[:, 1:-1, 1:-1]
    return (
        center
        - flux_adv[:, 1:-1, 1:-1]
        - 4.0 * flux_dif[:, 1:-1, 1:-1]
        + flux_adv[:, 2:, 1:-1]
        + (
            flux_dif[:, 2:, 1:-1]
            + flux_dif[:, :-2, 1:-1]
            + flux_dif[:, 1:-1, 2:]
            + flux_dif[:, 1:-1, :-2]
        )
        + VERTICAL_MIX * vertical(center)
        - drag_coef * drag_slope(state) * center
    )


def trim(array, margin, wanted):
    excess = margin - wanted
    if excess == 0:
        return array
    return array[:, excess:-excess, excess:-excess]


def profiles(first, starts, widths, period, length, inner):
    cells = jnp.arange(length, dtype=jnp.int32)
    cells = jnp.where(cells < inner, cells, cells - length)
    pos = (first + cells - starts[..., None]) % period
    cell_pos = pos.astype(jnp.float32) - (FP - 1) / 2.0
    profile = jnp.exp(-(cell_pos * cell_pos) / (2.0 * widths[..., None] * widths[..., None]))
    return jnp.where(pos < FP, profile, 0.0)


def level_gain():
    level_pos = jnp.arange(LEV, dtype=jnp.float32) - (LEV - 1) / 2.0
    return DRAG_SCALE * jnp.exp(-0.5 * level_pos * level_pos)


def shards(
    velocity, adjoint_seed, courant, viscosity, turbine_tile, turbine_offset, thrust, disk_width
):
    levels, rows, cols = velocity.shape
    n_gx = lax.axis_size("gx")
    n_gy = lax.axis_size("gy")
    m = MARGIN
    per = thrust.shape[0]
    fields = (
        turbine_tile[:, 0].astype(jnp.float32),
        turbine_offset[:, 0].astype(jnp.float32),
        turbine_offset[:, 1].astype(jnp.float32),
        thrust,
        disk_width,
    )
    info_row = jnp.pad(jnp.concatenate(fields)[None, :], ((0, 0), (0, 128 - len(fields) * per)))
    stack = jnp.concatenate([velocity, courant, viscosity, adjoint_seed], axis=0)
    opened = open_exchange(info_row, halo_pieces(stack, m))
    info = opened[0]
    tiles = info[:, 0:per].astype(jnp.int32)
    row_start = tiles // n_gy * rows + info[:, per : 2 * per].astype(jnp.int32)
    col_start = tiles % n_gy * cols + info[:, 2 * per : 3 * per].astype(jnp.int32)
    thrusts = info[:, 3 * per : 4 * per]
    widths = info[:, 4 * per : 5 * per]
    gx = lax.axis_index("gx")
    gy = lax.axis_index("gy")
    size_r = -(-(rows + 2 * m) // 8) * 8
    size_c = -(-(cols + 2 * m) // 128) * 128
    inner_r = rows + (size_r - rows) // 2
    inner_c = cols + (size_c - cols) // 2
    prof_r = profiles(gx * rows, row_start, widths, n_gx * rows, size_r, inner_r)
    prof_c = profiles(gy * cols, col_start, widths, n_gy * cols, size_c, inner_c)
    gain = level_gain()
    plane = jnp.einsum("dkr,dkc->rc", thrusts[..., None] * prof_r, prof_c, precision=HIGHEST)
    drag = gain[:, None, None] * plane[None]
    band = column_band(opened[1:], m, size_r, size_c, cols)
    adjoint_full, sens_full = stencil(stack, opened[1:], band, drag, levels)
    adjoint = adjoint_full[:, :rows, :cols]
    sensitivity = sens_full[:, :rows, :cols]

    weighted = jnp.einsum("l,lrc->rc", gain, sensitivity, precision=HIGHEST)
    own_r = prof_r[..., :rows]
    own_c = prof_c[..., :cols]
    across = jnp.einsum("rc,dkc->dkr", weighted, own_c, precision=HIGHEST)
    totals = jnp.sum(own_r * across, axis=2)
    values = thrusts * totals
    spread = jnp.pad(values, ((0, 0), (0, 128 - per)))
    grad = close_scatter(spread)[0, :per]
    return adjoint, grad


def solution(mesh):
    placed = (
        P(None, "gx", "gy"),
        P(None, "gx", "gy"),
        P(None, "gx", "gy"),
        P(None, "gx", "gy"),
        P(("gx", "gy"), None),
        P(("gx", "gy"), None),
        P(("gx", "gy")),
        P(("gx", "gy")),
    )
    return jax.shard_map(
        shards,
        mesh=mesh,
        in_specs=placed,
        out_specs=(P(None, "gx", "gy"), P(("gx", "gy"))),
        check_vma=False,
    )
```

```python
import functools

import jax
import jax.numpy as jnp
from jax import lax
from jax.experimental import pallas as pl
from jax.experimental.pallas import tpu as pltpu
from jax.sharding import PartitionSpec as P

LEV = 3
STEPS = 8
FP = 64
MARGIN = 2 * STEPS

VERTICAL_MIX = 0.05
DRAG_SCALE = 0.01
HIGHEST = lax.Precision.HIGHEST


MESH_ID = pl.DeviceIdType.MESH


HALO_MOVES = ((1, 0), (-1, 0), (0, 1), (0, -1), (1, 1), (1, -1), (-1, 1), (-1, -1))


def enter(n_gy, n_dev, me):
    barrier = pltpu.get_barrier_semaphore()
    for step in range(1, n_dev):
        target = lax.rem(me + step, n_dev)
        pl.semaphore_signal(
            barrier, inc=1, device_id=(target // n_gy, target % n_gy), device_id_type=MESH_ID
        )
    pl.semaphore_wait(barrier, n_dev - 1)


def spread_rows(n_gy, n_dev, me, src_of, slots, send_sem, recv_sem):
    for step in range(1, n_dev):
        target = lax.rem(me + step, n_dev)
        pltpu.make_async_remote_copy(
            src_of(target),
            slots.at[pl.ds(me, 1)],
            send_sem,
            recv_sem,
            device_id=(target // n_gy, target % n_gy),
            device_id_type=MESH_ID,
        ).start()
    first = lax.rem(me + 1, n_dev)
    rest = pl.ds(0, n_dev - 1)
    return pltpu.make_async_remote_copy(
        slots.at[rest],
        slots.at[rest],
        send_sem,
        recv_sem,
        device_id=(first // n_gy, first % n_gy),
        device_id_type=MESH_ID,
    )


def open_kernel(n_gx, n_gy, m, info_ref, block_ref, *refs):
    n_dev = n_gx * n_gy
    n_corner = len(HALO_MOVES) - 4
    corners = refs[:n_corner]
    gathered = refs[n_corner]
    landed = refs[n_corner + 1 : n_corner + 1 + len(HALO_MOVES)]
    columns, slots, send_sem, recv_sem, local_sem, halo_send, halo_recv = refs[
        n_corner + 1 + len(HALO_MOVES) :
    ]
    depth, rows, cols = block_ref.shape
    for index in range(depth):
        turned = block_ref[index].T
        columns[0, index] = turned[cols - m :]
        columns[1, index] = turned[:m]
    gx = lax.axis_index("gx")
    gy = lax.axis_index("gy")
    me = gx * n_gy + gy
    enter(n_gy, n_dev, me)
    local = pltpu.make_async_copy(info_ref, slots.at[pl.ds(me, 1)], local_sem)
    local.start()
    sources = (
        block_ref.at[:, rows - m :, :],
        block_ref.at[:, :m, :],
        columns.at[0],
        columns.at[1],
    ) + tuple(corners)
    halo = []
    for index, (dx, dy) in enumerate(HALO_MOVES):
        copy = pltpu.make_async_remote_copy(
            sources[index],
            landed[index],
            halo_send.at[index],
            halo_recv.at[index],
            device_id=(lax.rem(gx + dx + n_gx, n_gx), lax.rem(gy + dy + n_gy, n_gy)),
            device_id_type=MESH_ID,
        )
        copy.start()
        halo.append(copy)
    every = spread_rows(n_gy, n_dev, me, lambda target: info_ref, slots, send_sem, recv_sem)
    local.wait()
    for copy in halo:
        copy.wait()
    every.wait_send()
    every.wait_recv()
    gathered[...] = slots[...]


def open_exchange(info_row, block, corners, m):
    n_gx = lax.axis_size("gx")
    n_gy = lax.axis_size("gy")
    n_dev = n_gx * n_gy
    depth, rows, cols = block.shape
    vmem = pl.BlockSpec(memory_space=pltpu.VMEM)
    piece_shapes = [(depth, m, cols), (depth, m, cols), (depth, m, rows), (depth, m, rows)]
    piece_shapes += [corner.shape for corner in corners]
    out_shape = [jax.ShapeDtypeStruct((n_dev, info_row.shape[1]), jnp.float32)] + [
        jax.ShapeDtypeStruct(shape, jnp.float32) for shape in piece_shapes
    ]
    return pl.pallas_call(
        functools.partial(open_kernel, n_gx, n_gy, m),
        out_shape=out_shape,
        in_specs=[vmem] * (2 + len(corners)),
        out_specs=[vmem] * len(out_shape),
        scratch_shapes=[
            pltpu.VMEM((2, depth, m, rows), jnp.float32),
            pltpu.VMEM((n_dev, info_row.shape[1]), jnp.float32),
            pltpu.SemaphoreType.DMA,
            pltpu.SemaphoreType.DMA,
            pltpu.SemaphoreType.DMA,
            pltpu.SemaphoreType.DMA((len(piece_shapes),)),
            pltpu.SemaphoreType.DMA((len(piece_shapes),)),
        ],
        compiler_params=pltpu.CompilerParams(has_side_effects=True, collective_id=0),
    )(info_row, block, *corners)


def close_kernel(n_gy, n_dev, src_ref, out_ref, slots, send_sem, recv_sem, local_sem):
    gx = lax.axis_index("gx")
    gy = lax.axis_index("gy")
    me = gx * n_gy + gy
    enter(n_gy, n_dev, me)
    local = pltpu.make_async_copy(src_ref.at[pl.ds(me, 1)], slots.at[pl.ds(me, 1)], local_sem)
    local.start()
    every = spread_rows(
        n_gy, n_dev, me, lambda target: src_ref.at[pl.ds(target, 1)], slots, send_sem, recv_sem
    )
    local.wait()
    every.wait_send()
    every.wait_recv()
    out_ref[...] = jnp.sum(slots[...], axis=0, keepdims=True)


def close_scatter(rows):
    n_gy = lax.axis_size("gy")
    n_dev = lax.axis_size("gx") * n_gy
    vmem = pl.BlockSpec(memory_space=pltpu.VMEM)
    return pl.pallas_call(
        functools.partial(close_kernel, n_gy, n_dev),
        out_shape=jax.ShapeDtypeStruct((1, rows.shape[1]), jnp.float32),
        in_specs=[vmem],
        out_specs=vmem,
        scratch_shapes=[
            pltpu.VMEM(rows.shape, jnp.float32),
            pltpu.SemaphoreType.DMA,
            pltpu.SemaphoreType.DMA,
            pltpu.SemaphoreType.DMA,
        ],
        compiler_params=pltpu.CompilerParams(has_side_effects=True, collective_id=1),
    )(rows)


def corner_pieces(block, m):
    last_r, first_r = block[:, -m:, :], block[:, :m, :]
    return (
        jnp.swapaxes(last_r[:, :, -m:], 1, 2),
        jnp.swapaxes(last_r[:, :, :m], 1, 2),
        jnp.swapaxes(first_r[:, :, -m:], 1, 2),
        jnp.swapaxes(first_r[:, :, :m], 1, 2),
    )


def column_band(landed, m, size_r, size_c, cols):
    row_low, row_high, col_low, col_high, c_ll, c_lh, c_hl, c_hh = landed
    depth = col_low.shape[0]
    width = size_c - cols
    span = -(-size_r // 128) * 128

    def edge(column, high_corner, low_corner):
        fill = jnp.zeros((depth, m, span - size_r), jnp.float32)
        return jnp.concatenate(
            [column, high_corner, low_corner, fill],
            axis=2,
        )

    fill = jnp.zeros((depth, width - 2 * m, span), jnp.float32)
    return jnp.concatenate([edge(col_high, c_hh, c_lh), fill, edge(col_low, c_hl, c_ll)], axis=1)


def stencil_kernel(
    levels, steps, block_ref, high_ref, low_ref, band_ref, drag_ref, lam_out, sens_out,
    ext_ref, states, lams, sens_all,
):
    size_r, size_c = ext_ref.shape[1:]
    rows, cols = block_ref.shape[1:]
    m = high_ref.shape[1]
    for depth in range(ext_ref.shape[0]):
        ext_ref[depth, :rows, :cols] = block_ref[depth]
        ext_ref[depth, rows : rows + m, :cols] = high_ref[depth]
        ext_ref[depth, size_r - m :, :cols] = low_ref[depth]
        ext_ref[depth, :, cols:] = band_ref[depth].T[:size_r]

    def west(x):
        return pltpu.roll(x, 1, 0)

    def east(x):
        return pltpu.roll(x, size_r - 1, 0)

    def south(x):
        return pltpu.roll(x, 1, 1)

    def north(x):
        return pltpu.roll(x, size_c - 1, 1)

    def vertical(plane, level, center):
        mix = None
        if level + 1 < levels:
            mix = plane(level + 1) - center
        if level > 0:
            below = plane(level - 1) - center
            mix = below if mix is None else mix + below
        return mix

    for level in range(levels):
        states[0, level] = ext_ref[level]

    def forward(n, carry):
        for level in range(levels):
            center = states[n, level]
            upwind = west(center)
            advect = ext_ref[levels + level]
            diffuse = ext_ref[2 * levels + level]
            states[n + 1, level] = (
                center
                + advect * (upwind - center)
                + diffuse * (east(center) + upwind + north(center) + south(center) - 4.0 * center)
                + VERTICAL_MIX * vertical(lambda l: states[n, l], level, center)
                - drag_ref[level] * (center * jnp.sqrt(center * center + 1.0))
            )
        return carry

    lax.fori_loop(0, steps - 1, forward, 0)
    for level in range(levels):
        lams[0, level] = ext_ref[3 * levels + level]
        sens_all[level] = jnp.zeros(sens_all.shape[1:], jnp.float32)

    def backward(i, carry):
        n = steps - 1 - i
        now = i % 2
        for level in range(levels):
            adjoint = lams[now, level]
            state = states[n, level]
            sens_all[level] = sens_all[level] - adjoint * (state * jnp.sqrt(state * state + 1.0))
            flux_adv = ext_ref[levels + level] * adjoint
            flux_dif = ext_ref[2 * levels + level] * adjoint
            square_one = state * state + 1.0
            slope = (square_one + state * state) / jnp.sqrt(square_one)
            lams[1 - now, level] = (
                adjoint
                - flux_adv
                - 4.0 * flux_dif
                + east(flux_adv)
                + (east(flux_dif) + west(flux_dif) + north(flux_dif) + south(flux_dif))
                + VERTICAL_MIX * vertical(lambda l: lams[now, l], level, adjoint)
                - drag_ref[level] * slope * adjoint
            )
        return carry

    lax.fori_loop(0, steps, backward, 0)
    for level in range(levels):
        sens_out[level] = sens_all[level, :rows, :cols]
    for level in range(levels):
        lam_out[level] = lams[steps % 2, level, :rows, :cols]


def stencil(block, landed, band, drag, levels):
    size_r, size_c = drag.shape[1:]
    depth = block.shape[0]
    vmem = pl.BlockSpec(memory_space=pltpu.VMEM)
    plane = jax.ShapeDtypeStruct((levels,) + block.shape[1:], jnp.float32)
    cells = levels * size_r * size_c
    return pl.pallas_call(
        functools.partial(stencil_kernel, levels, STEPS),
        out_shape=[plane, plane],
        in_specs=[vmem] * 5,
        out_specs=[vmem, vmem],
        scratch_shapes=[
            pltpu.VMEM((depth, size_r, size_c), jnp.float32),
            pltpu.VMEM((STEPS, levels, size_r, size_c), jnp.float32),
            pltpu.VMEM((2, levels, size_r, size_c), jnp.float32),
            pltpu.VMEM((levels, size_r, size_c), jnp.float32),
        ],
        compiler_params=pltpu.CompilerParams(vmem_limit_bytes=48 * 1024 * 1024),
        cost_estimate=pl.CostEstimate(
            flops=60 * STEPS * cells, transcendentals=3 * STEPS * cells, bytes_accessed=28 * cells
        ),
    )(block, landed[1], landed[0], band, drag)


def drag_law(state):
    return state * jnp.sqrt(state * state + 1.0)


def drag_slope(state):
    square_one = state * state + 1.0
    return (square_one + state * state) / jnp.sqrt(square_one)


def vertical(center):
    zero_row = jnp.zeros_like(center[:1])
    from_above = jnp.concatenate([center[1:] - center[:-1], zero_row], axis=0)
    from_below = jnp.concatenate([zero_row, center[:-1] - center[1:]], axis=0)
    return from_above + from_below


def advance(padded, advect, diffuse, drag_coef):
    center = padded[:, 1:-1, 1:-1]
    upwind = padded[:, :-2, 1:-1]
    downwind = padded[:, 2:, 1:-1]
    left_cell = padded[:, 1:-1, :-2]
    right_cell = padded[:, 1:-1, 2:]
    return (
        center
        + advect * (upwind - center)
        + diffuse * (downwind + upwind + right_cell + left_cell - 4.0 * center)
        + VERTICAL_MIX * vertical(center)
        - drag_coef * drag_law(center)
    )


def retreat(padded, advect_ext, diffuse_ext, drag_coef, state):
    flux_adv = advect_ext * padded
    flux_dif = diffuse_ext * padded
    center = padded[:, 1:-1, 1:-1]
    return (
        center
        - flux_adv[:, 1:-1, 1:-1]
        - 4.0 * flux_dif[:, 1:-1, 1:-1]
        + flux_adv[:, 2:, 1:-1]
        + (
            flux_dif[:, 2:, 1:-1]
            + flux_dif[:, :-2, 1:-1]
            + flux_dif[:, 1:-1, 2:]
            + flux_dif[:, 1:-1, :-2]
        )
        + VERTICAL_MIX * vertical(center)
        - drag_coef * drag_slope(state) * center
    )


def trim(array, margin, wanted):
    excess = margin - wanted
    if excess == 0:
        return array
    return array[:, excess:-excess, excess:-excess]


def profiles(first, starts, widths, period, length, inner):
    cells = jnp.arange(length, dtype=jnp.int32)
    cells = jnp.where(cells < inner, cells, cells - length)
    pos = (first + cells - starts[..., None]) % period
    cell_pos = pos.astype(jnp.float32) - (FP - 1) / 2.0
    profile = jnp.exp(-(cell_pos * cell_pos) / (2.0 * widths[..., None] * widths[..., None]))
    return jnp.where(pos < FP, profile, 0.0)


def level_gain():
    level_pos = jnp.arange(LEV, dtype=jnp.float32) - (LEV - 1) / 2.0
    return DRAG_SCALE * jnp.exp(-0.5 * level_pos * level_pos)


def shards(
    velocity, adjoint_seed, courant, viscosity, turbine_tile, turbine_offset, thrust, disk_width
):
    levels, rows, cols = velocity.shape
    n_gx = lax.axis_size("gx")
    n_gy = lax.axis_size("gy")
    m = MARGIN
    per = thrust.shape[0]
    fields = (
        turbine_tile[:, 0].astype(jnp.float32),
        turbine_offset[:, 0].astype(jnp.float32),
        turbine_offset[:, 1].astype(jnp.float32),
        thrust,
        disk_width,
    )
    info_row = jnp.pad(jnp.concatenate(fields)[None, :], ((0, 0), (0, 128 - len(fields) * per)))
    stack = jnp.concatenate([velocity, courant, viscosity, adjoint_seed], axis=0)
    opened = open_exchange(info_row, stack, corner_pieces(stack, m), m)
    info = opened[0]
    tiles = info[:, 0:per].astype(jnp.int32)
    row_start = tiles // n_gy * rows + info[:, per : 2 * per].astype(jnp.int32)
    col_start = tiles % n_gy * cols + info[:, 2 * per : 3 * per].astype(jnp.int32)
    thrusts = info[:, 3 * per : 4 * per]
    widths = info[:, 4 * per : 5 * per]
    gx = lax.axis_index("gx")
    gy = lax.axis_index("gy")
    size_r = -(-(rows + 2 * m) // 8) * 8
    size_c = -(-(cols + 2 * m) // 128) * 128
    inner_r = rows + (size_r - rows) // 2
    inner_c = cols + (size_c - cols) // 2
    prof_r = profiles(gx * rows, row_start, widths, n_gx * rows, size_r, inner_r)
    prof_c = profiles(gy * cols, col_start, widths, n_gy * cols, size_c, inner_c)
    gain = level_gain()
    plane = jnp.einsum("dkr,dkc->rc", thrusts[..., None] * prof_r, prof_c, precision=HIGHEST)
    drag = gain[:, None, None] * plane[None]
    band = column_band(opened[1:], m, size_r, size_c, cols)
    adjoint_full, sens_full = stencil(stack, opened[1:], band, drag, levels)
    adjoint = adjoint_full
    sensitivity = sens_full

    weighted = jnp.einsum("l,lrc->rc", gain, sensitivity, precision=HIGHEST)
    own_r = prof_r[..., :rows]
    own_c = prof_c[..., :cols]
    across = jnp.einsum("rc,dkc->dkr", weighted, own_c, precision=HIGHEST)
    totals = jnp.sum(own_r * across, axis=2)
    values = thrusts * totals
    spread = jnp.pad(values, ((0, 0), (0, 128 - per)))
    grad = close_scatter(spread)[0, :per]
    return adjoint, grad


def solution(mesh):
    placed = (
        P(None, "gx", "gy"),
        P(None, "gx", "gy"),
        P(None, "gx", "gy"),
        P(None, "gx", "gy"),
        P(("gx", "gy"), None),
        P(("gx", "gy"), None),
        P(("gx", "gy")),
        P(("gx", "gy")),
    )
    return jax.shard_map(
        shards,
        mesh=mesh,
        in_specs=placed,
        out_specs=(P(None, "gx", "gy"), P(("gx", "gy"))),
        check_vma=False,
    )
```

```python
import functools

import jax
import jax.numpy as jnp
from jax import lax
from jax.experimental import pallas as pl
from jax.experimental.pallas import tpu as pltpu
from jax.sharding import PartitionSpec as P

LEV = 3
STEPS = 8
FP = 64
MARGIN = 2 * STEPS

VERTICAL_MIX = 0.05
DRAG_SCALE = 0.01
HIGHEST = lax.Precision.HIGHEST


MESH_ID = pl.DeviceIdType.MESH


HALO_MOVES = ((1, 0), (-1, 0), (0, 1), (0, -1), (1, 1), (1, -1), (-1, 1), (-1, -1))


def enter(n_gy, n_dev, me):
    barrier = pltpu.get_barrier_semaphore()
    for step in range(1, n_dev):
        target = lax.rem(me + step, n_dev)
        pl.semaphore_signal(
            barrier, inc=1, device_id=(target // n_gy, target % n_gy), device_id_type=MESH_ID
        )
    pl.semaphore_wait(barrier, n_dev - 1)


def spread_rows(n_gy, n_dev, me, src_of, slots, send_sem, recv_sem):
    for step in range(1, n_dev):
        target = lax.rem(me + step, n_dev)
        pltpu.make_async_remote_copy(
            src_of(target),
            slots.at[pl.ds(me, 1)],
            send_sem,
            recv_sem,
            device_id=(target // n_gy, target % n_gy),
            device_id_type=MESH_ID,
        ).start()
    first = lax.rem(me + 1, n_dev)
    rest = pl.ds(0, n_dev - 1)
    return pltpu.make_async_remote_copy(
        slots.at[rest],
        slots.at[rest],
        send_sem,
        recv_sem,
        device_id=(first // n_gy, first % n_gy),
        device_id_type=MESH_ID,
    )


def open_kernel(n_gx, n_gy, m, n_block, info_ref, *refs):
    n_dev = n_gx * n_gy
    n_corner = len(HALO_MOVES) - 4
    blocks = refs[:n_block]
    corners = refs[n_block : n_block + n_corner]
    gathered = refs[n_block + n_corner]
    landed = refs[n_block + n_corner + 1 : n_block + n_corner + 1 + len(HALO_MOVES)]
    columns, slots, send_sem, recv_sem, local_sem, halo_send, halo_recv = refs[
        n_block + n_corner + 1 + len(HALO_MOVES) :
    ]
    levels, rows, cols = blocks[0].shape
    for field, block_ref in enumerate(blocks):
        for level in range(levels):
            turned = block_ref[level].T
            columns[0, field * levels + level] = turned[cols - m :]
            columns[1, field * levels + level] = turned[:m]
    gx = lax.axis_index("gx")
    gy = lax.axis_index("gy")
    me = gx * n_gy + gy
    enter(n_gy, n_dev, me)
    local = pltpu.make_async_copy(info_ref, slots.at[pl.ds(me, 1)], local_sem)
    local.start()
    parts = lambda window: [
        (block_ref.at[:, window, :], pl.ds(field * levels, levels))
        for field, block_ref in enumerate(blocks)
    ]
    whole = pl.ds(0, n_block * levels)
    sources = (
        parts(pl.ds(rows - m, m)),
        parts(pl.ds(0, m)),
        [(columns.at[0], whole)],
        [(columns.at[1], whole)],
    ) + tuple([(corner, whole)] for corner in corners)
    waits = []
    for index, (dx, dy) in enumerate(HALO_MOVES):
        target = (lax.rem(gx + dx + n_gx, n_gx), lax.rem(gy + dy + n_gy, n_gy))
        for source, depth in sources[index]:
            pltpu.make_async_remote_copy(
                source,
                landed[index].at[depth],
                halo_send.at[index],
                halo_recv.at[index],
                device_id=target,
                device_id_type=MESH_ID,
            ).start()
        waits.append(
            pltpu.make_async_remote_copy(
                landed[index],
                landed[index],
                halo_send.at[index],
                halo_recv.at[index],
                device_id=target,
                device_id_type=MESH_ID,
            )
        )
    every = spread_rows(n_gy, n_dev, me, lambda target: info_ref, slots, send_sem, recv_sem)
    local.wait()
    for copy in waits:
        copy.wait_send()
        copy.wait_recv()
    every.wait_send()
    every.wait_recv()
    gathered[...] = slots[...]


def open_exchange(info_row, blocks, corners, m):
    n_gx = lax.axis_size("gx")
    n_gy = lax.axis_size("gy")
    n_dev = n_gx * n_gy
    levels, rows, cols = blocks[0].shape
    depth = levels * len(blocks)
    vmem = pl.BlockSpec(memory_space=pltpu.VMEM)
    piece_shapes = [(depth, m, cols), (depth, m, cols), (depth, m, rows), (depth, m, rows)]
    piece_shapes += [corner.shape for corner in corners]
    out_shape = [jax.ShapeDtypeStruct((n_dev, info_row.shape[1]), jnp.float32)] + [
        jax.ShapeDtypeStruct(shape, jnp.float32) for shape in piece_shapes
    ]
    return pl.pallas_call(
        functools.partial(open_kernel, n_gx, n_gy, m, len(blocks)),
        out_shape=out_shape,
        in_specs=[vmem] * (1 + len(blocks) + len(corners)),
        out_specs=[vmem] * len(out_shape),
        scratch_shapes=[
            pltpu.VMEM((2, depth, m, rows), jnp.float32),
            pltpu.VMEM((n_dev, info_row.shape[1]), jnp.float32),
            pltpu.SemaphoreType.DMA,
            pltpu.SemaphoreType.DMA,
            pltpu.SemaphoreType.DMA,
            pltpu.SemaphoreType.DMA((len(piece_shapes),)),
            pltpu.SemaphoreType.DMA((len(piece_shapes),)),
        ],
        compiler_params=pltpu.CompilerParams(has_side_effects=True, collective_id=0),
    )(info_row, *blocks, *corners)


def close_kernel(n_gy, n_dev, src_ref, out_ref, slots, send_sem, recv_sem, local_sem):
    gx = lax.axis_index("gx")
    gy = lax.axis_index("gy")
    me = gx * n_gy + gy
    enter(n_gy, n_dev, me)
    local = pltpu.make_async_copy(src_ref.at[pl.ds(me, 1)], slots.at[pl.ds(me, 1)], local_sem)
    local.start()
    every = spread_rows(
        n_gy, n_dev, me, lambda target: src_ref.at[pl.ds(target, 1)], slots, send_sem, recv_sem
    )
    local.wait()
    every.wait_send()
    every.wait_recv()
    out_ref[...] = jnp.sum(slots[...], axis=0, keepdims=True)


def close_scatter(rows):
    n_gy = lax.axis_size("gy")
    n_dev = lax.axis_size("gx") * n_gy
    vmem = pl.BlockSpec(memory_space=pltpu.VMEM)
    return pl.pallas_call(
        functools.partial(close_kernel, n_gy, n_dev),
        out_shape=jax.ShapeDtypeStruct((1, rows.shape[1]), jnp.float32),
        in_specs=[vmem],
        out_specs=vmem,
        scratch_shapes=[
            pltpu.VMEM(rows.shape, jnp.float32),
            pltpu.SemaphoreType.DMA,
            pltpu.SemaphoreType.DMA,
            pltpu.SemaphoreType.DMA,
        ],
        compiler_params=pltpu.CompilerParams(has_side_effects=True, collective_id=1),
    )(rows)


def corner_pieces(blocks, m):
    block = jnp.concatenate(
        [jnp.concatenate([piece[:, :m], piece[:, -m:]], axis=1) for piece in blocks], axis=0
    )
    last_r, first_r = block[:, -m:, :], block[:, :m, :]
    return (
        jnp.swapaxes(last_r[:, :, -m:], 1, 2),
        jnp.swapaxes(last_r[:, :, :m], 1, 2),
        jnp.swapaxes(first_r[:, :, -m:], 1, 2),
        jnp.swapaxes(first_r[:, :, :m], 1, 2),
    )


def column_band(landed, m, size_r, size_c, cols):
    row_low, row_high, col_low, col_high, c_ll, c_lh, c_hl, c_hh = landed
    depth = col_low.shape[0]
    width = size_c - cols
    span = -(-size_r // 128) * 128

    def edge(column, high_corner, low_corner):
        fill = jnp.zeros((depth, m, span - size_r), jnp.float32)
        return jnp.concatenate(
            [column, high_corner, low_corner, fill],
            axis=2,
        )

    fill = jnp.zeros((depth, width - 2 * m, span), jnp.float32)
    return jnp.concatenate([edge(col_high, c_hh, c_lh), fill, edge(col_low, c_hl, c_ll)], axis=1)


def stencil_kernel(levels, steps, n_block, *refs):
    blocks = refs[:n_block]
    high_ref, low_ref, band_ref, drag_ref, lam_out, sens_out, ext_ref, states, lams, sens_all = refs[
        n_block:
    ]
    size_r, size_c = ext_ref.shape[1:]
    rows, cols = blocks[0].shape[1:]
    m = high_ref.shape[1]
    for depth in range(ext_ref.shape[0]):
        ext_ref[depth, :rows, :cols] = blocks[depth // levels][depth % levels]
        ext_ref[depth, rows : rows + m, :cols] = high_ref[depth]
        ext_ref[depth, size_r - m :, :cols] = low_ref[depth]
        ext_ref[depth, :, cols:] = band_ref[depth].T[:size_r]

    def west(x):
        return pltpu.roll(x, 1, 0)

    def east(x):
        return pltpu.roll(x, size_r - 1, 0)

    def south(x):
        return pltpu.roll(x, 1, 1)

    def north(x):
        return pltpu.roll(x, size_c - 1, 1)

    def vertical(plane, level, center):
        mix = None
        if level + 1 < levels:
            mix = plane(level + 1) - center
        if level > 0:
            below = plane(level - 1) - center
            mix = below if mix is None else mix + below
        return mix

    for level in range(levels):
        states[0, level] = ext_ref[level]

    def forward(n, carry):
        for level in range(levels):
            center = states[n, level]
            upwind = west(center)
            advect = ext_ref[levels + level]
            diffuse = ext_ref[2 * levels + level]
            states[n + 1, level] = (
                center
                + advect * (upwind - center)
                + diffuse * (east(center) + upwind + north(center) + south(center) - 4.0 * center)
                + VERTICAL_MIX * vertical(lambda l: states[n, l], level, center)
                - drag_ref[level] * (center * jnp.sqrt(center * center + 1.0))
            )
        return carry

    lax.fori_loop(0, steps - 1, forward, 0)
    for level in range(levels):
        lams[0, level] = ext_ref[3 * levels + level]
        sens_all[level] = jnp.zeros(sens_all.shape[1:], jnp.float32)

    def backward(i, carry):
        n = steps - 1 - i
        now = i % 2
        for level in range(levels):
            adjoint = lams[now, level]
            state = states[n, level]
            sens_all[level] = sens_all[level] - adjoint * (state * jnp.sqrt(state * state + 1.0))
            flux_adv = ext_ref[levels + level] * adjoint
            flux_dif = ext_ref[2 * levels + level] * adjoint
            square_one = state * state + 1.0
            slope = (square_one + state * state) / jnp.sqrt(square_one)
            lams[1 - now, level] = (
                adjoint
                - flux_adv
                - 4.0 * flux_dif
                + east(flux_adv)
                + (east(flux_dif) + west(flux_dif) + north(flux_dif) + south(flux_dif))
                + VERTICAL_MIX * vertical(lambda l: lams[now, l], level, adjoint)
                - drag_ref[level] * slope * adjoint
            )
        return carry

    lax.fori_loop(0, steps, backward, 0)
    for level in range(levels):
        sens_out[level] = sens_all[level, :rows, :cols]
    for level in range(levels):
        lam_out[level] = lams[steps % 2, level, :rows, :cols]


def stencil(blocks, landed, band, drag, levels):
    size_r, size_c = drag.shape[1:]
    depth = levels * len(blocks)
    vmem = pl.BlockSpec(memory_space=pltpu.VMEM)
    plane = jax.ShapeDtypeStruct(blocks[0].shape, jnp.float32)
    cells = levels * size_r * size_c
    return pl.pallas_call(
        functools.partial(stencil_kernel, levels, STEPS, len(blocks)),
        out_shape=[plane, plane],
        in_specs=[vmem] * (len(blocks) + 4),
        out_specs=[vmem, vmem],
        scratch_shapes=[
            pltpu.VMEM((depth, size_r, size_c), jnp.float32),
            pltpu.VMEM((STEPS, levels, size_r, size_c), jnp.float32),
            pltpu.VMEM((2, levels, size_r, size_c), jnp.float32),
            pltpu.VMEM((levels, size_r, size_c), jnp.float32),
        ],
        compiler_params=pltpu.CompilerParams(vmem_limit_bytes=48 * 1024 * 1024),
        cost_estimate=pl.CostEstimate(
            flops=60 * STEPS * cells, transcendentals=3 * STEPS * cells, bytes_accessed=28 * cells
        ),
    )(*blocks, landed[1], landed[0], band, drag)


def drag_law(state):
    return state * jnp.sqrt(state * state + 1.0)


def drag_slope(state):
    square_one = state * state + 1.0
    return (square_one + state * state) / jnp.sqrt(square_one)


def vertical(center):
    zero_row = jnp.zeros_like(center[:1])
    from_above = jnp.concatenate([center[1:] - center[:-1], zero_row], axis=0)
    from_below = jnp.concatenate([zero_row, center[:-1] - center[1:]], axis=0)
    return from_above + from_below


def advance(padded, advect, diffuse, drag_coef):
    center = padded[:, 1:-1, 1:-1]
    upwind = padded[:, :-2, 1:-1]
    downwind = padded[:, 2:, 1:-1]
    left_cell = padded[:, 1:-1, :-2]
    right_cell = padded[:, 1:-1, 2:]
    return (
        center
        + advect * (upwind - center)
        + diffuse * (downwind + upwind + right_cell + left_cell - 4.0 * center)
        + VERTICAL_MIX * vertical(center)
        - drag_coef * drag_law(center)
    )


def retreat(padded, advect_ext, diffuse_ext, drag_coef, state):
    flux_adv = advect_ext * padded
    flux_dif = diffuse_ext * padded
    center = padded[:, 1:-1, 1:-1]
    return (
        center
        - flux_adv[:, 1:-1, 1:-1]
        - 4.0 * flux_dif[:, 1:-1, 1:-1]
        + flux_adv[:, 2:, 1:-1]
        + (
            flux_dif[:, 2:, 1:-1]
            + flux_dif[:, :-2, 1:-1]
            + flux_dif[:, 1:-1, 2:]
            + flux_dif[:, 1:-1, :-2]
        )
        + VERTICAL_MIX * vertical(center)
        - drag_coef * drag_slope(state) * center
    )


def trim(array, margin, wanted):
    excess = margin - wanted
    if excess == 0:
        return array
    return array[:, excess:-excess, excess:-excess]


def profiles(first, starts, widths, period, length, inner):
    cells = jnp.arange(length, dtype=jnp.int32)
    cells = jnp.where(cells < inner, cells, cells - length)
    pos = (first + cells - starts[..., None]) % period
    cell_pos = pos.astype(jnp.float32) - (FP - 1) / 2.0
    profile = jnp.exp(-(cell_pos * cell_pos) / (2.0 * widths[..., None] * widths[..., None]))
    return jnp.where(pos < FP, profile, 0.0)


def level_gain():
    level_pos = jnp.arange(LEV, dtype=jnp.float32) - (LEV - 1) / 2.0
    return DRAG_SCALE * jnp.exp(-0.5 * level_pos * level_pos)


def shards(
    velocity, adjoint_seed, courant, viscosity, turbine_tile, turbine_offset, thrust, disk_width
):
    levels, rows, cols = velocity.shape
    n_gx = lax.axis_size("gx")
    n_gy = lax.axis_size("gy")
    m = MARGIN
    per = thrust.shape[0]
    fields = (
        turbine_tile[:, 0].astype(jnp.float32),
        turbine_offset[:, 0].astype(jnp.float32),
        turbine_offset[:, 1].astype(jnp.float32),
        thrust,
        disk_width,
    )
    info_row = jnp.pad(jnp.concatenate(fields)[None, :], ((0, 0), (0, 128 - len(fields) * per)))
    blocks = (velocity, courant, viscosity, adjoint_seed)
    opened = open_exchange(info_row, blocks, corner_pieces(blocks, m), m)
    info = opened[0]
    tiles = info[:, 0:per].astype(jnp.int32)
    row_start = tiles // n_gy * rows + info[:, per : 2 * per].astype(jnp.int32)
    col_start = tiles % n_gy * cols + info[:, 2 * per : 3 * per].astype(jnp.int32)
    thrusts = info[:, 3 * per : 4 * per]
    widths = info[:, 4 * per : 5 * per]
    gx = lax.axis_index("gx")
    gy = lax.axis_index("gy")
    size_r = -(-(rows + 2 * m) // 8) * 8
    size_c = -(-(cols + 2 * m) // 128) * 128
    inner_r = rows + (size_r - rows) // 2
    inner_c = cols + (size_c - cols) // 2
    prof_r = profiles(gx * rows, row_start, widths, n_gx * rows, size_r, inner_r)
    prof_c = profiles(gy * cols, col_start, widths, n_gy * cols, size_c, inner_c)
    gain = level_gain()
    plane = jnp.einsum("dkr,dkc->rc", thrusts[..., None] * prof_r, prof_c, precision=HIGHEST)
    drag = gain[:, None, None] * plane[None]
    band = column_band(opened[1:], m, size_r, size_c, cols)
    adjoint_full, sens_full = stencil(blocks, opened[1:], band, drag, levels)
    adjoint = adjoint_full
    sensitivity = sens_full

    weighted = jnp.einsum("l,lrc->rc", gain, sensitivity, precision=HIGHEST)
    own_r = prof_r[..., :rows]
    own_c = prof_c[..., :cols]
    across = jnp.einsum("rc,dkc->dkr", weighted, own_c, precision=HIGHEST)
    totals = jnp.sum(own_r * across, axis=2)
    values = thrusts * totals
    spread = jnp.pad(values, ((0, 0), (0, 128 - per)))
    grad = close_scatter(spread)[0, :per]
    return adjoint, grad


def solution(mesh):
    placed = (
        P(None, "gx", "gy"),
        P(None, "gx", "gy"),
        P(None, "gx", "gy"),
        P(None, "gx", "gy"),
        P(("gx", "gy"), None),
        P(("gx", "gy"), None),
        P(("gx", "gy")),
        P(("gx", "gy")),
    )
    return jax.shard_map(
        shards,
        mesh=mesh,
        in_specs=placed,
        out_specs=(P(None, "gx", "gy"), P(("gx", "gy"))),
        check_vma=False,
    )
```

```python
import functools

import jax
import jax.numpy as jnp
from jax import lax
from jax.experimental import pallas as pl
from jax.experimental.pallas import tpu as pltpu
from jax.sharding import PartitionSpec as P

LEV = 3
STEPS = 8
FP = 64
MARGIN = 2 * STEPS

VERTICAL_MIX = 0.05
DRAG_SCALE = 0.01
HIGHEST = lax.Precision.HIGHEST


MESH_ID = pl.DeviceIdType.MESH


HALO_MOVES = ((1, 0), (-1, 0), (0, 1), (0, -1), (1, 1), (1, -1), (-1, 1), (-1, -1))


def enter(n_gy, n_dev, me):
    barrier = pltpu.get_barrier_semaphore()
    for step in range(1, n_dev):
        target = lax.rem(me + step, n_dev)
        pl.semaphore_signal(
            barrier, inc=1, device_id=(target // n_gy, target % n_gy), device_id_type=MESH_ID
        )
    pl.semaphore_wait(barrier, n_dev - 1)


def spread_rows(n_gy, n_dev, me, src_of, slots, send_sem, recv_sem):
    for step in range(1, n_dev):
        target = lax.rem(me + step, n_dev)
        pltpu.make_async_remote_copy(
            src_of(target),
            slots.at[pl.ds(me, 1)],
            send_sem,
            recv_sem,
            device_id=(target // n_gy, target % n_gy),
            device_id_type=MESH_ID,
        ).start()
    first = lax.rem(me + 1, n_dev)
    rest = pl.ds(0, n_dev - 1)
    return pltpu.make_async_remote_copy(
        slots.at[rest],
        slots.at[rest],
        send_sem,
        recv_sem,
        device_id=(first // n_gy, first % n_gy),
        device_id_type=MESH_ID,
    )


def open_kernel(n_gx, n_gy, m, n_block, info_ref, *refs):
    n_dev = n_gx * n_gy
    n_corner = 0
    blocks = refs[:n_block]
    gathered = refs[n_block + n_corner]
    landed = refs[n_block + n_corner + 1 : n_block + n_corner + 1 + len(HALO_MOVES)]
    columns, corners, slots, send_sem, recv_sem, local_sem, halo_send, halo_recv = refs[
        n_block + n_corner + 1 + len(HALO_MOVES) :
    ]
    levels, rows, cols = blocks[0].shape
    for field, block_ref in enumerate(blocks):
        for level in range(levels):
            turned = block_ref[level].T
            depth = field * levels + level
            columns[0, depth] = turned[cols - m :]
            columns[1, depth] = turned[:m]
            for index, (side, window) in enumerate(
                ((cols - m, rows - m), (0, rows - m), (cols - m, 0), (0, 0))
            ):
                corners[index, depth] = turned[side : side + m, window : window + m]
    gx = lax.axis_index("gx")
    gy = lax.axis_index("gy")
    me = gx * n_gy + gy
    enter(n_gy, n_dev, me)
    local = pltpu.make_async_copy(info_ref, slots.at[pl.ds(me, 1)], local_sem)
    local.start()
    parts = lambda window: [
        (block_ref.at[:, window, :], pl.ds(field * levels, levels))
        for field, block_ref in enumerate(blocks)
    ]
    whole = pl.ds(0, n_block * levels)
    sources = (
        parts(pl.ds(rows - m, m)),
        parts(pl.ds(0, m)),
        [(columns.at[0], whole)],
        [(columns.at[1], whole)],
    ) + tuple([(corners.at[index], whole)] for index in range(len(HALO_MOVES) - 4))
    waits = []
    for index, (dx, dy) in enumerate(HALO_MOVES):
        target = (lax.rem(gx + dx + n_gx, n_gx), lax.rem(gy + dy + n_gy, n_gy))
        for source, depth in sources[index]:
            pltpu.make_async_remote_copy(
                source,
                landed[index].at[depth],
                halo_send.at[index],
                halo_recv.at[index],
                device_id=target,
                device_id_type=MESH_ID,
            ).start()
        waits.append(
            pltpu.make_async_remote_copy(
                landed[index],
                landed[index],
                halo_send.at[index],
                halo_recv.at[index],
                device_id=target,
                device_id_type=MESH_ID,
            )
        )
    every = spread_rows(n_gy, n_dev, me, lambda target: info_ref, slots, send_sem, recv_sem)
    local.wait()
    for copy in waits:
        copy.wait_send()
        copy.wait_recv()
    every.wait_send()
    every.wait_recv()
    gathered[...] = slots[...]


def open_exchange(info_row, blocks, m):
    n_gx = lax.axis_size("gx")
    n_gy = lax.axis_size("gy")
    n_dev = n_gx * n_gy
    levels, rows, cols = blocks[0].shape
    depth = levels * len(blocks)
    vmem = pl.BlockSpec(memory_space=pltpu.VMEM)
    piece_shapes = [(depth, m, cols), (depth, m, cols), (depth, m, rows), (depth, m, rows)]
    piece_shapes += [(depth, m, m)] * (len(HALO_MOVES) - 4)
    out_shape = [jax.ShapeDtypeStruct((n_dev, info_row.shape[1]), jnp.float32)] + [
        jax.ShapeDtypeStruct(shape, jnp.float32) for shape in piece_shapes
    ]
    return pl.pallas_call(
        functools.partial(open_kernel, n_gx, n_gy, m, len(blocks)),
        out_shape=out_shape,
        in_specs=[vmem] * (1 + len(blocks)),
        out_specs=[vmem] * len(out_shape),
        scratch_shapes=[
            pltpu.VMEM((2, depth, m, rows), jnp.float32),
            pltpu.VMEM((len(HALO_MOVES) - 4, depth, m, m), jnp.float32),
            pltpu.VMEM((n_dev, info_row.shape[1]), jnp.float32),
            pltpu.SemaphoreType.DMA,
            pltpu.SemaphoreType.DMA,
            pltpu.SemaphoreType.DMA,
            pltpu.SemaphoreType.DMA((len(piece_shapes),)),
            pltpu.SemaphoreType.DMA((len(piece_shapes),)),
        ],
        compiler_params=pltpu.CompilerParams(has_side_effects=True, collective_id=0),
    )(info_row, *blocks)


def close_kernel(n_gy, n_dev, src_ref, out_ref, slots, send_sem, recv_sem, local_sem):
    gx = lax.axis_index("gx")
    gy = lax.axis_index("gy")
    me = gx * n_gy + gy
    enter(n_gy, n_dev, me)
    local = pltpu.make_async_copy(src_ref.at[pl.ds(me, 1)], slots.at[pl.ds(me, 1)], local_sem)
    local.start()
    every = spread_rows(
        n_gy, n_dev, me, lambda target: src_ref.at[pl.ds(target, 1)], slots, send_sem, recv_sem
    )
    local.wait()
    every.wait_send()
    every.wait_recv()
    out_ref[...] = jnp.sum(slots[...], axis=0, keepdims=True)


def close_scatter(rows):
    n_gy = lax.axis_size("gy")
    n_dev = lax.axis_size("gx") * n_gy
    vmem = pl.BlockSpec(memory_space=pltpu.VMEM)
    return pl.pallas_call(
        functools.partial(close_kernel, n_gy, n_dev),
        out_shape=jax.ShapeDtypeStruct((1, rows.shape[1]), jnp.float32),
        in_specs=[vmem],
        out_specs=vmem,
        scratch_shapes=[
            pltpu.VMEM(rows.shape, jnp.float32),
            pltpu.SemaphoreType.DMA,
            pltpu.SemaphoreType.DMA,
            pltpu.SemaphoreType.DMA,
        ],
        compiler_params=pltpu.CompilerParams(has_side_effects=True, collective_id=1),
    )(rows)


def column_band(landed, m, size_r, size_c, cols):
    row_low, row_high, col_low, col_high, c_ll, c_lh, c_hl, c_hh = landed
    depth = col_low.shape[0]
    width = size_c - cols
    span = -(-size_r // 128) * 128

    def edge(column, high_corner, low_corner):
        fill = jnp.zeros((depth, m, span - size_r), jnp.float32)
        return jnp.concatenate(
            [column, high_corner, low_corner, fill],
            axis=2,
        )

    fill = jnp.zeros((depth, width - 2 * m, span), jnp.float32)
    return jnp.concatenate([edge(col_high, c_hh, c_lh), fill, edge(col_low, c_hl, c_ll)], axis=1)


def stencil_kernel(levels, steps, n_block, *refs):
    blocks = refs[:n_block]
    high_ref, low_ref, band_ref, drag_ref, lam_out, sens_out, ext_ref, states, lams, sens_all = refs[
        n_block:
    ]
    size_r, size_c = ext_ref.shape[1:]
    rows, cols = blocks[0].shape[1:]
    m = high_ref.shape[1]
    for depth in range(ext_ref.shape[0]):
        ext_ref[depth, :rows, :cols] = blocks[depth // levels][depth % levels]
        ext_ref[depth, rows : rows + m, :cols] = high_ref[depth]
        ext_ref[depth, size_r - m :, :cols] = low_ref[depth]
        ext_ref[depth, :, cols:] = band_ref[depth].T[:size_r]

    def west(x):
        return pltpu.roll(x, 1, 0)

    def east(x):
        return pltpu.roll(x, size_r - 1, 0)

    def south(x):
        return pltpu.roll(x, 1, 1)

    def north(x):
        return pltpu.roll(x, size_c - 1, 1)

    def vertical(plane, level, center):
        mix = None
        if level + 1 < levels:
            mix = plane(level + 1) - center
        if level > 0:
            below = plane(level - 1) - center
            mix = below if mix is None else mix + below
        return mix

    for level in range(levels):
        states[0, level] = ext_ref[level]

    def forward(n, carry):
        for level in range(levels):
            center = states[n, level]
            upwind = west(center)
            advect = ext_ref[levels + level]
            diffuse = ext_ref[2 * levels + level]
            states[n + 1, level] = (
                center
                + advect * (upwind - center)
                + diffuse * (east(center) + upwind + north(center) + south(center) - 4.0 * center)
                + VERTICAL_MIX * vertical(lambda l: states[n, l], level, center)
                - drag_ref[level] * (center * jnp.sqrt(center * center + 1.0))
            )
        return carry

    lax.fori_loop(0, steps - 1, forward, 0)
    for level in range(levels):
        lams[0, level] = ext_ref[3 * levels + level]
        sens_all[level] = jnp.zeros(sens_all.shape[1:], jnp.float32)

    def backward(i, carry):
        n = steps - 1 - i
        now = i % 2
        for level in range(levels):
            adjoint = lams[now, level]
            state = states[n, level]
            sens_all[level] = sens_all[level] - adjoint * (state * jnp.sqrt(state * state + 1.0))
            flux_adv = ext_ref[levels + level] * adjoint
            flux_dif = ext_ref[2 * levels + level] * adjoint
            square_one = state * state + 1.0
            slope = (square_one + state * state) / jnp.sqrt(square_one)
            lams[1 - now, level] = (
                adjoint
                - flux_adv
                - 4.0 * flux_dif
                + east(flux_adv)
                + (east(flux_dif) + west(flux_dif) + north(flux_dif) + south(flux_dif))
                + VERTICAL_MIX * vertical(lambda l: lams[now, l], level, adjoint)
                - drag_ref[level] * slope * adjoint
            )
        return carry

    lax.fori_loop(0, steps, backward, 0)
    for level in range(levels):
        sens_out[level] = sens_all[level, :rows, :cols]
    for level in range(levels):
        lam_out[level] = lams[steps % 2, level, :rows, :cols]


def stencil(blocks, landed, band, drag, levels):
    size_r, size_c = drag.shape[1:]
    depth = levels * len(blocks)
    vmem = pl.BlockSpec(memory_space=pltpu.VMEM)
    plane = jax.ShapeDtypeStruct(blocks[0].shape, jnp.float32)
    cells = levels * size_r * size_c
    return pl.pallas_call(
        functools.partial(stencil_kernel, levels, STEPS, len(blocks)),
        out_shape=[plane, plane],
        in_specs=[vmem] * (len(blocks) + 4),
        out_specs=[vmem, vmem],
        scratch_shapes=[
            pltpu.VMEM((depth, size_r, size_c), jnp.float32),
            pltpu.VMEM((STEPS, levels, size_r, size_c), jnp.float32),
            pltpu.VMEM((2, levels, size_r, size_c), jnp.float32),
            pltpu.VMEM((levels, size_r, size_c), jnp.float32),
        ],
        compiler_params=pltpu.CompilerParams(vmem_limit_bytes=48 * 1024 * 1024),
        cost_estimate=pl.CostEstimate(
            flops=60 * STEPS * cells, transcendentals=3 * STEPS * cells, bytes_accessed=28 * cells
        ),
    )(*blocks, landed[1], landed[0], band, drag)


def drag_law(state):
    return state * jnp.sqrt(state * state + 1.0)


def drag_slope(state):
    square_one = state * state + 1.0
    return (square_one + state * state) / jnp.sqrt(square_one)


def vertical(center):
    zero_row = jnp.zeros_like(center[:1])
    from_above = jnp.concatenate([center[1:] - center[:-1], zero_row], axis=0)
    from_below = jnp.concatenate([zero_row, center[:-1] - center[1:]], axis=0)
    return from_above + from_below


def advance(padded, advect, diffuse, drag_coef):
    center = padded[:, 1:-1, 1:-1]
    upwind = padded[:, :-2, 1:-1]
    downwind = padded[:, 2:, 1:-1]
    left_cell = padded[:, 1:-1, :-2]
    right_cell = padded[:, 1:-1, 2:]
    return (
        center
        + advect * (upwind - center)
        + diffuse * (downwind + upwind + right_cell + left_cell - 4.0 * center)
        + VERTICAL_MIX * vertical(center)
        - drag_coef * drag_law(center)
    )


def retreat(padded, advect_ext, diffuse_ext, drag_coef, state):
    flux_adv = advect_ext * padded
    flux_dif = diffuse_ext * padded
    center = padded[:, 1:-1, 1:-1]
    return (
        center
        - flux_adv[:, 1:-1, 1:-1]
        - 4.0 * flux_dif[:, 1:-1, 1:-1]
        + flux_adv[:, 2:, 1:-1]
        + (
            flux_dif[:, 2:, 1:-1]
            + flux_dif[:, :-2, 1:-1]
            + flux_dif[:, 1:-1, 2:]
            + flux_dif[:, 1:-1, :-2]
        )
        + VERTICAL_MIX * vertical(center)
        - drag_coef * drag_slope(state) * center
    )


def trim(array, margin, wanted):
    excess = margin - wanted
    if excess == 0:
        return array
    return array[:, excess:-excess, excess:-excess]


def profiles(first, starts, widths, period, length, inner):
    cells = jnp.arange(length, dtype=jnp.int32)
    cells = jnp.where(cells < inner, cells, cells - length)
    pos = (first + cells - starts[..., None]) % period
    cell_pos = pos.astype(jnp.float32) - (FP - 1) / 2.0
    profile = jnp.exp(-(cell_pos * cell_pos) / (2.0 * widths[..., None] * widths[..., None]))
    return jnp.where(pos < FP, profile, 0.0)


def level_gain():
    level_pos = jnp.arange(LEV, dtype=jnp.float32) - (LEV - 1) / 2.0
    return DRAG_SCALE * jnp.exp(-0.5 * level_pos * level_pos)


def shards(
    velocity, adjoint_seed, courant, viscosity, turbine_tile, turbine_offset, thrust, disk_width
):
    levels, rows, cols = velocity.shape
    n_gx = lax.axis_size("gx")
    n_gy = lax.axis_size("gy")
    m = MARGIN
    per = thrust.shape[0]
    fields = (
        turbine_tile[:, 0].astype(jnp.float32),
        turbine_offset[:, 0].astype(jnp.float32),
        turbine_offset[:, 1].astype(jnp.float32),
        thrust,
        disk_width,
    )
    info_row = jnp.pad(jnp.concatenate(fields)[None, :], ((0, 0), (0, 128 - len(fields) * per)))
    blocks = (velocity, courant, viscosity, adjoint_seed)
    opened = open_exchange(info_row, blocks, m)
    info = opened[0]
    tiles = info[:, 0:per].astype(jnp.int32)
    row_start = tiles // n_gy * rows + info[:, per : 2 * per].astype(jnp.int32)
    col_start = tiles % n_gy * cols + info[:, 2 * per : 3 * per].astype(jnp.int32)
    thrusts = info[:, 3 * per : 4 * per]
    widths = info[:, 4 * per : 5 * per]
    gx = lax.axis_index("gx")
    gy = lax.axis_index("gy")
    size_r = -(-(rows + 2 * m) // 8) * 8
    size_c = -(-(cols + 2 * m) // 128) * 128
    inner_r = rows + (size_r - rows) // 2
    inner_c = cols + (size_c - cols) // 2
    prof_r = profiles(gx * rows, row_start, widths, n_gx * rows, size_r, inner_r)
    prof_c = profiles(gy * cols, col_start, widths, n_gy * cols, size_c, inner_c)
    gain = level_gain()
    plane = jnp.einsum("dkr,dkc->rc", thrusts[..., None] * prof_r, prof_c, precision=HIGHEST)
    drag = gain[:, None, None] * plane[None]
    band = column_band(opened[1:], m, size_r, size_c, cols)
    adjoint_full, sens_full = stencil(blocks, opened[1:], band, drag, levels)
    adjoint = adjoint_full
    sensitivity = sens_full

    weighted = jnp.einsum("l,lrc->rc", gain, sensitivity, precision=HIGHEST)
    own_r = prof_r[..., :rows]
    own_c = prof_c[..., :cols]
    across = jnp.einsum("rc,dkc->dkr", weighted, own_c, precision=HIGHEST)
    totals = jnp.sum(own_r * across, axis=2)
    values = thrusts * totals
    spread = jnp.pad(values, ((0, 0), (0, 128 - per)))
    grad = close_scatter(spread)[0, :per]
    return adjoint, grad


def solution(mesh):
    placed = (
        P(None, "gx", "gy"),
        P(None, "gx", "gy"),
        P(None, "gx", "gy"),
        P(None, "gx", "gy"),
        P(("gx", "gy"), None),
        P(("gx", "gy"), None),
        P(("gx", "gy")),
        P(("gx", "gy")),
    )
    return jax.shard_map(
        shards,
        mesh=mesh,
        in_specs=placed,
        out_specs=(P(None, "gx", "gy"), P(("gx", "gy"))),
        check_vma=False,
    )
```

```python
import functools

import jax
import jax.numpy as jnp
from jax import lax
from jax.experimental import pallas as pl
from jax.experimental.pallas import tpu as pltpu
from jax.sharding import PartitionSpec as P

LEV = 3
STEPS = 8
FP = 64
MARGIN = 2 * STEPS

VERTICAL_MIX = 0.05
DRAG_SCALE = 0.01
HIGHEST = lax.Precision.HIGHEST


MESH_ID = pl.DeviceIdType.MESH


HALO_MOVES = ((1, 0), (-1, 0), (0, 1), (0, -1), (1, 1), (1, -1), (-1, 1), (-1, -1))


def enter(n_gy, n_dev, me):
    barrier = pltpu.get_barrier_semaphore()
    for step in range(1, n_dev):
        target = lax.rem(me + step, n_dev)
        pl.semaphore_signal(
            barrier, inc=1, device_id=(target // n_gy, target % n_gy), device_id_type=MESH_ID
        )
    pl.semaphore_wait(barrier, n_dev - 1)


def spread_rows(n_gy, n_dev, me, src_of, slots, send_sem, recv_sem):
    for step in range(1, n_dev):
        target = lax.rem(me + step, n_dev)
        pltpu.make_async_remote_copy(
            src_of(target),
            slots.at[pl.ds(me, 1)],
            send_sem,
            recv_sem,
            device_id=(target // n_gy, target % n_gy),
            device_id_type=MESH_ID,
        ).start()
    first = lax.rem(me + 1, n_dev)
    rest = pl.ds(0, n_dev - 1)
    return pltpu.make_async_remote_copy(
        slots.at[rest],
        slots.at[rest],
        send_sem,
        recv_sem,
        device_id=(first // n_gy, first % n_gy),
        device_id_type=MESH_ID,
    )


def open_kernel(n_gx, n_gy, m, n_block, info_ref, *refs):
    n_dev = n_gx * n_gy
    n_corner = 0
    blocks = refs[:n_block]
    gathered = refs[n_block + n_corner]
    landed = refs[n_block + n_corner + 1 : n_block + n_corner + 1 + len(HALO_MOVES)]
    columns, corners, slots, send_sem, recv_sem, local_sem, halo_send, halo_recv = refs[
        n_block + n_corner + 1 + len(HALO_MOVES) :
    ]
    levels, rows, cols = blocks[0].shape
    for field, block_ref in enumerate(blocks):
        for level in range(levels):
            turned = block_ref[level].T
            depth = field * levels + level
            columns[0, depth] = turned[cols - m :]
            columns[1, depth] = turned[:m]
            for index, (side, window) in enumerate(
                ((cols - m, rows - m), (0, rows - m), (cols - m, 0), (0, 0))
            ):
                corners[index, depth] = turned[side : side + m, window : window + m]
    gx = lax.axis_index("gx")
    gy = lax.axis_index("gy")
    me = gx * n_gy + gy
    enter(n_gy, n_dev, me)
    local = pltpu.make_async_copy(info_ref, slots.at[pl.ds(me, 1)], local_sem)
    local.start()
    parts = lambda window: [
        (block_ref.at[:, window, :], pl.ds(field * levels, levels))
        for field, block_ref in enumerate(blocks)
    ]
    whole = pl.ds(0, n_block * levels)
    sources = (
        parts(pl.ds(rows - m, m)),
        parts(pl.ds(0, m)),
        [(columns.at[0], whole)],
        [(columns.at[1], whole)],
    ) + tuple([(corners.at[index], whole)] for index in range(len(HALO_MOVES) - 4))
    waits = []
    for index, (dx, dy) in enumerate(HALO_MOVES):
        target = (lax.rem(gx + dx + n_gx, n_gx), lax.rem(gy + dy + n_gy, n_gy))
        for source, depth in sources[index]:
            pltpu.make_async_remote_copy(
                source,
                landed[index].at[depth],
                halo_send.at[index],
                halo_recv.at[index],
                device_id=target,
                device_id_type=MESH_ID,
            ).start()
        waits.append(
            pltpu.make_async_remote_copy(
                landed[index],
                landed[index],
                halo_send.at[index],
                halo_recv.at[index],
                device_id=target,
                device_id_type=MESH_ID,
            )
        )
    every = spread_rows(n_gy, n_dev, me, lambda target: info_ref, slots, send_sem, recv_sem)
    local.wait()
    for copy in waits:
        copy.wait_send()
        copy.wait_recv()
    every.wait_send()
    every.wait_recv()
    gathered[...] = slots[...]


def open_exchange(info_row, blocks, m):
    n_gx = lax.axis_size("gx")
    n_gy = lax.axis_size("gy")
    n_dev = n_gx * n_gy
    levels, rows, cols = blocks[0].shape
    depth = levels * len(blocks)
    vmem = pl.BlockSpec(memory_space=pltpu.VMEM)
    piece_shapes = [(depth, m, cols), (depth, m, cols), (depth, m, rows), (depth, m, rows)]
    piece_shapes += [(depth, m, m)] * (len(HALO_MOVES) - 4)
    out_shape = [jax.ShapeDtypeStruct((n_dev, info_row.shape[1]), jnp.float32)] + [
        jax.ShapeDtypeStruct(shape, jnp.float32) for shape in piece_shapes
    ]
    return pl.pallas_call(
        functools.partial(open_kernel, n_gx, n_gy, m, len(blocks)),
        out_shape=out_shape,
        in_specs=[vmem] * (1 + len(blocks)),
        out_specs=[vmem] * len(out_shape),
        scratch_shapes=[
            pltpu.VMEM((2, depth, m, rows), jnp.float32),
            pltpu.VMEM((len(HALO_MOVES) - 4, depth, m, m), jnp.float32),
            pltpu.VMEM((n_dev, info_row.shape[1]), jnp.float32),
            pltpu.SemaphoreType.DMA,
            pltpu.SemaphoreType.DMA,
            pltpu.SemaphoreType.DMA,
            pltpu.SemaphoreType.DMA((len(piece_shapes),)),
            pltpu.SemaphoreType.DMA((len(piece_shapes),)),
        ],
        compiler_params=pltpu.CompilerParams(has_side_effects=True, collective_id=0),
    )(info_row, *blocks)


def close_kernel(n_gy, n_dev, src_ref, out_ref, slots, send_sem, recv_sem, local_sem):
    gx = lax.axis_index("gx")
    gy = lax.axis_index("gy")
    me = gx * n_gy + gy
    enter(n_gy, n_dev, me)
    local = pltpu.make_async_copy(src_ref.at[pl.ds(me, 1)], slots.at[pl.ds(me, 1)], local_sem)
    local.start()
    every = spread_rows(
        n_gy, n_dev, me, lambda target: src_ref.at[pl.ds(target, 1)], slots, send_sem, recv_sem
    )
    local.wait()
    every.wait_send()
    every.wait_recv()
    out_ref[...] = jnp.sum(slots[...], axis=0, keepdims=True)


def close_scatter(rows):
    n_gy = lax.axis_size("gy")
    n_dev = lax.axis_size("gx") * n_gy
    vmem = pl.BlockSpec(memory_space=pltpu.VMEM)
    return pl.pallas_call(
        functools.partial(close_kernel, n_gy, n_dev),
        out_shape=jax.ShapeDtypeStruct((1, rows.shape[1]), jnp.float32),
        in_specs=[vmem],
        out_specs=vmem,
        scratch_shapes=[
            pltpu.VMEM(rows.shape, jnp.float32),
            pltpu.SemaphoreType.DMA,
            pltpu.SemaphoreType.DMA,
            pltpu.SemaphoreType.DMA,
        ],
        compiler_params=pltpu.CompilerParams(has_side_effects=True, collective_id=1),
    )(rows)


def column_band(landed, m, size_r, size_c, cols):
    row_low, row_high, col_low, col_high, c_ll, c_lh, c_hl, c_hh = landed
    depth = col_low.shape[0]
    width = size_c - cols
    span = -(-size_r // 128) * 128

    def edge(column, high_corner, low_corner):
        fill = jnp.zeros((depth, m, span - size_r), jnp.float32)
        return jnp.concatenate(
            [column, high_corner, low_corner, fill],
            axis=2,
        )

    fill = jnp.zeros((depth, width - 2 * m, span), jnp.float32)
    return jnp.concatenate([edge(col_high, c_hh, c_lh), fill, edge(col_low, c_hl, c_ll)], axis=1)


def stencil_kernel(n_gx, n_gy, levels, steps, n_block, *refs):
    blocks = refs[:n_block]
    (
        high_ref, low_ref, band_ref, drag_ref, row_ref, col_ref, thrust_ref, gain_ref,
        lam_out, grad_out,
        ext_ref, states, lams, sens_all, sending, slots, send_sem, recv_sem, local_sem,
    ) = refs[n_block:]
    n_dev = n_gx * n_gy
    me = lax.axis_index("gx") * n_gy + lax.axis_index("gy")
    barrier = pltpu.get_barrier_semaphore()
    for step in range(1, n_dev):
        target = lax.rem(me + step, n_dev)
        pl.semaphore_signal(
            barrier, inc=1, device_id=(target // n_gy, target % n_gy), device_id_type=MESH_ID
        )
    size_r, size_c = ext_ref.shape[1:]
    rows, cols = blocks[0].shape[1:]
    m = high_ref.shape[1]
    for depth in range(ext_ref.shape[0]):
        ext_ref[depth, :rows, :cols] = blocks[depth // levels][depth % levels]
        ext_ref[depth, rows : rows + m, :cols] = high_ref[depth]
        ext_ref[depth, size_r - m :, :cols] = low_ref[depth]
        ext_ref[depth, :, cols:] = band_ref[depth].T[:size_r]

    def west(x):
        return pltpu.roll(x, 1, 0)

    def east(x):
        return pltpu.roll(x, size_r - 1, 0)

    def south(x):
        return pltpu.roll(x, 1, 1)

    def north(x):
        return pltpu.roll(x, size_c - 1, 1)

    def vertical(plane, level, center):
        mix = None
        if level + 1 < levels:
            mix = plane(level + 1) - center
        if level > 0:
            below = plane(level - 1) - center
            mix = below if mix is None else mix + below
        return mix

    for level in range(levels):
        states[0, level] = ext_ref[level]

    def forward(n, carry):
        for level in range(levels):
            center = states[n, level]
            upwind = west(center)
            advect = ext_ref[levels + level]
            diffuse = ext_ref[2 * levels + level]
            states[n + 1, level] = (
                center
                + advect * (upwind - center)
                + diffuse * (east(center) + upwind + north(center) + south(center) - 4.0 * center)
                + VERTICAL_MIX * vertical(lambda l: states[n, l], level, center)
                - drag_ref[level] * (center * jnp.sqrt(center * center + 1.0))
            )
        return carry

    lax.fori_loop(0, steps - 1, forward, 0)
    for level in range(levels):
        lams[0, level] = ext_ref[3 * levels + level]
        sens_all[level] = jnp.zeros(sens_all.shape[1:], jnp.float32)

    def backward(i, carry):
        n = steps - 1 - i
        now = i % 2
        for level in range(levels):
            adjoint = lams[now, level]
            state = states[n, level]
            sens_all[level] = sens_all[level] - adjoint * (state * jnp.sqrt(state * state + 1.0))
            flux_adv = ext_ref[levels + level] * adjoint
            flux_dif = ext_ref[2 * levels + level] * adjoint
            square_one = state * state + 1.0
            slope = (square_one + state * state) / jnp.sqrt(square_one)
            lams[1 - now, level] = (
                adjoint
                - flux_adv
                - 4.0 * flux_dif
                + east(flux_adv)
                + (east(flux_dif) + west(flux_dif) + north(flux_dif) + south(flux_dif))
                + VERTICAL_MIX * vertical(lambda l: lams[now, l], level, adjoint)
                - drag_ref[level] * slope * adjoint
            )
        return carry

    lax.fori_loop(0, steps, backward, 0)
    weighted = gain_ref[0] * sens_all[0, :rows, :cols]
    for level in range(1, levels):
        weighted = weighted + gain_ref[level] * sens_all[level, :rows, :cols]
    sending[...] = jnp.zeros(sending.shape, jnp.float32)
    for slot in range(row_ref.shape[0]):
        across = jnp.dot(
            weighted, col_ref[slot], precision=HIGHEST, preferred_element_type=jnp.float32
        )
        totals = jnp.sum(row_ref[slot] * across, axis=0, keepdims=True)
        sending[slot : slot + 1, :] = thrust_ref[slot] * totals
    sending[...] = sending[...].T
    pl.semaphore_wait(barrier, n_dev - 1)
    local = pltpu.make_async_copy(sending.at[pl.ds(me, 1)], slots.at[pl.ds(me, 1)], local_sem)
    local.start()
    every = spread_rows(
        n_gy, n_dev, me, lambda target: sending.at[pl.ds(target, 1)], slots, send_sem, recv_sem
    )
    local.wait()
    every.wait_send()
    every.wait_recv()
    grad_out[...] = jnp.sum(slots[...], axis=0, keepdims=True)
    for level in range(levels):
        lam_out[level] = lams[steps % 2, level, :rows, :cols]


def stencil(blocks, landed, band, drag, levels, row_prof, col_prof, thrust_rows, gain_rows):
    size_r, size_c = drag.shape[1:]
    depth = levels * len(blocks)
    vmem = pl.BlockSpec(memory_space=pltpu.VMEM)
    plane = jax.ShapeDtypeStruct(blocks[0].shape, jnp.float32)
    n_gx = lax.axis_size("gx")
    n_gy = lax.axis_size("gy")
    n_dev = n_gx * n_gy
    width = row_prof.shape[2]
    cells = levels * size_r * size_c
    return pl.pallas_call(
        functools.partial(stencil_kernel, n_gx, n_gy, levels, STEPS, len(blocks)),
        out_shape=[plane, jax.ShapeDtypeStruct((1, width), jnp.float32)],
        in_specs=[vmem] * (len(blocks) + 8),
        out_specs=[vmem, vmem],
        scratch_shapes=[
            pltpu.VMEM((depth, size_r, size_c), jnp.float32),
            pltpu.VMEM((STEPS, levels, size_r, size_c), jnp.float32),
            pltpu.VMEM((2, levels, size_r, size_c), jnp.float32),
            pltpu.VMEM((levels, size_r, size_c), jnp.float32),
            pltpu.VMEM((width, width), jnp.float32),
            pltpu.VMEM((n_dev, width), jnp.float32),
            pltpu.SemaphoreType.DMA,
            pltpu.SemaphoreType.DMA,
            pltpu.SemaphoreType.DMA,
        ],
        compiler_params=pltpu.CompilerParams(
            vmem_limit_bytes=48 * 1024 * 1024, has_side_effects=True, collective_id=1
        ),
        cost_estimate=pl.CostEstimate(
            flops=60 * STEPS * cells, transcendentals=3 * STEPS * cells, bytes_accessed=28 * cells
        ),
    )(*blocks, landed[1], landed[0], band, drag, row_prof, col_prof, thrust_rows, gain_rows)


def drag_law(state):
    return state * jnp.sqrt(state * state + 1.0)


def drag_slope(state):
    square_one = state * state + 1.0
    return (square_one + state * state) / jnp.sqrt(square_one)


def vertical(center):
    zero_row = jnp.zeros_like(center[:1])
    from_above = jnp.concatenate([center[1:] - center[:-1], zero_row], axis=0)
    from_below = jnp.concatenate([zero_row, center[:-1] - center[1:]], axis=0)
    return from_above + from_below


def advance(padded, advect, diffuse, drag_coef):
    center = padded[:, 1:-1, 1:-1]
    upwind = padded[:, :-2, 1:-1]
    downwind = padded[:, 2:, 1:-1]
    left_cell = padded[:, 1:-1, :-2]
    right_cell = padded[:, 1:-1, 2:]
    return (
        center
        + advect * (upwind - center)
        + diffuse * (downwind + upwind + right_cell + left_cell - 4.0 * center)
        + VERTICAL_MIX * vertical(center)
        - drag_coef * drag_law(center)
    )


def retreat(padded, advect_ext, diffuse_ext, drag_coef, state):
    flux_adv = advect_ext * padded
    flux_dif = diffuse_ext * padded
    center = padded[:, 1:-1, 1:-1]
    return (
        center
        - flux_adv[:, 1:-1, 1:-1]
        - 4.0 * flux_dif[:, 1:-1, 1:-1]
        + flux_adv[:, 2:, 1:-1]
        + (
            flux_dif[:, 2:, 1:-1]
            + flux_dif[:, :-2, 1:-1]
            + flux_dif[:, 1:-1, 2:]
            + flux_dif[:, 1:-1, :-2]
        )
        + VERTICAL_MIX * vertical(center)
        - drag_coef * drag_slope(state) * center
    )


def trim(array, margin, wanted):
    excess = margin - wanted
    if excess == 0:
        return array
    return array[:, excess:-excess, excess:-excess]


def profiles(first, starts, widths, period, length, inner):
    cells = jnp.arange(length, dtype=jnp.int32)
    cells = jnp.where(cells < inner, cells, cells - length)
    pos = (first + cells - starts[..., None]) % period
    cell_pos = pos.astype(jnp.float32) - (FP - 1) / 2.0
    profile = jnp.exp(-(cell_pos * cell_pos) / (2.0 * widths[..., None] * widths[..., None]))
    return jnp.where(pos < FP, profile, 0.0)


def level_gain():
    level_pos = jnp.arange(LEV, dtype=jnp.float32) - (LEV - 1) / 2.0
    return DRAG_SCALE * jnp.exp(-0.5 * level_pos * level_pos)


def shards(
    velocity, adjoint_seed, courant, viscosity, turbine_tile, turbine_offset, thrust, disk_width
):
    levels, rows, cols = velocity.shape
    n_gx = lax.axis_size("gx")
    n_gy = lax.axis_size("gy")
    m = MARGIN
    per = thrust.shape[0]
    fields = (
        turbine_tile[:, 0].astype(jnp.float32),
        turbine_offset[:, 0].astype(jnp.float32),
        turbine_offset[:, 1].astype(jnp.float32),
        thrust,
        disk_width,
    )
    info_row = jnp.pad(jnp.concatenate(fields)[None, :], ((0, 0), (0, 128 - len(fields) * per)))
    blocks = (velocity, courant, viscosity, adjoint_seed)
    opened = open_exchange(info_row, blocks, m)
    info = opened[0]
    tiles = info[:, 0:per].astype(jnp.int32)
    row_start = tiles // n_gy * rows + info[:, per : 2 * per].astype(jnp.int32)
    col_start = tiles % n_gy * cols + info[:, 2 * per : 3 * per].astype(jnp.int32)
    thrusts = info[:, 3 * per : 4 * per]
    widths = info[:, 4 * per : 5 * per]
    gx = lax.axis_index("gx")
    gy = lax.axis_index("gy")
    size_r = -(-(rows + 2 * m) // 8) * 8
    size_c = -(-(cols + 2 * m) // 128) * 128
    inner_r = rows + (size_r - rows) // 2
    inner_c = cols + (size_c - cols) // 2
    prof_r = profiles(gx * rows, row_start, widths, n_gx * rows, size_r, inner_r)
    prof_c = profiles(gy * cols, col_start, widths, n_gy * cols, size_c, inner_c)
    gain = level_gain()
    plane = jnp.einsum("dkr,dkc->rc", thrusts[..., None] * prof_r, prof_c, precision=HIGHEST)
    drag = gain[:, None, None] * plane[None]
    band = column_band(opened[1:], m, size_r, size_c, cols)
    spare = ((0, 0), (0, 0), (0, -(-n_gx * n_gy // 128) * 128 - n_gx * n_gy))
    row_prof = jnp.pad(jnp.transpose(prof_r[..., :rows], (1, 2, 0)), spare)
    col_prof = jnp.pad(jnp.transpose(prof_c[..., :cols], (1, 2, 0)), spare)
    thrust_rows = jnp.pad(jnp.transpose(thrusts)[:, None, :], spare)
    gain_rows = jnp.broadcast_to(gain[:, None, None], (levels, 1, cols))
    adjoint, grad = stencil(
        blocks, opened[1:], band, drag, levels, row_prof, col_prof, thrust_rows, gain_rows
    )
    return adjoint, grad[0, :per]


def solution(mesh):
    placed = (
        P(None, "gx", "gy"),
        P(None, "gx", "gy"),
        P(None, "gx", "gy"),
        P(None, "gx", "gy"),
        P(("gx", "gy"), None),
        P(("gx", "gy"), None),
        P(("gx", "gy")),
        P(("gx", "gy")),
    )
    return jax.shard_map(
        shards,
        mesh=mesh,
        in_specs=placed,
        out_specs=(P(None, "gx", "gy"), P(("gx", "gy"))),
        check_vma=False,
    )
```

```python
import functools

import jax
import jax.numpy as jnp
from jax import lax
from jax.experimental import pallas as pl
from jax.experimental.pallas import tpu as pltpu
from jax.sharding import PartitionSpec as P

LEV = 3
STEPS = 8
FP = 64
MARGIN = 2 * STEPS

VERTICAL_MIX = 0.05
DRAG_SCALE = 0.01
HIGHEST = lax.Precision.HIGHEST


MESH_ID = pl.DeviceIdType.MESH


HALO_MOVES = ((1, 0), (-1, 0), (0, 1), (0, -1), (1, 1), (1, -1), (-1, 1), (-1, -1))


def greet(n_gy, n_dev, me):
    barrier = pltpu.get_barrier_semaphore()
    for step in range(1, n_dev):
        target = lax.rem(me + step, n_dev)
        pl.semaphore_signal(
            barrier, inc=1, device_id=(target // n_gy, target % n_gy), device_id_type=MESH_ID
        )
    return barrier


def spread_rows(n_gy, n_dev, me, src_of, slots, send_sem, recv_sem):
    for step in range(1, n_dev):
        target = lax.rem(me + step, n_dev)
        pltpu.make_async_remote_copy(
            src_of(target),
            slots.at[pl.ds(me, 1)],
            send_sem,
            recv_sem,
            device_id=(target // n_gy, target % n_gy),
            device_id_type=MESH_ID,
        ).start()
    first = lax.rem(me + 1, n_dev)
    rest = pl.ds(0, n_dev - 1)
    return pltpu.make_async_remote_copy(
        slots.at[rest],
        slots.at[rest],
        send_sem,
        recv_sem,
        device_id=(first // n_gy, first % n_gy),
        device_id_type=MESH_ID,
    )


def open_kernel(n_gx, n_gy, m, n_block, info_ref, *refs):
    n_dev = n_gx * n_gy
    n_corner = 0
    blocks = refs[:n_block]
    gathered = refs[n_block + n_corner]
    landed = refs[n_block + n_corner + 1 : n_block + n_corner + 1 + len(HALO_MOVES)]
    columns, corners, slots, send_sem, recv_sem, local_sem, halo_send, halo_recv = refs[
        n_block + n_corner + 1 + len(HALO_MOVES) :
    ]
    levels, rows, cols = blocks[0].shape
    gx = lax.axis_index("gx")
    gy = lax.axis_index("gy")
    me = gx * n_gy + gy
    barrier = greet(n_gy, n_dev, me)
    for field, block_ref in enumerate(blocks):
        for level in range(levels):
            turned = block_ref[level].T
            depth = field * levels + level
            columns[0, depth] = turned[cols - m :]
            columns[1, depth] = turned[:m]
            for index, (side, window) in enumerate(
                ((cols - m, rows - m), (0, rows - m), (cols - m, 0), (0, 0))
            ):
                corners[index, depth] = turned[side : side + m, window : window + m]
    pl.semaphore_wait(barrier, n_dev - 1)
    local = pltpu.make_async_copy(info_ref, slots.at[pl.ds(me, 1)], local_sem)
    local.start()
    parts = lambda window: [
        (block_ref.at[:, window, :], pl.ds(field * levels, levels))
        for field, block_ref in enumerate(blocks)
    ]
    whole = pl.ds(0, n_block * levels)
    sources = (
        parts(pl.ds(rows - m, m)),
        parts(pl.ds(0, m)),
        [(columns.at[0], whole)],
        [(columns.at[1], whole)],
    ) + tuple([(corners.at[index], whole)] for index in range(len(HALO_MOVES) - 4))
    waits = []
    for index, (dx, dy) in enumerate(HALO_MOVES):
        target = (lax.rem(gx + dx + n_gx, n_gx), lax.rem(gy + dy + n_gy, n_gy))
        for source, depth in sources[index]:
            pltpu.make_async_remote_copy(
                source,
                landed[index].at[depth],
                halo_send.at[index],
                halo_recv.at[index],
                device_id=target,
                device_id_type=MESH_ID,
            ).start()
        waits.append(
            pltpu.make_async_remote_copy(
                landed[index],
                landed[index],
                halo_send.at[index],
                halo_recv.at[index],
                device_id=target,
                device_id_type=MESH_ID,
            )
        )
    every = spread_rows(n_gy, n_dev, me, lambda target: info_ref, slots, send_sem, recv_sem)
    local.wait()
    for copy in waits:
        copy.wait_send()
        copy.wait_recv()
    every.wait_send()
    every.wait_recv()
    gathered[...] = slots[...]


def open_exchange(info_row, blocks, m):
    n_gx = lax.axis_size("gx")
    n_gy = lax.axis_size("gy")
    n_dev = n_gx * n_gy
    levels, rows, cols = blocks[0].shape
    depth = levels * len(blocks)
    vmem = pl.BlockSpec(memory_space=pltpu.VMEM)
    piece_shapes = [(depth, m, cols), (depth, m, cols), (depth, m, rows), (depth, m, rows)]
    piece_shapes += [(depth, m, m)] * (len(HALO_MOVES) - 4)
    out_shape = [jax.ShapeDtypeStruct((n_dev, info_row.shape[1]), jnp.float32)] + [
        jax.ShapeDtypeStruct(shape, jnp.float32) for shape in piece_shapes
    ]
    return pl.pallas_call(
        functools.partial(open_kernel, n_gx, n_gy, m, len(blocks)),
        out_shape=out_shape,
        in_specs=[vmem] * (1 + len(blocks)),
        out_specs=[vmem] * len(out_shape),
        scratch_shapes=[
            pltpu.VMEM((2, depth, m, rows), jnp.float32),
            pltpu.VMEM((len(HALO_MOVES) - 4, depth, m, m), jnp.float32),
            pltpu.VMEM((n_dev, info_row.shape[1]), jnp.float32),
            pltpu.SemaphoreType.DMA,
            pltpu.SemaphoreType.DMA,
            pltpu.SemaphoreType.DMA,
            pltpu.SemaphoreType.DMA((len(piece_shapes),)),
            pltpu.SemaphoreType.DMA((len(piece_shapes),)),
        ],
        compiler_params=pltpu.CompilerParams(has_side_effects=True, collective_id=0),
    )(info_row, *blocks)


def column_band(landed, m, size_r, size_c, cols):
    row_low, row_high, col_low, col_high, c_ll, c_lh, c_hl, c_hh = landed
    depth = col_low.shape[0]
    width = size_c - cols
    span = -(-size_r // 128) * 128

    def edge(column, high_corner, low_corner):
        fill = jnp.zeros((depth, m, span - size_r), jnp.float32)
        return jnp.concatenate(
            [column, high_corner, low_corner, fill],
            axis=2,
        )

    fill = jnp.zeros((depth, width - 2 * m, span), jnp.float32)
    return jnp.concatenate([edge(col_high, c_hh, c_lh), fill, edge(col_low, c_hl, c_ll)], axis=1)


def stencil_kernel(n_gx, n_gy, levels, steps, n_block, *refs):
    blocks = refs[:n_block]
    (
        high_ref, low_ref, band_ref, drag_ref, row_ref, col_ref, thrust_ref, gain_ref,
        lam_out, grad_out,
        ext_ref, states, lams, sens_all, sending, slots, send_sem, recv_sem, local_sem,
    ) = refs[n_block:]
    n_dev = n_gx * n_gy
    me = lax.axis_index("gx") * n_gy + lax.axis_index("gy")
    barrier = greet(n_gy, n_dev, me)
    size_r, size_c = ext_ref.shape[1:]
    rows, cols = blocks[0].shape[1:]
    m = high_ref.shape[1]
    for depth in range(ext_ref.shape[0]):
        ext_ref[depth, :rows, :cols] = blocks[depth // levels][depth % levels]
        ext_ref[depth, rows : rows + m, :cols] = high_ref[depth]
        ext_ref[depth, size_r - m :, :cols] = low_ref[depth]
        ext_ref[depth, :, cols:] = band_ref[depth].T[:size_r]

    def west(x):
        return pltpu.roll(x, 1, 0)

    def east(x):
        return pltpu.roll(x, size_r - 1, 0)

    def south(x):
        return pltpu.roll(x, 1, 1)

    def north(x):
        return pltpu.roll(x, size_c - 1, 1)

    def vertical(plane, level, center):
        mix = None
        if level + 1 < levels:
            mix = plane(level + 1) - center
        if level > 0:
            below = plane(level - 1) - center
            mix = below if mix is None else mix + below
        return mix

    for level in range(levels):
        states[0, level] = ext_ref[level]

    def forward(n, carry):
        for level in range(levels):
            center = states[n, level]
            upwind = west(center)
            advect = ext_ref[levels + level]
            diffuse = ext_ref[2 * levels + level]
            states[n + 1, level] = (
                center
                + advect * (upwind - center)
                + diffuse * (east(center) + upwind + north(center) + south(center) - 4.0 * center)
                + VERTICAL_MIX * vertical(lambda l: states[n, l], level, center)
                - drag_ref[level] * (center * jnp.sqrt(center * center + 1.0))
            )
        return carry

    lax.fori_loop(0, steps - 1, forward, 0)
    for level in range(levels):
        lams[0, level] = ext_ref[3 * levels + level]
        sens_all[level] = jnp.zeros(sens_all.shape[1:], jnp.float32)

    def backward(i, carry):
        n = steps - 1 - i
        now = i % 2
        for level in range(levels):
            adjoint = lams[now, level]
            state = states[n, level]
            sens_all[level] = sens_all[level] - adjoint * (state * jnp.sqrt(state * state + 1.0))
            flux_adv = ext_ref[levels + level] * adjoint
            flux_dif = ext_ref[2 * levels + level] * adjoint
            square_one = state * state + 1.0
            slope = (square_one + state * state) / jnp.sqrt(square_one)
            lams[1 - now, level] = (
                adjoint
                - flux_adv
                - 4.0 * flux_dif
                + east(flux_adv)
                + (east(flux_dif) + west(flux_dif) + north(flux_dif) + south(flux_dif))
                + VERTICAL_MIX * vertical(lambda l: lams[now, l], level, adjoint)
                - drag_ref[level] * slope * adjoint
            )
        return carry

    lax.fori_loop(0, steps, backward, 0)
    weighted = gain_ref[0] * sens_all[0, :rows, :cols]
    for level in range(1, levels):
        weighted = weighted + gain_ref[level] * sens_all[level, :rows, :cols]
    sending[...] = jnp.zeros(sending.shape, jnp.float32)
    for slot in range(row_ref.shape[0]):
        across = jnp.dot(
            weighted, col_ref[slot], precision=HIGHEST, preferred_element_type=jnp.float32
        )
        totals = jnp.sum(row_ref[slot] * across, axis=0, keepdims=True)
        sending[slot : slot + 1, :] = thrust_ref[slot] * totals
    sending[...] = sending[...].T
    pl.semaphore_wait(barrier, n_dev - 1)
    local = pltpu.make_async_copy(sending.at[pl.ds(me, 1)], slots.at[pl.ds(me, 1)], local_sem)
    local.start()
    every = spread_rows(
        n_gy, n_dev, me, lambda target: sending.at[pl.ds(target, 1)], slots, send_sem, recv_sem
    )
    local.wait()
    every.wait_send()
    every.wait_recv()
    grad_out[...] = jnp.sum(slots[...], axis=0, keepdims=True)
    for level in range(levels):
        lam_out[level] = lams[steps % 2, level, :rows, :cols]


def stencil(blocks, landed, band, drag, levels, row_prof, col_prof, thrust_rows, gain_rows):
    size_r, size_c = drag.shape[1:]
    depth = levels * len(blocks)
    vmem = pl.BlockSpec(memory_space=pltpu.VMEM)
    plane = jax.ShapeDtypeStruct(blocks[0].shape, jnp.float32)
    n_gx = lax.axis_size("gx")
    n_gy = lax.axis_size("gy")
    n_dev = n_gx * n_gy
    width = row_prof.shape[2]
    cells = levels * size_r * size_c
    return pl.pallas_call(
        functools.partial(stencil_kernel, n_gx, n_gy, levels, STEPS, len(blocks)),
        out_shape=[plane, jax.ShapeDtypeStruct((1, width), jnp.float32)],
        in_specs=[vmem] * (len(blocks) + 8),
        out_specs=[vmem, vmem],
        scratch_shapes=[
            pltpu.VMEM((depth, size_r, size_c), jnp.float32),
            pltpu.VMEM((STEPS, levels, size_r, size_c), jnp.float32),
            pltpu.VMEM((2, levels, size_r, size_c), jnp.float32),
            pltpu.VMEM((levels, size_r, size_c), jnp.float32),
            pltpu.VMEM((width, width), jnp.float32),
            pltpu.VMEM((n_dev, width), jnp.float32),
            pltpu.SemaphoreType.DMA,
            pltpu.SemaphoreType.DMA,
            pltpu.SemaphoreType.DMA,
        ],
        compiler_params=pltpu.CompilerParams(
            vmem_limit_bytes=48 * 1024 * 1024, has_side_effects=True, collective_id=1
        ),
        cost_estimate=pl.CostEstimate(
            flops=60 * STEPS * cells, transcendentals=3 * STEPS * cells, bytes_accessed=28 * cells
        ),
    )(*blocks, landed[1], landed[0], band, drag, row_prof, col_prof, thrust_rows, gain_rows)


def drag_law(state):
    return state * jnp.sqrt(state * state + 1.0)


def drag_slope(state):
    square_one = state * state + 1.0
    return (square_one + state * state) / jnp.sqrt(square_one)


def vertical(center):
    zero_row = jnp.zeros_like(center[:1])
    from_above = jnp.concatenate([center[1:] - center[:-1], zero_row], axis=0)
    from_below = jnp.concatenate([zero_row, center[:-1] - center[1:]], axis=0)
    return from_above + from_below


def advance(padded, advect, diffuse, drag_coef):
    center = padded[:, 1:-1, 1:-1]
    upwind = padded[:, :-2, 1:-1]
    downwind = padded[:, 2:, 1:-1]
    left_cell = padded[:, 1:-1, :-2]
    right_cell = padded[:, 1:-1, 2:]
    return (
        center
        + advect * (upwind - center)
        + diffuse * (downwind + upwind + right_cell + left_cell - 4.0 * center)
        + VERTICAL_MIX * vertical(center)
        - drag_coef * drag_law(center)
    )


def retreat(padded, advect_ext, diffuse_ext, drag_coef, state):
    flux_adv = advect_ext * padded
    flux_dif = diffuse_ext * padded
    center = padded[:, 1:-1, 1:-1]
    return (
        center
        - flux_adv[:, 1:-1, 1:-1]
        - 4.0 * flux_dif[:, 1:-1, 1:-1]
        + flux_adv[:, 2:, 1:-1]
        + (
            flux_dif[:, 2:, 1:-1]
            + flux_dif[:, :-2, 1:-1]
            + flux_dif[:, 1:-1, 2:]
            + flux_dif[:, 1:-1, :-2]
        )
        + VERTICAL_MIX * vertical(center)
        - drag_coef * drag_slope(state) * center
    )


def trim(array, margin, wanted):
    excess = margin - wanted
    if excess == 0:
        return array
    return array[:, excess:-excess, excess:-excess]


def profiles(first, starts, widths, period, length, inner):
    cells = jnp.arange(length, dtype=jnp.int32)
    cells = jnp.where(cells < inner, cells, cells - length)
    pos = (first + cells - starts[..., None]) % period
    cell_pos = pos.astype(jnp.float32) - (FP - 1) / 2.0
    profile = jnp.exp(-(cell_pos * cell_pos) / (2.0 * widths[..., None] * widths[..., None]))
    return jnp.where(pos < FP, profile, 0.0)


def level_gain():
    level_pos = jnp.arange(LEV, dtype=jnp.float32) - (LEV - 1) / 2.0
    return DRAG_SCALE * jnp.exp(-0.5 * level_pos * level_pos)


def shards(
    velocity, adjoint_seed, courant, viscosity, turbine_tile, turbine_offset, thrust, disk_width
):
    levels, rows, cols = velocity.shape
    n_gx = lax.axis_size("gx")
    n_gy = lax.axis_size("gy")
    m = MARGIN
    per = thrust.shape[0]
    fields = (
        turbine_tile[:, 0].astype(jnp.float32),
        turbine_offset[:, 0].astype(jnp.float32),
        turbine_offset[:, 1].astype(jnp.float32),
        thrust,
        disk_width,
    )
    spare = jnp.zeros((128 - len(fields) * per,), jnp.float32)
    info_row = jnp.concatenate(fields + (spare,))[None, :]
    blocks = (velocity, courant, viscosity, adjoint_seed)
    opened = open_exchange(info_row, blocks, m)
    info = opened[0]
    tiles = info[:, 0:per].astype(jnp.int32)
    row_start = tiles // n_gy * rows + info[:, per : 2 * per].astype(jnp.int32)
    col_start = tiles % n_gy * cols + info[:, 2 * per : 3 * per].astype(jnp.int32)
    thrusts = info[:, 3 * per : 4 * per]
    widths = info[:, 4 * per : 5 * per]
    gx = lax.axis_index("gx")
    gy = lax.axis_index("gy")
    size_r = -(-(rows + 2 * m) // 8) * 8
    size_c = -(-(cols + 2 * m) // 128) * 128
    inner_r = rows + (size_r - rows) // 2
    inner_c = cols + (size_c - cols) // 2
    prof_r = profiles(gx * rows, row_start, widths, n_gx * rows, size_r, inner_r)
    prof_c = profiles(gy * cols, col_start, widths, n_gy * cols, size_c, inner_c)
    gain = level_gain()
    plane = jnp.einsum("dkr,dkc->rc", thrusts[..., None] * prof_r, prof_c, precision=HIGHEST)
    drag = gain[:, None, None] * plane[None]
    band = column_band(opened[1:], m, size_r, size_c, cols)
    spare = ((0, 0), (0, 0), (0, -(-n_gx * n_gy // 128) * 128 - n_gx * n_gy))
    row_prof = jnp.pad(jnp.transpose(prof_r[..., :rows], (1, 2, 0)), spare)
    col_prof = jnp.pad(jnp.transpose(prof_c[..., :cols], (1, 2, 0)), spare)
    thrust_rows = jnp.pad(jnp.transpose(thrusts)[:, None, :], spare)
    gain_rows = jnp.broadcast_to(gain[:, None, None], (levels, 1, cols))
    adjoint, grad = stencil(
        blocks, opened[1:], band, drag, levels, row_prof, col_prof, thrust_rows, gain_rows
    )
    return adjoint, grad[0, :per]


def solution(mesh):
    placed = (
        P(None, "gx", "gy"),
        P(None, "gx", "gy"),
        P(None, "gx", "gy"),
        P(None, "gx", "gy"),
        P(("gx", "gy"), None),
        P(("gx", "gy"), None),
        P(("gx", "gy")),
        P(("gx", "gy")),
    )
    return jax.shard_map(
        shards,
        mesh=mesh,
        in_specs=placed,
        out_specs=(P(None, "gx", "gy"), P(("gx", "gy"))),
        check_vma=False,
    )
```

```python
import functools

import jax
import jax.numpy as jnp
from jax import lax
from jax.experimental import pallas as pl
from jax.experimental.pallas import tpu as pltpu
from jax.sharding import PartitionSpec as P

LEV = 3
STEPS = 8
FP = 64
MARGIN = 2 * STEPS

VERTICAL_MIX = 0.05
DRAG_SCALE = 0.01
HIGHEST = lax.Precision.HIGHEST


MESH_ID = pl.DeviceIdType.MESH


HALO_MOVES = ((1, 0), (-1, 0), (0, 1), (0, -1), (1, 1), (1, -1), (-1, 1), (-1, -1))


def greet(n_gy, n_dev, me):
    barrier = pltpu.get_barrier_semaphore()
    for step in range(1, n_dev):
        target = lax.rem(me + step, n_dev)
        pl.semaphore_signal(
            barrier, inc=1, device_id=(target // n_gy, target % n_gy), device_id_type=MESH_ID
        )
    return barrier


def spread_rows(n_gy, n_dev, me, src_of, slots, send_sem, recv_sem):
    for step in range(1, n_dev):
        target = lax.rem(me + step, n_dev)
        pltpu.make_async_remote_copy(
            src_of(target),
            slots.at[pl.ds(me, 1)],
            send_sem,
            recv_sem,
            device_id=(target // n_gy, target % n_gy),
            device_id_type=MESH_ID,
        ).start()
    first = lax.rem(me + 1, n_dev)
    rest = pl.ds(0, n_dev - 1)
    return pltpu.make_async_remote_copy(
        slots.at[rest],
        slots.at[rest],
        send_sem,
        recv_sem,
        device_id=(first // n_gy, first % n_gy),
        device_id_type=MESH_ID,
    )


def open_kernel(n_gx, n_gy, m, n_block, info_ref, *refs):
    n_dev = n_gx * n_gy
    n_corner = 0
    blocks = refs[:n_block]
    gathered = refs[n_block + n_corner]
    landed = refs[n_block + n_corner + 1 : n_block + n_corner + 1 + len(HALO_MOVES)]
    columns, corners, slots, send_sem, recv_sem, local_sem, halo_send, halo_recv = refs[
        n_block + n_corner + 1 + len(HALO_MOVES) :
    ]
    levels, rows, cols = blocks[0].shape
    gx = lax.axis_index("gx")
    gy = lax.axis_index("gy")
    me = gx * n_gy + gy
    barrier = greet(n_gy, n_dev, me)
    for field, block_ref in enumerate(blocks):
        for level in range(levels):
            turned = block_ref[level].T
            depth = field * levels + level
            columns[0, depth] = turned[cols - m :]
            columns[1, depth] = turned[:m]
            for index, (side, window) in enumerate(
                ((cols - m, rows - m), (0, rows - m), (cols - m, 0), (0, 0))
            ):
                corners[index, depth] = turned[side : side + m, window : window + m]
    pl.semaphore_wait(barrier, n_dev - 1)
    local = pltpu.make_async_copy(info_ref, slots.at[pl.ds(me, 1)], local_sem)
    local.start()
    parts = lambda window: [
        (block_ref.at[:, window, :], pl.ds(field * levels, levels))
        for field, block_ref in enumerate(blocks)
    ]
    whole = pl.ds(0, n_block * levels)
    sources = (
        parts(pl.ds(rows - m, m)),
        parts(pl.ds(0, m)),
        [(columns.at[0], whole)],
        [(columns.at[1], whole)],
    ) + tuple([(corners.at[index], whole)] for index in range(len(HALO_MOVES) - 4))
    waits = []
    for index, (dx, dy) in enumerate(HALO_MOVES):
        target = (lax.rem(gx + dx + n_gx, n_gx), lax.rem(gy + dy + n_gy, n_gy))
        for source, depth in sources[index]:
            pltpu.make_async_remote_copy(
                source,
                landed[index].at[depth],
                halo_send.at[index],
                halo_recv.at[index],
                device_id=target,
                device_id_type=MESH_ID,
            ).start()
        waits.append(
            pltpu.make_async_remote_copy(
                landed[index],
                landed[index],
                halo_send.at[index],
                halo_recv.at[index],
                device_id=target,
                device_id_type=MESH_ID,
            )
        )
    every = spread_rows(n_gy, n_dev, me, lambda target: info_ref, slots, send_sem, recv_sem)
    local.wait()
    for copy in waits:
        copy.wait_send()
        copy.wait_recv()
    every.wait_send()
    every.wait_recv()
    gathered[...] = slots[...]


def open_exchange(info_row, blocks, m):
    n_gx = lax.axis_size("gx")
    n_gy = lax.axis_size("gy")
    n_dev = n_gx * n_gy
    levels, rows, cols = blocks[0].shape
    depth = levels * len(blocks)
    vmem = pl.BlockSpec(memory_space=pltpu.VMEM)
    piece_shapes = [(depth, m, cols), (depth, m, cols), (depth, m, rows), (depth, m, rows)]
    piece_shapes += [(depth, m, m)] * (len(HALO_MOVES) - 4)
    out_shape = [jax.ShapeDtypeStruct((n_dev, info_row.shape[1]), jnp.float32)] + [
        jax.ShapeDtypeStruct(shape, jnp.float32) for shape in piece_shapes
    ]
    return pl.pallas_call(
        functools.partial(open_kernel, n_gx, n_gy, m, len(blocks)),
        out_shape=out_shape,
        in_specs=[vmem] * (1 + len(blocks)),
        out_specs=[vmem] * len(out_shape),
        scratch_shapes=[
            pltpu.VMEM((2, depth, m, rows), jnp.float32),
            pltpu.VMEM((len(HALO_MOVES) - 4, depth, m, m), jnp.float32),
            pltpu.VMEM((n_dev, info_row.shape[1]), jnp.float32),
            pltpu.SemaphoreType.DMA,
            pltpu.SemaphoreType.DMA,
            pltpu.SemaphoreType.DMA,
            pltpu.SemaphoreType.DMA((len(piece_shapes),)),
            pltpu.SemaphoreType.DMA((len(piece_shapes),)),
        ],
        compiler_params=pltpu.CompilerParams(has_side_effects=True, collective_id=0),
    )(info_row, *blocks)


def stencil_kernel(n_gx, n_gy, levels, steps, n_block, *refs):
    blocks = refs[:n_block]
    (
        high_ref, low_ref, col_low, col_high, c_ll, c_lh, c_hl, c_hh,
        drag_ref, row_ref, col_ref, thrust_ref, gain_ref,
        lam_out, grad_out,
        ext_ref, states, lams, sens_all, sending, slots, band, send_sem, recv_sem, local_sem,
    ) = refs[n_block:]
    n_dev = n_gx * n_gy
    me = lax.axis_index("gx") * n_gy + lax.axis_index("gy")
    barrier = greet(n_gy, n_dev, me)
    size_r, size_c = ext_ref.shape[1:]
    rows, cols = blocks[0].shape[1:]
    m = high_ref.shape[1]
    band[...] = jnp.zeros(band.shape, jnp.float32)
    width = size_c - cols
    for depth in range(ext_ref.shape[0]):
        ext_ref[depth, :rows, :cols] = blocks[depth // levels][depth % levels]
        ext_ref[depth, rows : rows + m, :cols] = high_ref[depth]
        ext_ref[depth, size_r - m :, :cols] = low_ref[depth]
        for first, column, high_corner, low_corner in (
            (0, col_high, c_hh, c_lh),
            (width - m, col_low, c_hl, c_ll),
        ):
            band[first : first + m, :rows] = column[depth]
            band[first : first + m, rows : rows + m] = high_corner[depth]
            band[first : first + m, size_r - m : size_r] = low_corner[depth]
        ext_ref[depth, :, cols:] = band[...].T[:size_r]

    def west(x):
        return pltpu.roll(x, 1, 0)

    def east(x):
        return pltpu.roll(x, size_r - 1, 0)

    def south(x):
        return pltpu.roll(x, 1, 1)

    def north(x):
        return pltpu.roll(x, size_c - 1, 1)

    def vertical(plane, level, center):
        mix = None
        if level + 1 < levels:
            mix = plane(level + 1) - center
        if level > 0:
            below = plane(level - 1) - center
            mix = below if mix is None else mix + below
        return mix

    for level in range(levels):
        states[0, level] = ext_ref[level]

    def forward(n, carry):
        for level in range(levels):
            center = states[n, level]
            upwind = west(center)
            advect = ext_ref[levels + level]
            diffuse = ext_ref[2 * levels + level]
            states[n + 1, level] = (
                center
                + advect * (upwind - center)
                + diffuse * (east(center) + upwind + north(center) + south(center) - 4.0 * center)
                + VERTICAL_MIX * vertical(lambda l: states[n, l], level, center)
                - drag_ref[level] * (center * jnp.sqrt(center * center + 1.0))
            )
        return carry

    lax.fori_loop(0, steps - 1, forward, 0)
    for level in range(levels):
        lams[0, level] = ext_ref[3 * levels + level]
        sens_all[level] = jnp.zeros(sens_all.shape[1:], jnp.float32)

    def backward(i, carry):
        n = steps - 1 - i
        now = i % 2
        for level in range(levels):
            adjoint = lams[now, level]
            state = states[n, level]
            sens_all[level] = sens_all[level] - adjoint * (state * jnp.sqrt(state * state + 1.0))
            flux_adv = ext_ref[levels + level] * adjoint
            flux_dif = ext_ref[2 * levels + level] * adjoint
            square_one = state * state + 1.0
            slope = (square_one + state * state) / jnp.sqrt(square_one)
            lams[1 - now, level] = (
                adjoint
                - flux_adv
                - 4.0 * flux_dif
                + (east(flux_adv + flux_dif) + west(flux_dif) + north(flux_dif) + south(flux_dif))
                + VERTICAL_MIX * vertical(lambda l: lams[now, l], level, adjoint)
                - drag_ref[level] * slope * adjoint
            )
        return carry

    lax.fori_loop(0, steps, backward, 0)
    weighted = gain_ref[0] * sens_all[0, :rows, :cols]
    for level in range(1, levels):
        weighted = weighted + gain_ref[level] * sens_all[level, :rows, :cols]
    sending[...] = jnp.zeros(sending.shape, jnp.float32)
    for slot in range(row_ref.shape[0]):
        across = jnp.dot(
            weighted, col_ref[slot], precision=HIGHEST, preferred_element_type=jnp.float32
        )
        totals = jnp.sum(row_ref[slot] * across, axis=0, keepdims=True)
        sending[slot : slot + 1, :] = thrust_ref[slot] * totals
    sending[...] = sending[...].T
    pl.semaphore_wait(barrier, n_dev - 1)
    local = pltpu.make_async_copy(sending.at[pl.ds(me, 1)], slots.at[pl.ds(me, 1)], local_sem)
    local.start()
    every = spread_rows(
        n_gy, n_dev, me, lambda target: sending.at[pl.ds(target, 1)], slots, send_sem, recv_sem
    )
    local.wait()
    every.wait_send()
    every.wait_recv()
    grad_out[...] = jnp.sum(slots[...], axis=0, keepdims=True)
    for level in range(levels):
        lam_out[level] = lams[steps % 2, level, :rows, :cols]


def stencil(blocks, landed, drag, levels, row_prof, col_prof, thrust_rows, gain_rows):
    size_r, size_c = drag.shape[1:]
    depth = levels * len(blocks)
    vmem = pl.BlockSpec(memory_space=pltpu.VMEM)
    plane = jax.ShapeDtypeStruct(blocks[0].shape, jnp.float32)
    n_gx = lax.axis_size("gx")
    n_gy = lax.axis_size("gy")
    n_dev = n_gx * n_gy
    width = row_prof.shape[2]
    cells = levels * size_r * size_c
    return pl.pallas_call(
        functools.partial(stencil_kernel, n_gx, n_gy, levels, STEPS, len(blocks)),
        out_shape=[plane, jax.ShapeDtypeStruct((1, width), jnp.float32)],
        in_specs=[vmem] * (len(blocks) + 13),
        out_specs=[vmem, vmem],
        scratch_shapes=[
            pltpu.VMEM((depth, size_r, size_c), jnp.float32),
            pltpu.VMEM((STEPS, levels, size_r, size_c), jnp.float32),
            pltpu.VMEM((2, levels, size_r, size_c), jnp.float32),
            pltpu.VMEM((levels, size_r, size_c), jnp.float32),
            pltpu.VMEM((width, width), jnp.float32),
            pltpu.VMEM((n_dev, width), jnp.float32),
            pltpu.VMEM((size_c - blocks[0].shape[2], -(-size_r // 128) * 128), jnp.float32),
            pltpu.SemaphoreType.DMA,
            pltpu.SemaphoreType.DMA,
            pltpu.SemaphoreType.DMA,
        ],
        compiler_params=pltpu.CompilerParams(
            vmem_limit_bytes=48 * 1024 * 1024, has_side_effects=True, collective_id=1
        ),
        cost_estimate=pl.CostEstimate(
            flops=60 * STEPS * cells, transcendentals=3 * STEPS * cells, bytes_accessed=28 * cells
        ),
    )(*blocks, landed[1], landed[0], *landed[2:], drag, row_prof, col_prof, thrust_rows, gain_rows)


def drag_law(state):
    return state * jnp.sqrt(state * state + 1.0)


def drag_slope(state):
    square_one = state * state + 1.0
    return (square_one + state * state) / jnp.sqrt(square_one)


def vertical(center):
    zero_row = jnp.zeros_like(center[:1])
    from_above = jnp.concatenate([center[1:] - center[:-1], zero_row], axis=0)
    from_below = jnp.concatenate([zero_row, center[:-1] - center[1:]], axis=0)
    return from_above + from_below


def advance(padded, advect, diffuse, drag_coef):
    center = padded[:, 1:-1, 1:-1]
    upwind = padded[:, :-2, 1:-1]
    downwind = padded[:, 2:, 1:-1]
    left_cell = padded[:, 1:-1, :-2]
    right_cell = padded[:, 1:-1, 2:]
    return (
        center
        + advect * (upwind - center)
        + diffuse * (downwind + upwind + right_cell + left_cell - 4.0 * center)
        + VERTICAL_MIX * vertical(center)
        - drag_coef * drag_law(center)
    )


def retreat(padded, advect_ext, diffuse_ext, drag_coef, state):
    flux_adv = advect_ext * padded
    flux_dif = diffuse_ext * padded
    center = padded[:, 1:-1, 1:-1]
    return (
        center
        - flux_adv[:, 1:-1, 1:-1]
        - 4.0 * flux_dif[:, 1:-1, 1:-1]
        + flux_adv[:, 2:, 1:-1]
        + (
            flux_dif[:, 2:, 1:-1]
            + flux_dif[:, :-2, 1:-1]
            + flux_dif[:, 1:-1, 2:]
            + flux_dif[:, 1:-1, :-2]
        )
        + VERTICAL_MIX * vertical(center)
        - drag_coef * drag_slope(state) * center
    )


def trim(array, margin, wanted):
    excess = margin - wanted
    if excess == 0:
        return array
    return array[:, excess:-excess, excess:-excess]


def profiles(first, starts, widths, period, length, inner):
    cells = jnp.arange(length, dtype=jnp.int32)
    cells = jnp.where(cells < inner, cells, cells - length)
    pos = (first + cells - starts[..., None]) % period
    cell_pos = pos.astype(jnp.float32) - (FP - 1) / 2.0
    profile = jnp.exp(-(cell_pos * cell_pos) / (2.0 * widths[..., None] * widths[..., None]))
    return jnp.where(pos < FP, profile, 0.0)


def level_gain():
    level_pos = jnp.arange(LEV, dtype=jnp.float32) - (LEV - 1) / 2.0
    return DRAG_SCALE * jnp.exp(-0.5 * level_pos * level_pos)


def shards(
    velocity, adjoint_seed, courant, viscosity, turbine_tile, turbine_offset, thrust, disk_width
):
    levels, rows, cols = velocity.shape
    n_gx = lax.axis_size("gx")
    n_gy = lax.axis_size("gy")
    m = MARGIN
    per = thrust.shape[0]
    fields = (
        turbine_tile[:, 0].astype(jnp.float32),
        turbine_offset[:, 0].astype(jnp.float32),
        turbine_offset[:, 1].astype(jnp.float32),
        thrust,
        disk_width,
    )
    spare = jnp.zeros((128 - len(fields) * per,), jnp.float32)
    info_row = jnp.concatenate(fields + (spare,))[None, :]
    blocks = (velocity, courant, viscosity, adjoint_seed)
    opened = open_exchange(info_row, blocks, m)
    info = opened[0]
    tiles = info[:, 0:per].astype(jnp.int32)
    row_start = tiles // n_gy * rows + info[:, per : 2 * per].astype(jnp.int32)
    col_start = tiles % n_gy * cols + info[:, 2 * per : 3 * per].astype(jnp.int32)
    thrusts = info[:, 3 * per : 4 * per]
    widths = info[:, 4 * per : 5 * per]
    gx = lax.axis_index("gx")
    gy = lax.axis_index("gy")
    size_r = -(-(rows + 2 * m) // 8) * 8
    size_c = -(-(cols + 2 * m) // 128) * 128
    inner_r = rows + (size_r - rows) // 2
    inner_c = cols + (size_c - cols) // 2
    prof_r = profiles(gx * rows, row_start, widths, n_gx * rows, size_r, inner_r)
    prof_c = profiles(gy * cols, col_start, widths, n_gy * cols, size_c, inner_c)
    gain = level_gain()
    plane = jnp.einsum("dkr,dkc->rc", thrusts[..., None] * prof_r, prof_c, precision=HIGHEST)
    drag = gain[:, None, None] * plane[None]
    spare = ((0, 0), (0, 0), (0, -(-n_gx * n_gy // 128) * 128 - n_gx * n_gy))
    row_prof = jnp.pad(jnp.transpose(prof_r[..., :rows], (1, 2, 0)), spare)
    col_prof = jnp.pad(jnp.transpose(prof_c[..., :cols], (1, 2, 0)), spare)
    thrust_rows = jnp.pad(jnp.transpose(thrusts)[:, None, :], spare)
    gain_rows = jnp.broadcast_to(gain[:, None, None], (levels, 1, cols))
    adjoint, grad = stencil(
        blocks, opened[1:], drag, levels, row_prof, col_prof, thrust_rows, gain_rows
    )
    return adjoint, grad[0, :per]


def solution(mesh):
    placed = (
        P(None, "gx", "gy"),
        P(None, "gx", "gy"),
        P(None, "gx", "gy"),
        P(None, "gx", "gy"),
        P(("gx", "gy"), None),
        P(("gx", "gy"), None),
        P(("gx", "gy")),
        P(("gx", "gy")),
    )
    return jax.shard_map(
        shards,
        mesh=mesh,
        in_specs=placed,
        out_specs=(P(None, "gx", "gy"), P(("gx", "gy"))),
        check_vma=False,
    )
```

```python
import functools

import jax
import jax.numpy as jnp
from jax import lax
from jax.experimental import pallas as pl
from jax.experimental.pallas import tpu as pltpu
from jax.sharding import PartitionSpec as P

LEV = 3
STEPS = 8
FP = 64
MARGIN = 2 * STEPS

VERTICAL_MIX = 0.05
DRAG_SCALE = 0.01
HIGHEST = lax.Precision.HIGHEST


MESH_ID = pl.DeviceIdType.MESH


HALO_MOVES = ((1, 0), (-1, 0), (0, 1), (0, -1), (1, 1), (1, -1), (-1, 1), (-1, -1))


def greet(n_gy, n_dev, me):
    barrier = pltpu.get_barrier_semaphore()
    for step in range(1, n_dev):
        target = lax.rem(me + step, n_dev)
        pl.semaphore_signal(
            barrier, inc=1, device_id=(target // n_gy, target % n_gy), device_id_type=MESH_ID
        )
    return barrier


def spread_rows(n_gy, n_dev, me, src_of, slots, send_sem, recv_sem):
    for step in range(1, n_dev):
        target = lax.rem(me + step, n_dev)
        pltpu.make_async_remote_copy(
            src_of(target),
            slots.at[pl.ds(me, 1)],
            send_sem,
            recv_sem,
            device_id=(target // n_gy, target % n_gy),
            device_id_type=MESH_ID,
        ).start()
    first = lax.rem(me + 1, n_dev)
    rest = pl.ds(0, n_dev - 1)
    return pltpu.make_async_remote_copy(
        slots.at[rest],
        slots.at[rest],
        send_sem,
        recv_sem,
        device_id=(first // n_gy, first % n_gy),
        device_id_type=MESH_ID,
    )


def open_kernel(n_gx, n_gy, m, n_block, info_ref, *refs):
    n_dev = n_gx * n_gy
    n_corner = 0
    blocks = refs[:n_block]
    gathered = refs[n_block + n_corner]
    landed = refs[n_block + n_corner + 1 : n_block + n_corner + 1 + len(HALO_MOVES)]
    columns, corners, slots, send_sem, recv_sem, local_sem, halo_send, halo_recv = refs[
        n_block + n_corner + 1 + len(HALO_MOVES) :
    ]
    levels, rows, cols = blocks[0].shape
    gx = lax.axis_index("gx")
    gy = lax.axis_index("gy")
    me = gx * n_gy + gy
    barrier = greet(n_gy, n_dev, me)
    for field, block_ref in enumerate(blocks):
        for level in range(levels):
            turned = block_ref[level].T
            depth = field * levels + level
            columns[0, depth] = turned[cols - m :]
            columns[1, depth] = turned[:m]
            for index, (side, window) in enumerate(
                ((cols - m, rows - m), (0, rows - m), (cols - m, 0), (0, 0))
            ):
                corners[index, depth] = turned[side : side + m, window : window + m]
    pl.semaphore_wait(barrier, n_dev - 1)
    local = pltpu.make_async_copy(info_ref, slots.at[pl.ds(me, 1)], local_sem)
    local.start()
    parts = lambda window: [
        (block_ref.at[:, window, :], pl.ds(field * levels, levels))
        for field, block_ref in enumerate(blocks)
    ]
    whole = pl.ds(0, n_block * levels)
    sources = (
        parts(pl.ds(rows - m, m)),
        parts(pl.ds(0, m)),
        [(columns.at[0], whole)],
        [(columns.at[1], whole)],
    ) + tuple([(corners.at[index], whole)] for index in range(len(HALO_MOVES) - 4))
    waits = []
    for index, (dx, dy) in enumerate(HALO_MOVES):
        target = (lax.rem(gx + dx + n_gx, n_gx), lax.rem(gy + dy + n_gy, n_gy))
        for source, depth in sources[index]:
            pltpu.make_async_remote_copy(
                source,
                landed[index].at[depth],
                halo_send.at[index],
                halo_recv.at[index],
                device_id=target,
                device_id_type=MESH_ID,
            ).start()
        waits.append(
            pltpu.make_async_remote_copy(
                landed[index],
                landed[index],
                halo_send.at[index],
                halo_recv.at[index],
                device_id=target,
                device_id_type=MESH_ID,
            )
        )
    every = spread_rows(n_gy, n_dev, me, lambda target: info_ref, slots, send_sem, recv_sem)
    local.wait()
    for copy in waits:
        copy.wait_send()
        copy.wait_recv()
    every.wait_send()
    every.wait_recv()
    gathered[...] = slots[...]


def open_exchange(info_row, blocks, m):
    n_gx = lax.axis_size("gx")
    n_gy = lax.axis_size("gy")
    n_dev = n_gx * n_gy
    levels, rows, cols = blocks[0].shape
    depth = levels * len(blocks)
    vmem = pl.BlockSpec(memory_space=pltpu.VMEM)
    piece_shapes = [(depth, m, cols), (depth, m, cols), (depth, m, rows), (depth, m, rows)]
    piece_shapes += [(depth, m, m)] * (len(HALO_MOVES) - 4)
    out_shape = [jax.ShapeDtypeStruct((n_dev, info_row.shape[1]), jnp.float32)] + [
        jax.ShapeDtypeStruct(shape, jnp.float32) for shape in piece_shapes
    ]
    return pl.pallas_call(
        functools.partial(open_kernel, n_gx, n_gy, m, len(blocks)),
        out_shape=out_shape,
        in_specs=[vmem] * (1 + len(blocks)),
        out_specs=[vmem] * len(out_shape),
        scratch_shapes=[
            pltpu.VMEM((2, depth, m, rows), jnp.float32),
            pltpu.VMEM((len(HALO_MOVES) - 4, depth, m, m), jnp.float32),
            pltpu.VMEM((n_dev, info_row.shape[1]), jnp.float32),
            pltpu.SemaphoreType.DMA,
            pltpu.SemaphoreType.DMA,
            pltpu.SemaphoreType.DMA,
            pltpu.SemaphoreType.DMA((len(piece_shapes),)),
            pltpu.SemaphoreType.DMA((len(piece_shapes),)),
        ],
        compiler_params=pltpu.CompilerParams(has_side_effects=True, collective_id=0),
    )(info_row, *blocks)


def column_band(landed, m, size_r, size_c, cols):
    row_low, row_high, col_low, col_high, c_ll, c_lh, c_hl, c_hh = landed
    depth = col_low.shape[0]
    width = size_c - cols
    span = -(-size_r // 128) * 128

    def edge(column, high_corner, low_corner):
        fill = jnp.zeros((depth, m, span - size_r), jnp.float32)
        return jnp.concatenate(
            [column, high_corner, low_corner, fill],
            axis=2,
        )

    fill = jnp.zeros((depth, width - 2 * m, span), jnp.float32)
    return jnp.concatenate([edge(col_high, c_hh, c_lh), fill, edge(col_low, c_hl, c_ll)], axis=1)


def stencil_kernel(n_gx, n_gy, levels, steps, n_block, *refs):
    blocks = refs[:n_block]
    (
        high_ref, low_ref, band_ref, drag_ref, row_ref, col_ref, thrust_ref, gain_ref,
        lam_out, grad_out,
        ext_ref, states, lams, sens_all, sending, slots, roots, send_sem, recv_sem, local_sem,
    ) = refs[n_block:]
    n_dev = n_gx * n_gy
    me = lax.axis_index("gx") * n_gy + lax.axis_index("gy")
    barrier = greet(n_gy, n_dev, me)
    size_r, size_c = ext_ref.shape[1:]
    rows, cols = blocks[0].shape[1:]
    m = high_ref.shape[1]
    for depth in range(ext_ref.shape[0]):
        ext_ref[depth, :rows, :cols] = blocks[depth // levels][depth % levels]
        ext_ref[depth, rows : rows + m, :cols] = high_ref[depth]
        ext_ref[depth, size_r - m :, :cols] = low_ref[depth]
        ext_ref[depth, :, cols:] = band_ref[depth].T[:size_r]

    def west(x):
        return pltpu.roll(x, 1, 0)

    def east(x):
        return pltpu.roll(x, size_r - 1, 0)

    def south(x):
        return pltpu.roll(x, 1, 1)

    def north(x):
        return pltpu.roll(x, size_c - 1, 1)

    def vertical(plane, level, center):
        mix = None
        if level + 1 < levels:
            mix = plane(level + 1) - center
        if level > 0:
            below = plane(level - 1) - center
            mix = below if mix is None else mix + below
        return mix

    for level in range(levels):
        states[0, level] = ext_ref[level]

    def forward(n, carry):
        for level in range(levels):
            center = states[n, level]
            root = jnp.sqrt(center * center + 1.0)
            roots[n, level] = root
            upwind = west(center)
            advect = ext_ref[levels + level]
            diffuse = ext_ref[2 * levels + level]
            states[n + 1, level] = (
                center
                + advect * (upwind - center)
                + diffuse * (east(center) + upwind + north(center) + south(center) - 4.0 * center)
                + VERTICAL_MIX * vertical(lambda l: states[n, l], level, center)
                - drag_ref[level] * (center * root)
            )
        return carry

    lax.fori_loop(0, steps - 1, forward, 0)
    for level in range(levels):
        last = states[steps - 1, level]
        roots[steps - 1, level] = jnp.sqrt(last * last + 1.0)
    for level in range(levels):
        lams[0, level] = ext_ref[3 * levels + level]
        sens_all[level] = jnp.zeros(sens_all.shape[1:], jnp.float32)

    def backward(i, carry):
        n = steps - 1 - i
        now = i % 2
        for level in range(levels):
            adjoint = lams[now, level]
            state = states[n, level]
            root = roots[n, level]
            sens_all[level] = sens_all[level] - adjoint * (state * root)
            flux_adv = ext_ref[levels + level] * adjoint
            flux_dif = ext_ref[2 * levels + level] * adjoint
            square = state * state
            slope = ((square + 1.0) + square) / root
            lams[1 - now, level] = (
                adjoint
                - flux_adv
                - 4.0 * flux_dif
                + (east(flux_adv + flux_dif) + west(flux_dif) + north(flux_dif) + south(flux_dif))
                + VERTICAL_MIX * vertical(lambda l: lams[now, l], level, adjoint)
                - drag_ref[level] * slope * adjoint
            )
        return carry

    lax.fori_loop(0, steps, backward, 0)
    weighted = gain_ref[0] * sens_all[0, :rows, :cols]
    for level in range(1, levels):
        weighted = weighted + gain_ref[level] * sens_all[level, :rows, :cols]
    sending[...] = jnp.zeros(sending.shape, jnp.float32)
    for slot in range(row_ref.shape[0]):
        across = jnp.dot(
            weighted, col_ref[slot], precision=HIGHEST, preferred_element_type=jnp.float32
        )
        totals = jnp.sum(row_ref[slot] * across, axis=0, keepdims=True)
        sending[slot : slot + 1, :] = thrust_ref[slot] * totals
    sending[...] = sending[...].T
    pl.semaphore_wait(barrier, n_dev - 1)
    local = pltpu.make_async_copy(sending.at[pl.ds(me, 1)], slots.at[pl.ds(me, 1)], local_sem)
    local.start()
    every = spread_rows(
        n_gy, n_dev, me, lambda target: sending.at[pl.ds(target, 1)], slots, send_sem, recv_sem
    )
    local.wait()
    every.wait_send()
    every.wait_recv()
    grad_out[...] = jnp.sum(slots[...], axis=0, keepdims=True)
    for level in range(levels):
        lam_out[level] = lams[steps % 2, level, :rows, :cols]


def stencil(blocks, landed, band, drag, levels, row_prof, col_prof, thrust_rows, gain_rows):
    size_r, size_c = drag.shape[1:]
    depth = levels * len(blocks)
    vmem = pl.BlockSpec(memory_space=pltpu.VMEM)
    plane = jax.ShapeDtypeStruct(blocks[0].shape, jnp.float32)
    n_gx = lax.axis_size("gx")
    n_gy = lax.axis_size("gy")
    n_dev = n_gx * n_gy
    width = row_prof.shape[2]
    cells = levels * size_r * size_c
    return pl.pallas_call(
        functools.partial(stencil_kernel, n_gx, n_gy, levels, STEPS, len(blocks)),
        out_shape=[plane, jax.ShapeDtypeStruct((1, width), jnp.float32)],
        in_specs=[vmem] * (len(blocks) + 8),
        out_specs=[vmem, vmem],
        scratch_shapes=[
            pltpu.VMEM((depth, size_r, size_c), jnp.float32),
            pltpu.VMEM((STEPS, levels, size_r, size_c), jnp.float32),
            pltpu.VMEM((2, levels, size_r, size_c), jnp.float32),
            pltpu.VMEM((levels, size_r, size_c), jnp.float32),
            pltpu.VMEM((width, width), jnp.float32),
            pltpu.VMEM((n_dev, width), jnp.float32),
            pltpu.VMEM((STEPS, levels, size_r, size_c), jnp.float32),
            pltpu.SemaphoreType.DMA,
            pltpu.SemaphoreType.DMA,
            pltpu.SemaphoreType.DMA,
        ],
        compiler_params=pltpu.CompilerParams(
            vmem_limit_bytes=48 * 1024 * 1024, has_side_effects=True, collective_id=1
        ),
        cost_estimate=pl.CostEstimate(
            flops=60 * STEPS * cells, transcendentals=3 * STEPS * cells, bytes_accessed=28 * cells
        ),
    )(*blocks, landed[1], landed[0], band, drag, row_prof, col_prof, thrust_rows, gain_rows)


def drag_law(state):
    return state * jnp.sqrt(state * state + 1.0)


def drag_slope(state):
    square_one = state * state + 1.0
    return (square_one + state * state) / jnp.sqrt(square_one)


def vertical(center):
    zero_row = jnp.zeros_like(center[:1])
    from_above = jnp.concatenate([center[1:] - center[:-1], zero_row], axis=0)
    from_below = jnp.concatenate([zero_row, center[:-1] - center[1:]], axis=0)
    return from_above + from_below


def advance(padded, advect, diffuse, drag_coef):
    center = padded[:, 1:-1, 1:-1]
    upwind = padded[:, :-2, 1:-1]
    downwind = padded[:, 2:, 1:-1]
    left_cell = padded[:, 1:-1, :-2]
    right_cell = padded[:, 1:-1, 2:]
    return (
        center
        + advect * (upwind - center)
        + diffuse * (downwind + upwind + right_cell + left_cell - 4.0 * center)
        + VERTICAL_MIX * vertical(center)
        - drag_coef * drag_law(center)
    )


def retreat(padded, advect_ext, diffuse_ext, drag_coef, state):
    flux_adv = advect_ext * padded
    flux_dif = diffuse_ext * padded
    center = padded[:, 1:-1, 1:-1]
    return (
        center
        - flux_adv[:, 1:-1, 1:-1]
        - 4.0 * flux_dif[:, 1:-1, 1:-1]
        + flux_adv[:, 2:, 1:-1]
        + (
            flux_dif[:, 2:, 1:-1]
            + flux_dif[:, :-2, 1:-1]
            + flux_dif[:, 1:-1, 2:]
            + flux_dif[:, 1:-1, :-2]
        )
        + VERTICAL_MIX * vertical(center)
        - drag_coef * drag_slope(state) * center
    )


def trim(array, margin, wanted):
    excess = margin - wanted
    if excess == 0:
        return array
    return array[:, excess:-excess, excess:-excess]


def profiles(first, starts, widths, period, length, inner):
    cells = jnp.arange(length, dtype=jnp.int32)
    cells = jnp.where(cells < inner, cells, cells - length)
    pos = (first + cells - starts[..., None]) % period
    cell_pos = pos.astype(jnp.float32) - (FP - 1) / 2.0
    profile = jnp.exp(-(cell_pos * cell_pos) / (2.0 * widths[..., None] * widths[..., None]))
    return jnp.where(pos < FP, profile, 0.0)


def level_gain():
    level_pos = jnp.arange(LEV, dtype=jnp.float32) - (LEV - 1) / 2.0
    return DRAG_SCALE * jnp.exp(-0.5 * level_pos * level_pos)


def shards(
    velocity, adjoint_seed, courant, viscosity, turbine_tile, turbine_offset, thrust, disk_width
):
    levels, rows, cols = velocity.shape
    n_gx = lax.axis_size("gx")
    n_gy = lax.axis_size("gy")
    m = MARGIN
    per = thrust.shape[0]
    fields = (
        turbine_tile[:, 0].astype(jnp.float32),
        turbine_offset[:, 0].astype(jnp.float32),
        turbine_offset[:, 1].astype(jnp.float32),
        thrust,
        disk_width,
    )
    spare = jnp.zeros((128 - len(fields) * per,), jnp.float32)
    info_row = jnp.concatenate(fields + (spare,))[None, :]
    blocks = (velocity, courant, viscosity, adjoint_seed)
    opened = open_exchange(info_row, blocks, m)
    info = opened[0]
    tiles = info[:, 0:per].astype(jnp.int32)
    row_start = tiles // n_gy * rows + info[:, per : 2 * per].astype(jnp.int32)
    col_start = tiles % n_gy * cols + info[:, 2 * per : 3 * per].astype(jnp.int32)
    thrusts = info[:, 3 * per : 4 * per]
    widths = info[:, 4 * per : 5 * per]
    gx = lax.axis_index("gx")
    gy = lax.axis_index("gy")
    size_r = -(-(rows + 2 * m) // 8) * 8
    size_c = -(-(cols + 2 * m) // 128) * 128
    inner_r = rows + (size_r - rows) // 2
    inner_c = cols + (size_c - cols) // 2
    prof_r = profiles(gx * rows, row_start, widths, n_gx * rows, size_r, inner_r)
    prof_c = profiles(gy * cols, col_start, widths, n_gy * cols, size_c, inner_c)
    gain = level_gain()
    plane = jnp.einsum("dkr,dkc->rc", thrusts[..., None] * prof_r, prof_c, precision=HIGHEST)
    drag = gain[:, None, None] * plane[None]
    band = column_band(opened[1:], m, size_r, size_c, cols)
    spare = ((0, 0), (0, 0), (0, -(-n_gx * n_gy // 128) * 128 - n_gx * n_gy))
    row_prof = jnp.pad(jnp.transpose(prof_r[..., :rows], (1, 2, 0)), spare)
    col_prof = jnp.pad(jnp.transpose(prof_c[..., :cols], (1, 2, 0)), spare)
    thrust_rows = jnp.pad(jnp.transpose(thrusts)[:, None, :], spare)
    gain_rows = jnp.broadcast_to(gain[:, None, None], (levels, 1, cols))
    adjoint, grad = stencil(
        blocks, opened[1:], band, drag, levels, row_prof, col_prof, thrust_rows, gain_rows
    )
    return adjoint, grad[0, :per]


def solution(mesh):
    placed = (
        P(None, "gx", "gy"),
        P(None, "gx", "gy"),
        P(None, "gx", "gy"),
        P(None, "gx", "gy"),
        P(("gx", "gy"), None),
        P(("gx", "gy"), None),
        P(("gx", "gy")),
        P(("gx", "gy")),
    )
    return jax.shard_map(
        shards,
        mesh=mesh,
        in_specs=placed,
        out_specs=(P(None, "gx", "gy"), P(("gx", "gy"))),
        check_vma=False,
    )
```

```python
import functools

import jax
import jax.numpy as jnp
from jax import lax
from jax.experimental import pallas as pl
from jax.experimental.pallas import tpu as pltpu
from jax.sharding import PartitionSpec as P

LEV = 3
STEPS = 8
FP = 64
MARGIN = 2 * STEPS

VERTICAL_MIX = 0.05
DRAG_SCALE = 0.01
HIGHEST = lax.Precision.HIGHEST


MESH_ID = pl.DeviceIdType.MESH


HALO_MOVES = ((1, 0), (-1, 0), (0, 1), (0, -1), (1, 1), (1, -1), (-1, 1), (-1, -1))


def greet(n_gy, n_dev, me):
    barrier = pltpu.get_barrier_semaphore()
    for step in range(1, n_dev):
        target = lax.rem(me + step, n_dev)
        pl.semaphore_signal(
            barrier, inc=1, device_id=(target // n_gy, target % n_gy), device_id_type=MESH_ID
        )
    return barrier


def spread_rows(n_gy, n_dev, me, src_of, slots, send_sem, recv_sem):
    for step in range(1, n_dev):
        target = lax.rem(me + step, n_dev)
        pltpu.make_async_remote_copy(
            src_of(target),
            slots.at[pl.ds(me, 1)],
            send_sem,
            recv_sem,
            device_id=(target // n_gy, target % n_gy),
            device_id_type=MESH_ID,
        ).start()
    first = lax.rem(me + 1, n_dev)
    rest = pl.ds(0, n_dev - 1)
    return pltpu.make_async_remote_copy(
        slots.at[rest],
        slots.at[rest],
        send_sem,
        recv_sem,
        device_id=(first // n_gy, first % n_gy),
        device_id_type=MESH_ID,
    )


def open_kernel(n_gx, n_gy, m, n_block, info_ref, *refs):
    n_dev = n_gx * n_gy
    n_corner = 0
    blocks = refs[:n_block]
    gathered = refs[n_block + n_corner]
    landed = refs[n_block + n_corner + 1 : n_block + n_corner + 1 + len(HALO_MOVES)]
    columns, corners, slots, send_sem, recv_sem, local_sem, halo_send, halo_recv = refs[
        n_block + n_corner + 1 + len(HALO_MOVES) :
    ]
    levels, rows, cols = blocks[0].shape
    gx = lax.axis_index("gx")
    gy = lax.axis_index("gy")
    me = gx * n_gy + gy
    barrier = greet(n_gy, n_dev, me)
    for field, block_ref in enumerate(blocks):
        for level in range(levels):
            turned = block_ref[level].T
            depth = field * levels + level
            columns[0, depth] = turned[cols - m :]
            columns[1, depth] = turned[:m]
            for index, (side, window) in enumerate(
                ((cols - m, rows - m), (0, rows - m), (cols - m, 0), (0, 0))
            ):
                corners[index, depth] = turned[side : side + m, window : window + m]
    pl.semaphore_wait(barrier, n_dev - 1)
    local = pltpu.make_async_copy(info_ref, slots.at[pl.ds(me, 1)], local_sem)
    local.start()
    parts = lambda window: [
        (block_ref.at[:, window, :], pl.ds(field * levels, levels))
        for field, block_ref in enumerate(blocks)
    ]
    whole = pl.ds(0, n_block * levels)
    sources = (
        parts(pl.ds(rows - m, m)),
        parts(pl.ds(0, m)),
        [(columns.at[0], whole)],
        [(columns.at[1], whole)],
    ) + tuple([(corners.at[index], whole)] for index in range(len(HALO_MOVES) - 4))
    waits = []
    for index, (dx, dy) in enumerate(HALO_MOVES):
        target = (lax.rem(gx + dx + n_gx, n_gx), lax.rem(gy + dy + n_gy, n_gy))
        for source, depth in sources[index]:
            pltpu.make_async_remote_copy(
                source,
                landed[index].at[depth],
                halo_send.at[index],
                halo_recv.at[index],
                device_id=target,
                device_id_type=MESH_ID,
            ).start()
        waits.append(
            pltpu.make_async_remote_copy(
                landed[index],
                landed[index],
                halo_send.at[index],
                halo_recv.at[index],
                device_id=target,
                device_id_type=MESH_ID,
            )
        )
    every = spread_rows(n_gy, n_dev, me, lambda target: info_ref, slots, send_sem, recv_sem)
    local.wait()
    for copy in waits:
        copy.wait_send()
        copy.wait_recv()
    every.wait_send()
    every.wait_recv()
    gathered[...] = slots[...]


def open_exchange(info_row, blocks, m):
    n_gx = lax.axis_size("gx")
    n_gy = lax.axis_size("gy")
    n_dev = n_gx * n_gy
    levels, rows, cols = blocks[0].shape
    depth = levels * len(blocks)
    vmem = pl.BlockSpec(memory_space=pltpu.VMEM)
    piece_shapes = [(depth, m, cols), (depth, m, cols), (depth, m, rows), (depth, m, rows)]
    piece_shapes += [(depth, m, m)] * (len(HALO_MOVES) - 4)
    out_shape = [jax.ShapeDtypeStruct((n_dev, info_row.shape[1]), jnp.float32)] + [
        jax.ShapeDtypeStruct(shape, jnp.float32) for shape in piece_shapes
    ]
    return pl.pallas_call(
        functools.partial(open_kernel, n_gx, n_gy, m, len(blocks)),
        out_shape=out_shape,
        in_specs=[vmem] * (1 + len(blocks)),
        out_specs=[vmem] * len(out_shape),
        scratch_shapes=[
            pltpu.VMEM((2, depth, m, rows), jnp.float32),
            pltpu.VMEM((len(HALO_MOVES) - 4, depth, m, m), jnp.float32),
            pltpu.VMEM((n_dev, info_row.shape[1]), jnp.float32),
            pltpu.SemaphoreType.DMA,
            pltpu.SemaphoreType.DMA,
            pltpu.SemaphoreType.DMA,
            pltpu.SemaphoreType.DMA((len(piece_shapes),)),
            pltpu.SemaphoreType.DMA((len(piece_shapes),)),
        ],
        compiler_params=pltpu.CompilerParams(has_side_effects=True, collective_id=0),
    )(info_row, *blocks)


def column_band(landed, m, size_r, size_c, cols):
    row_low, row_high, col_low, col_high, c_ll, c_lh, c_hl, c_hh = landed
    depth = col_low.shape[0]
    width = size_c - cols
    span = -(-size_r // 128) * 128

    def edge(column, high_corner, low_corner):
        fill = jnp.zeros((depth, m, span - size_r), jnp.float32)
        return jnp.concatenate(
            [column, high_corner, low_corner, fill],
            axis=2,
        )

    fill = jnp.zeros((depth, width - 2 * m, span), jnp.float32)
    return jnp.concatenate([edge(col_high, c_hh, c_lh), fill, edge(col_low, c_hl, c_ll)], axis=1)


def stencil_kernel(n_gx, n_gy, levels, steps, n_block, *refs):
    blocks = refs[:n_block]
    (
        high_ref, low_ref, band_ref, drag_ref, row_ref, col_ref, thrust_ref, gain_ref,
        lam_out, grad_out,
        ext_ref, states, lams, sens_all, sending, slots, roots, send_sem, recv_sem, local_sem,
    ) = refs[n_block:]
    n_dev = n_gx * n_gy
    me = lax.axis_index("gx") * n_gy + lax.axis_index("gy")
    barrier = greet(n_gy, n_dev, me)
    size_r, size_c = ext_ref.shape[1:]
    rows, cols = blocks[0].shape[1:]
    m = high_ref.shape[1]
    for depth in range(ext_ref.shape[0]):
        ext_ref[depth, :rows, :cols] = blocks[depth // levels][depth % levels]
        ext_ref[depth, rows : rows + m, :cols] = high_ref[depth]
        ext_ref[depth, size_r - m :, :cols] = low_ref[depth]
        ext_ref[depth, :, cols:] = band_ref[depth].T[:size_r]

    def west(x):
        return pltpu.roll(x, 1, 0)

    def east(x):
        return pltpu.roll(x, size_r - 1, 0)

    def south(x):
        return pltpu.roll(x, 1, 1)

    def north(x):
        return pltpu.roll(x, size_c - 1, 1)

    def vertical(plane, level, center):
        mix = None
        if level + 1 < levels:
            mix = plane(level + 1) - center
        if level > 0:
            below = plane(level - 1) - center
            mix = below if mix is None else mix + below
        return mix

    for level in range(levels):
        states[0, level] = ext_ref[level]

    def forward(n, carry):
        for level in range(levels):
            center = states[n, level]
            root = jnp.sqrt(center * center + 1.0)
            roots[n, level] = root
            upwind = west(center)
            advect = ext_ref[levels + level]
            diffuse = ext_ref[2 * levels + level]
            states[n + 1, level] = (
                center
                + advect * (upwind - center)
                + diffuse * (east(center) + upwind + north(center) + south(center) - 4.0 * center)
                + VERTICAL_MIX * vertical(lambda l: states[n, l], level, center)
                - drag_ref[level] * (center * root)
            )
        return carry

    lax.fori_loop(0, steps - 1, forward, 0, unroll=True)
    for level in range(levels):
        last = states[steps - 1, level]
        roots[steps - 1, level] = jnp.sqrt(last * last + 1.0)
    for level in range(levels):
        lams[0, level] = ext_ref[3 * levels + level]
        sens_all[level] = jnp.zeros(sens_all.shape[1:], jnp.float32)

    def backward(i, carry):
        n = steps - 1 - i
        now = i % 2
        for level in range(levels):
            adjoint = lams[now, level]
            state = states[n, level]
            root = roots[n, level]
            sens_all[level] = sens_all[level] - adjoint * (state * root)
            flux_adv = ext_ref[levels + level] * adjoint
            flux_dif = ext_ref[2 * levels + level] * adjoint
            square = state * state
            slope = ((square + 1.0) + square) / root
            lams[1 - now, level] = (
                adjoint
                - flux_adv
                - 4.0 * flux_dif
                + (east(flux_adv + flux_dif) + west(flux_dif) + north(flux_dif) + south(flux_dif))
                + VERTICAL_MIX * vertical(lambda l: lams[now, l], level, adjoint)
                - drag_ref[level] * slope * adjoint
            )
        return carry

    lax.fori_loop(0, steps, backward, 0, unroll=True)
    weighted = gain_ref[0] * sens_all[0, :rows, :cols]
    for level in range(1, levels):
        weighted = weighted + gain_ref[level] * sens_all[level, :rows, :cols]
    sending[...] = jnp.zeros(sending.shape, jnp.float32)
    for slot in range(row_ref.shape[0]):
        across = jnp.dot(
            weighted, col_ref[slot], precision=HIGHEST, preferred_element_type=jnp.float32
        )
        totals = jnp.sum(row_ref[slot] * across, axis=0, keepdims=True)
        sending[slot : slot + 1, :] = thrust_ref[slot] * totals
    sending[...] = sending[...].T
    pl.semaphore_wait(barrier, n_dev - 1)
    local = pltpu.make_async_copy(sending.at[pl.ds(me, 1)], slots.at[pl.ds(me, 1)], local_sem)
    local.start()
    every = spread_rows(
        n_gy, n_dev, me, lambda target: sending.at[pl.ds(target, 1)], slots, send_sem, recv_sem
    )
    local.wait()
    every.wait_send()
    every.wait_recv()
    grad_out[...] = jnp.sum(slots[...], axis=0, keepdims=True)
    for level in range(levels):
        lam_out[level] = lams[steps % 2, level, :rows, :cols]


def stencil(blocks, landed, band, drag, levels, row_prof, col_prof, thrust_rows, gain_rows):
    size_r, size_c = drag.shape[1:]
    depth = levels * len(blocks)
    vmem = pl.BlockSpec(memory_space=pltpu.VMEM)
    plane = jax.ShapeDtypeStruct(blocks[0].shape, jnp.float32)
    n_gx = lax.axis_size("gx")
    n_gy = lax.axis_size("gy")
    n_dev = n_gx * n_gy
    width = row_prof.shape[2]
    cells = levels * size_r * size_c
    return pl.pallas_call(
        functools.partial(stencil_kernel, n_gx, n_gy, levels, STEPS, len(blocks)),
        out_shape=[plane, jax.ShapeDtypeStruct((1, width), jnp.float32)],
        in_specs=[vmem] * (len(blocks) + 8),
        out_specs=[vmem, vmem],
        scratch_shapes=[
            pltpu.VMEM((depth, size_r, size_c), jnp.float32),
            pltpu.VMEM((STEPS, levels, size_r, size_c), jnp.float32),
            pltpu.VMEM((2, levels, size_r, size_c), jnp.float32),
            pltpu.VMEM((levels, size_r, size_c), jnp.float32),
            pltpu.VMEM((width, width), jnp.float32),
            pltpu.VMEM((n_dev, width), jnp.float32),
            pltpu.VMEM((STEPS, levels, size_r, size_c), jnp.float32),
            pltpu.SemaphoreType.DMA,
            pltpu.SemaphoreType.DMA,
            pltpu.SemaphoreType.DMA,
        ],
        compiler_params=pltpu.CompilerParams(
            vmem_limit_bytes=48 * 1024 * 1024, has_side_effects=True, collective_id=1
        ),
        cost_estimate=pl.CostEstimate(
            flops=60 * STEPS * cells, transcendentals=3 * STEPS * cells, bytes_accessed=28 * cells
        ),
    )(*blocks, landed[1], landed[0], band, drag, row_prof, col_prof, thrust_rows, gain_rows)


def drag_law(state):
    return state * jnp.sqrt(state * state + 1.0)


def drag_slope(state):
    square_one = state * state + 1.0
    return (square_one + state * state) / jnp.sqrt(square_one)


def vertical(center):
    zero_row = jnp.zeros_like(center[:1])
    from_above = jnp.concatenate([center[1:] - center[:-1], zero_row], axis=0)
    from_below = jnp.concatenate([zero_row, center[:-1] - center[1:]], axis=0)
    return from_above + from_below


def advance(padded, advect, diffuse, drag_coef):
    center = padded[:, 1:-1, 1:-1]
    upwind = padded[:, :-2, 1:-1]
    downwind = padded[:, 2:, 1:-1]
    left_cell = padded[:, 1:-1, :-2]
    right_cell = padded[:, 1:-1, 2:]
    return (
        center
        + advect * (upwind - center)
        + diffuse * (downwind + upwind + right_cell + left_cell - 4.0 * center)
        + VERTICAL_MIX * vertical(center)
        - drag_coef * drag_law(center)
    )


def retreat(padded, advect_ext, diffuse_ext, drag_coef, state):
    flux_adv = advect_ext * padded
    flux_dif = diffuse_ext * padded
    center = padded[:, 1:-1, 1:-1]
    return (
        center
        - flux_adv[:, 1:-1, 1:-1]
        - 4.0 * flux_dif[:, 1:-1, 1:-1]
        + flux_adv[:, 2:, 1:-1]
        + (
            flux_dif[:, 2:, 1:-1]
            + flux_dif[:, :-2, 1:-1]
            + flux_dif[:, 1:-1, 2:]
            + flux_dif[:, 1:-1, :-2]
        )
        + VERTICAL_MIX * vertical(center)
        - drag_coef * drag_slope(state) * center
    )


def trim(array, margin, wanted):
    excess = margin - wanted
    if excess == 0:
        return array
    return array[:, excess:-excess, excess:-excess]


def profiles(first, starts, widths, period, length, inner):
    cells = jnp.arange(length, dtype=jnp.int32)
    cells = jnp.where(cells < inner, cells, cells - length)
    pos = (first + cells - starts[..., None]) % period
    cell_pos = pos.astype(jnp.float32) - (FP - 1) / 2.0
    profile = jnp.exp(-(cell_pos * cell_pos) / (2.0 * widths[..., None] * widths[..., None]))
    return jnp.where(pos < FP, profile, 0.0)


def level_gain():
    level_pos = jnp.arange(LEV, dtype=jnp.float32) - (LEV - 1) / 2.0
    return DRAG_SCALE * jnp.exp(-0.5 * level_pos * level_pos)


def shards(
    velocity, adjoint_seed, courant, viscosity, turbine_tile, turbine_offset, thrust, disk_width
):
    levels, rows, cols = velocity.shape
    n_gx = lax.axis_size("gx")
    n_gy = lax.axis_size("gy")
    m = MARGIN
    per = thrust.shape[0]
    fields = (
        turbine_tile[:, 0].astype(jnp.float32),
        turbine_offset[:, 0].astype(jnp.float32),
        turbine_offset[:, 1].astype(jnp.float32),
        thrust,
        disk_width,
    )
    spare = jnp.zeros((128 - len(fields) * per,), jnp.float32)
    info_row = jnp.concatenate(fields + (spare,))[None, :]
    blocks = (velocity, courant, viscosity, adjoint_seed)
    opened = open_exchange(info_row, blocks, m)
    info = opened[0]
    tiles = info[:, 0:per].astype(jnp.int32)
    row_start = tiles // n_gy * rows + info[:, per : 2 * per].astype(jnp.int32)
    col_start = tiles % n_gy * cols + info[:, 2 * per : 3 * per].astype(jnp.int32)
    thrusts = info[:, 3 * per : 4 * per]
    widths = info[:, 4 * per : 5 * per]
    gx = lax.axis_index("gx")
    gy = lax.axis_index("gy")
    size_r = -(-(rows + 2 * m) // 8) * 8
    size_c = -(-(cols + 2 * m) // 128) * 128
    inner_r = rows + (size_r - rows) // 2
    inner_c = cols + (size_c - cols) // 2
    prof_r = profiles(gx * rows, row_start, widths, n_gx * rows, size_r, inner_r)
    prof_c = profiles(gy * cols, col_start, widths, n_gy * cols, size_c, inner_c)
    gain = level_gain()
    plane = jnp.einsum("dkr,dkc->rc", thrusts[..., None] * prof_r, prof_c, precision=HIGHEST)
    drag = gain[:, None, None] * plane[None]
    band = column_band(opened[1:], m, size_r, size_c, cols)
    spare = ((0, 0), (0, 0), (0, -(-n_gx * n_gy // 128) * 128 - n_gx * n_gy))
    row_prof = jnp.pad(jnp.transpose(prof_r[..., :rows], (1, 2, 0)), spare)
    col_prof = jnp.pad(jnp.transpose(prof_c[..., :cols], (1, 2, 0)), spare)
    thrust_rows = jnp.pad(jnp.transpose(thrusts)[:, None, :], spare)
    gain_rows = jnp.broadcast_to(gain[:, None, None], (levels, 1, cols))
    adjoint, grad = stencil(
        blocks, opened[1:], band, drag, levels, row_prof, col_prof, thrust_rows, gain_rows
    )
    return adjoint, grad[0, :per]


def solution(mesh):
    placed = (
        P(None, "gx", "gy"),
        P(None, "gx", "gy"),
        P(None, "gx", "gy"),
        P(None, "gx", "gy"),
        P(("gx", "gy"), None),
        P(("gx", "gy"), None),
        P(("gx", "gy")),
        P(("gx", "gy")),
    )
    return jax.shard_map(
        shards,
        mesh=mesh,
        in_specs=placed,
        out_specs=(P(None, "gx", "gy"), P(("gx", "gy"))),
        check_vma=False,
    )
```

```python
import functools

import jax
import jax.numpy as jnp
from jax import lax
from jax.experimental import pallas as pl
from jax.experimental.pallas import tpu as pltpu
from jax.sharding import PartitionSpec as P

LEV = 3
STEPS = 8
FP = 64
MARGIN = 2 * STEPS

VERTICAL_MIX = 0.05
DRAG_SCALE = 0.01
HIGHEST = lax.Precision.HIGHEST


MESH_ID = pl.DeviceIdType.MESH


HALO_MOVES = ((1, 0), (-1, 0), (0, 1), (0, -1), (1, 1), (1, -1), (-1, 1), (-1, -1))


def greet(n_gy, n_dev, me):
    barrier = pltpu.get_barrier_semaphore()
    for step in range(1, n_dev):
        target = lax.rem(me + step, n_dev)
        pl.semaphore_signal(
            barrier, inc=1, device_id=(target // n_gy, target % n_gy), device_id_type=MESH_ID
        )
    return barrier


def spread_rows(n_gy, n_dev, me, src_of, slots, send_sem, recv_sem):
    for step in range(1, n_dev):
        target = lax.rem(me + step, n_dev)
        pltpu.make_async_remote_copy(
            src_of(target),
            slots.at[pl.ds(me, 1)],
            send_sem,
            recv_sem,
            device_id=(target // n_gy, target % n_gy),
            device_id_type=MESH_ID,
        ).start()
    first = lax.rem(me + 1, n_dev)
    rest = pl.ds(0, n_dev - 1)
    return pltpu.make_async_remote_copy(
        slots.at[rest],
        slots.at[rest],
        send_sem,
        recv_sem,
        device_id=(first // n_gy, first % n_gy),
        device_id_type=MESH_ID,
    )


def open_kernel(n_gx, n_gy, m, n_block, info_ref, *refs):
    n_dev = n_gx * n_gy
    n_corner = 0
    blocks = refs[:n_block]
    gathered = refs[n_block + n_corner]
    landed = refs[n_block + n_corner + 1 : n_block + n_corner + 1 + len(HALO_MOVES)]
    columns, corners, slots, send_sem, recv_sem, local_sem, halo_send, halo_recv = refs[
        n_block + n_corner + 1 + len(HALO_MOVES) :
    ]
    levels, rows, cols = blocks[0].shape
    gx = lax.axis_index("gx")
    gy = lax.axis_index("gy")
    me = gx * n_gy + gy
    barrier = greet(n_gy, n_dev, me)
    for field, block_ref in enumerate(blocks):
        for level in range(levels):
            turned = block_ref[level].T
            depth = field * levels + level
            columns[0, depth] = turned[cols - m :]
            columns[1, depth] = turned[:m]
            for index, (side, window) in enumerate(
                ((cols - m, rows - m), (0, rows - m), (cols - m, 0), (0, 0))
            ):
                corners[index, depth] = turned[side : side + m, window : window + m]
    pl.semaphore_wait(barrier, n_dev - 1)
    local = pltpu.make_async_copy(info_ref, slots.at[pl.ds(me, 1)], local_sem)
    local.start()
    parts = lambda window: [
        (block_ref.at[:, window, :], pl.ds(field * levels, levels))
        for field, block_ref in enumerate(blocks)
    ]
    whole = pl.ds(0, n_block * levels)
    sources = (
        parts(pl.ds(rows - m, m)),
        parts(pl.ds(0, m)),
        [(columns.at[0], whole)],
        [(columns.at[1], whole)],
    ) + tuple([(corners.at[index], whole)] for index in range(len(HALO_MOVES) - 4))
    waits = []
    for index, (dx, dy) in enumerate(HALO_MOVES):
        target = (lax.rem(gx + dx + n_gx, n_gx), lax.rem(gy + dy + n_gy, n_gy))
        for source, depth in sources[index]:
            pltpu.make_async_remote_copy(
                source,
                landed[index].at[depth],
                halo_send.at[index],
                halo_recv.at[index],
                device_id=target,
                device_id_type=MESH_ID,
            ).start()
        waits.append(
            pltpu.make_async_remote_copy(
                landed[index],
                landed[index],
                halo_send.at[index],
                halo_recv.at[index],
                device_id=target,
                device_id_type=MESH_ID,
            )
        )
    every = spread_rows(n_gy, n_dev, me, lambda target: info_ref, slots, send_sem, recv_sem)
    local.wait()
    for copy in waits:
        copy.wait_send()
        copy.wait_recv()
    every.wait_send()
    every.wait_recv()
    gathered[...] = slots[...]


def open_exchange(info_row, blocks, m):
    n_gx = lax.axis_size("gx")
    n_gy = lax.axis_size("gy")
    n_dev = n_gx * n_gy
    levels, rows, cols = blocks[0].shape
    depth = levels * len(blocks)
    vmem = pl.BlockSpec(memory_space=pltpu.VMEM)
    piece_shapes = [(depth, m, cols), (depth, m, cols), (depth, m, rows), (depth, m, rows)]
    piece_shapes += [(depth, m, m)] * (len(HALO_MOVES) - 4)
    out_shape = [jax.ShapeDtypeStruct((n_dev, info_row.shape[1]), jnp.float32)] + [
        jax.ShapeDtypeStruct(shape, jnp.float32) for shape in piece_shapes
    ]
    return pl.pallas_call(
        functools.partial(open_kernel, n_gx, n_gy, m, len(blocks)),
        out_shape=out_shape,
        in_specs=[vmem] * (1 + len(blocks)),
        out_specs=[vmem] * len(out_shape),
        scratch_shapes=[
            pltpu.VMEM((2, depth, m, rows), jnp.float32),
            pltpu.VMEM((len(HALO_MOVES) - 4, depth, m, m), jnp.float32),
            pltpu.VMEM((n_dev, info_row.shape[1]), jnp.float32),
            pltpu.SemaphoreType.DMA,
            pltpu.SemaphoreType.DMA,
            pltpu.SemaphoreType.DMA,
            pltpu.SemaphoreType.DMA((len(piece_shapes),)),
            pltpu.SemaphoreType.DMA((len(piece_shapes),)),
        ],
        compiler_params=pltpu.CompilerParams(has_side_effects=True, collective_id=0),
    )(info_row, *blocks)


def column_band(landed, m, size_r, size_c, cols):
    row_low, row_high, col_low, col_high, c_ll, c_lh, c_hl, c_hh = landed
    depth = col_low.shape[0]
    width = size_c - cols
    span = -(-size_r // 128) * 128

    def edge(column, high_corner, low_corner):
        fill = jnp.zeros((depth, m, span - size_r), jnp.float32)
        return jnp.concatenate(
            [column, high_corner, low_corner, fill],
            axis=2,
        )

    fill = jnp.zeros((depth, width - 2 * m, span), jnp.float32)
    return jnp.concatenate([edge(col_high, c_hh, c_lh), fill, edge(col_low, c_hl, c_ll)], axis=1)


def stencil_kernel(n_gx, n_gy, levels, steps, n_block, *refs):
    blocks = refs[:n_block]
    (
        high_ref, low_ref, band_ref, plane_ref, row_ref, col_ref, thrust_ref, gain_ref,
        lam_out, grad_out,
        ext_ref, states, lams, sens_all, sending, slots, roots, drag_ref,
        send_sem, recv_sem, local_sem,
    ) = refs[n_block:]
    n_dev = n_gx * n_gy
    me = lax.axis_index("gx") * n_gy + lax.axis_index("gy")
    barrier = greet(n_gy, n_dev, me)
    size_r, size_c = ext_ref.shape[1:]
    rows, cols = blocks[0].shape[1:]
    m = high_ref.shape[1]
    for level in range(levels):
        drag_ref[level] = gain_ref[level][:, :1] * plane_ref[...]
    for depth in range(ext_ref.shape[0]):
        ext_ref[depth, :rows, :cols] = blocks[depth // levels][depth % levels]
        ext_ref[depth, rows : rows + m, :cols] = high_ref[depth]
        ext_ref[depth, size_r - m :, :cols] = low_ref[depth]
        ext_ref[depth, :, cols:] = band_ref[depth].T[:size_r]

    def west(x):
        return pltpu.roll(x, 1, 0)

    def east(x):
        return pltpu.roll(x, size_r - 1, 0)

    def south(x):
        return pltpu.roll(x, 1, 1)

    def north(x):
        return pltpu.roll(x, size_c - 1, 1)

    def vertical(plane, level, center):
        mix = None
        if level + 1 < levels:
            mix = plane(level + 1) - center
        if level > 0:
            below = plane(level - 1) - center
            mix = below if mix is None else mix + below
        return mix

    for level in range(levels):
        states[0, level] = ext_ref[level]

    def forward(n, carry):
        for level in range(levels):
            center = states[n, level]
            root = jnp.sqrt(center * center + 1.0)
            roots[n, level] = root
            upwind = west(center)
            advect = ext_ref[levels + level]
            diffuse = ext_ref[2 * levels + level]
            states[n + 1, level] = (
                center
                + advect * (upwind - center)
                + diffuse * (east(center) + upwind + north(center) + south(center) - 4.0 * center)
                + VERTICAL_MIX * vertical(lambda l: states[n, l], level, center)
                - drag_ref[level] * (center * root)
            )
        return carry

    lax.fori_loop(0, steps - 1, forward, 0, unroll=True)
    for level in range(levels):
        last = states[steps - 1, level]
        roots[steps - 1, level] = jnp.sqrt(last * last + 1.0)
    for level in range(levels):
        lams[0, level] = ext_ref[3 * levels + level]
        sens_all[level] = jnp.zeros(sens_all.shape[1:], jnp.float32)

    def backward(i, carry):
        n = steps - 1 - i
        now = i % 2
        for level in range(levels):
            adjoint = lams[now, level]
            state = states[n, level]
            root = roots[n, level]
            sens_all[level] = sens_all[level] - adjoint * (state * root)
            flux_adv = ext_ref[levels + level] * adjoint
            flux_dif = ext_ref[2 * levels + level] * adjoint
            square = state * state
            slope = ((square + 1.0) + square) / root
            lams[1 - now, level] = (
                adjoint
                - flux_adv
                - 4.0 * flux_dif
                + (east(flux_adv + flux_dif) + west(flux_dif) + north(flux_dif) + south(flux_dif))
                + VERTICAL_MIX * vertical(lambda l: lams[now, l], level, adjoint)
                - drag_ref[level] * slope * adjoint
            )
        return carry

    lax.fori_loop(0, steps, backward, 0, unroll=True)
    weighted = gain_ref[0] * sens_all[0, :rows, :cols]
    for level in range(1, levels):
        weighted = weighted + gain_ref[level] * sens_all[level, :rows, :cols]
    sending[...] = jnp.zeros(sending.shape, jnp.float32)
    for slot in range(row_ref.shape[0]):
        across = jnp.dot(
            weighted, col_ref[slot], precision=HIGHEST, preferred_element_type=jnp.float32
        )
        totals = jnp.sum(row_ref[slot] * across, axis=0, keepdims=True)
        sending[slot : slot + 1, :] = thrust_ref[slot] * totals
    sending[...] = sending[...].T
    pl.semaphore_wait(barrier, n_dev - 1)
    local = pltpu.make_async_copy(sending.at[pl.ds(me, 1)], slots.at[pl.ds(me, 1)], local_sem)
    local.start()
    every = spread_rows(
        n_gy, n_dev, me, lambda target: sending.at[pl.ds(target, 1)], slots, send_sem, recv_sem
    )
    local.wait()
    every.wait_send()
    every.wait_recv()
    grad_out[...] = jnp.sum(slots[...], axis=0, keepdims=True)
    for level in range(levels):
        lam_out[level] = lams[steps % 2, level, :rows, :cols]


def stencil(blocks, landed, band, drag, levels, row_prof, col_prof, thrust_rows, gain_rows):
    size_r, size_c = drag.shape
    depth = levels * len(blocks)
    vmem = pl.BlockSpec(memory_space=pltpu.VMEM)
    plane = jax.ShapeDtypeStruct(blocks[0].shape, jnp.float32)
    n_gx = lax.axis_size("gx")
    n_gy = lax.axis_size("gy")
    n_dev = n_gx * n_gy
    width = row_prof.shape[2]
    cells = levels * size_r * size_c
    return pl.pallas_call(
        functools.partial(stencil_kernel, n_gx, n_gy, levels, STEPS, len(blocks)),
        out_shape=[plane, jax.ShapeDtypeStruct((1, width), jnp.float32)],
        in_specs=[vmem] * (len(blocks) + 8),
        out_specs=[vmem, vmem],
        scratch_shapes=[
            pltpu.VMEM((depth, size_r, size_c), jnp.float32),
            pltpu.VMEM((STEPS, levels, size_r, size_c), jnp.float32),
            pltpu.VMEM((2, levels, size_r, size_c), jnp.float32),
            pltpu.VMEM((levels, size_r, size_c), jnp.float32),
            pltpu.VMEM((width, width), jnp.float32),
            pltpu.VMEM((n_dev, width), jnp.float32),
            pltpu.VMEM((STEPS, levels, size_r, size_c), jnp.float32),
            pltpu.VMEM((levels, size_r, size_c), jnp.float32),
            pltpu.SemaphoreType.DMA,
            pltpu.SemaphoreType.DMA,
            pltpu.SemaphoreType.DMA,
        ],
        compiler_params=pltpu.CompilerParams(
            vmem_limit_bytes=48 * 1024 * 1024, has_side_effects=True, collective_id=1
        ),
        cost_estimate=pl.CostEstimate(
            flops=60 * STEPS * cells, transcendentals=3 * STEPS * cells, bytes_accessed=28 * cells
        ),
    )(*blocks, landed[1], landed[0], band, drag, row_prof, col_prof, thrust_rows, gain_rows)


def drag_law(state):
    return state * jnp.sqrt(state * state + 1.0)


def drag_slope(state):
    square_one = state * state + 1.0
    return (square_one + state * state) / jnp.sqrt(square_one)


def vertical(center):
    zero_row = jnp.zeros_like(center[:1])
    from_above = jnp.concatenate([center[1:] - center[:-1], zero_row], axis=0)
    from_below = jnp.concatenate([zero_row, center[:-1] - center[1:]], axis=0)
    return from_above + from_below


def advance(padded, advect, diffuse, drag_coef):
    center = padded[:, 1:-1, 1:-1]
    upwind = padded[:, :-2, 1:-1]
    downwind = padded[:, 2:, 1:-1]
    left_cell = padded[:, 1:-1, :-2]
    right_cell = padded[:, 1:-1, 2:]
    return (
        center
        + advect * (upwind - center)
        + diffuse * (downwind + upwind + right_cell + left_cell - 4.0 * center)
        + VERTICAL_MIX * vertical(center)
        - drag_coef * drag_law(center)
    )


def retreat(padded, advect_ext, diffuse_ext, drag_coef, state):
    flux_adv = advect_ext * padded
    flux_dif = diffuse_ext * padded
    center = padded[:, 1:-1, 1:-1]
    return (
        center
        - flux_adv[:, 1:-1, 1:-1]
        - 4.0 * flux_dif[:, 1:-1, 1:-1]
        + flux_adv[:, 2:, 1:-1]
        + (
            flux_dif[:, 2:, 1:-1]
            + flux_dif[:, :-2, 1:-1]
            + flux_dif[:, 1:-1, 2:]
            + flux_dif[:, 1:-1, :-2]
        )
        + VERTICAL_MIX * vertical(center)
        - drag_coef * drag_slope(state) * center
    )


def trim(array, margin, wanted):
    excess = margin - wanted
    if excess == 0:
        return array
    return array[:, excess:-excess, excess:-excess]


def profiles(first, starts, widths, period, length, inner):
    cells = jnp.arange(length, dtype=jnp.int32)
    cells = jnp.where(cells < inner, cells, cells - length)
    pos = (first + cells - starts[..., None]) % period
    cell_pos = pos.astype(jnp.float32) - (FP - 1) / 2.0
    profile = jnp.exp(-(cell_pos * cell_pos) / (2.0 * widths[..., None] * widths[..., None]))
    return jnp.where(pos < FP, profile, 0.0)


def level_gain():
    level_pos = jnp.arange(LEV, dtype=jnp.float32) - (LEV - 1) / 2.0
    return DRAG_SCALE * jnp.exp(-0.5 * level_pos * level_pos)


def shards(
    velocity, adjoint_seed, courant, viscosity, turbine_tile, turbine_offset, thrust, disk_width
):
    levels, rows, cols = velocity.shape
    n_gx = lax.axis_size("gx")
    n_gy = lax.axis_size("gy")
    m = MARGIN
    per = thrust.shape[0]
    fields = (
        turbine_tile[:, 0].astype(jnp.float32),
        turbine_offset[:, 0].astype(jnp.float32),
        turbine_offset[:, 1].astype(jnp.float32),
        thrust,
        disk_width,
    )
    spare = jnp.zeros((128 - len(fields) * per,), jnp.float32)
    info_row = jnp.concatenate(fields + (spare,))[None, :]
    blocks = (velocity, courant, viscosity, adjoint_seed)
    opened = open_exchange(info_row, blocks, m)
    info = opened[0]
    tiles = info[:, 0:per].astype(jnp.int32)
    row_start = tiles // n_gy * rows + info[:, per : 2 * per].astype(jnp.int32)
    col_start = tiles % n_gy * cols + info[:, 2 * per : 3 * per].astype(jnp.int32)
    thrusts = info[:, 3 * per : 4 * per]
    widths = info[:, 4 * per : 5 * per]
    gx = lax.axis_index("gx")
    gy = lax.axis_index("gy")
    size_r = -(-(rows + 2 * m) // 8) * 8
    size_c = -(-(cols + 2 * m) // 128) * 128
    inner_r = rows + (size_r - rows) // 2
    inner_c = cols + (size_c - cols) // 2
    prof_r = profiles(gx * rows, row_start, widths, n_gx * rows, size_r, inner_r)
    prof_c = profiles(gy * cols, col_start, widths, n_gy * cols, size_c, inner_c)
    gain = level_gain()
    plane = jnp.einsum("dkr,dkc->rc", thrusts[..., None] * prof_r, prof_c, precision=HIGHEST)
    band = column_band(opened[1:], m, size_r, size_c, cols)
    spare = ((0, 0), (0, 0), (0, -(-n_gx * n_gy // 128) * 128 - n_gx * n_gy))
    row_prof = jnp.pad(jnp.transpose(prof_r[..., :rows], (1, 2, 0)), spare)
    col_prof = jnp.pad(jnp.transpose(prof_c[..., :cols], (1, 2, 0)), spare)
    thrust_rows = jnp.pad(jnp.transpose(thrusts)[:, None, :], spare)
    gain_rows = jnp.broadcast_to(gain[:, None, None], (levels, 1, cols))
    adjoint, grad = stencil(
        blocks, opened[1:], band, plane, levels, row_prof, col_prof, thrust_rows, gain_rows
    )
    return adjoint, grad[0, :per]


def solution(mesh):
    placed = (
        P(None, "gx", "gy"),
        P(None, "gx", "gy"),
        P(None, "gx", "gy"),
        P(None, "gx", "gy"),
        P(("gx", "gy"), None),
        P(("gx", "gy"), None),
        P(("gx", "gy")),
        P(("gx", "gy")),
    )
    return jax.shard_map(
        shards,
        mesh=mesh,
        in_specs=placed,
        out_specs=(P(None, "gx", "gy"), P(("gx", "gy"))),
        check_vma=False,
    )
```

```python
import functools

import jax
import jax.numpy as jnp
from jax import lax
from jax.experimental import pallas as pl
from jax.experimental.pallas import tpu as pltpu
from jax.sharding import PartitionSpec as P

LEV = 3
STEPS = 8
FP = 64
MARGIN = 2 * STEPS

VERTICAL_MIX = 0.05
DRAG_SCALE = 0.01
HIGHEST = lax.Precision.HIGHEST


MESH_ID = pl.DeviceIdType.MESH


HALO_MOVES = ((1, 0), (-1, 0), (0, 1), (0, -1), (1, 1), (1, -1), (-1, 1), (-1, -1))


def greet(n_gy, n_dev, me):
    barrier = pltpu.get_barrier_semaphore()
    for step in range(1, n_dev):
        target = lax.rem(me + step, n_dev)
        pl.semaphore_signal(
            barrier, inc=1, device_id=(target // n_gy, target % n_gy), device_id_type=MESH_ID
        )
    return barrier


def spread_rows(n_gy, n_dev, me, src_of, slots, send_sem, recv_sem):
    for step in range(1, n_dev):
        target = lax.rem(me + step, n_dev)
        pltpu.make_async_remote_copy(
            src_of(target),
            slots.at[pl.ds(me, 1)],
            send_sem,
            recv_sem,
            device_id=(target // n_gy, target % n_gy),
            device_id_type=MESH_ID,
        ).start()
    first = lax.rem(me + 1, n_dev)
    rest = pl.ds(0, n_dev - 1)
    return pltpu.make_async_remote_copy(
        slots.at[rest],
        slots.at[rest],
        send_sem,
        recv_sem,
        device_id=(first // n_gy, first % n_gy),
        device_id_type=MESH_ID,
    )


def open_kernel(n_gx, n_gy, m, n_block, info_ref, *refs):
    n_dev = n_gx * n_gy
    n_corner = 0
    blocks = refs[:n_block]
    gathered = refs[n_block + n_corner]
    landed = refs[n_block + n_corner + 1 : n_block + n_corner + 1 + len(HALO_MOVES)]
    columns, corners, slots, send_sem, recv_sem, local_sem, halo_send, halo_recv = refs[
        n_block + n_corner + 1 + len(HALO_MOVES) :
    ]
    levels, rows, cols = blocks[0].shape
    gx = lax.axis_index("gx")
    gy = lax.axis_index("gy")
    me = gx * n_gy + gy
    barrier = greet(n_gy, n_dev, me)
    for field, block_ref in enumerate(blocks):
        for level in range(levels):
            turned = block_ref[level].T
            depth = field * levels + level
            columns[0, depth] = turned[cols - m :]
            columns[1, depth] = turned[:m]
            for index, (side, window) in enumerate(
                ((cols - m, rows - m), (0, rows - m), (cols - m, 0), (0, 0))
            ):
                corners[index, depth] = turned[side : side + m, window : window + m]
    pl.semaphore_wait(barrier, n_dev - 1)
    local = pltpu.make_async_copy(info_ref, slots.at[pl.ds(me, 1)], local_sem)
    local.start()
    parts = lambda window: [
        (block_ref.at[:, window, :], pl.ds(field * levels, levels))
        for field, block_ref in enumerate(blocks)
    ]
    whole = pl.ds(0, n_block * levels)
    sources = (
        parts(pl.ds(rows - m, m)),
        parts(pl.ds(0, m)),
        [(columns.at[0], whole)],
        [(columns.at[1], whole)],
    ) + tuple([(corners.at[index], whole)] for index in range(len(HALO_MOVES) - 4))
    waits = []
    for index, (dx, dy) in enumerate(HALO_MOVES):
        target = (lax.rem(gx + dx + n_gx, n_gx), lax.rem(gy + dy + n_gy, n_gy))
        for source, depth in sources[index]:
            pltpu.make_async_remote_copy(
                source,
                landed[index].at[depth],
                halo_send.at[index],
                halo_recv.at[index],
                device_id=target,
                device_id_type=MESH_ID,
            ).start()
        waits.append(
            pltpu.make_async_remote_copy(
                landed[index],
                landed[index],
                halo_send.at[index],
                halo_recv.at[index],
                device_id=target,
                device_id_type=MESH_ID,
            )
        )
    every = spread_rows(n_gy, n_dev, me, lambda target: info_ref, slots, send_sem, recv_sem)
    local.wait()
    for copy in waits:
        copy.wait_send()
        copy.wait_recv()
    every.wait_send()
    every.wait_recv()
    gathered[...] = slots[...]


def open_exchange(info_row, blocks, m):
    n_gx = lax.axis_size("gx")
    n_gy = lax.axis_size("gy")
    n_dev = n_gx * n_gy
    levels, rows, cols = blocks[0].shape
    depth = levels * len(blocks)
    vmem = pl.BlockSpec(memory_space=pltpu.VMEM)
    piece_shapes = [(depth, m, cols), (depth, m, cols), (depth, m, rows), (depth, m, rows)]
    piece_shapes += [(depth, m, m)] * (len(HALO_MOVES) - 4)
    out_shape = [jax.ShapeDtypeStruct((n_dev, info_row.shape[1]), jnp.float32)] + [
        jax.ShapeDtypeStruct(shape, jnp.float32) for shape in piece_shapes
    ]
    return pl.pallas_call(
        functools.partial(open_kernel, n_gx, n_gy, m, len(blocks)),
        out_shape=out_shape,
        in_specs=[vmem] * (1 + len(blocks)),
        out_specs=[vmem] * len(out_shape),
        scratch_shapes=[
            pltpu.VMEM((2, depth, m, rows), jnp.float32),
            pltpu.VMEM((len(HALO_MOVES) - 4, depth, m, m), jnp.float32),
            pltpu.VMEM((n_dev, info_row.shape[1]), jnp.float32),
            pltpu.SemaphoreType.DMA,
            pltpu.SemaphoreType.DMA,
            pltpu.SemaphoreType.DMA,
            pltpu.SemaphoreType.DMA((len(piece_shapes),)),
            pltpu.SemaphoreType.DMA((len(piece_shapes),)),
        ],
        compiler_params=pltpu.CompilerParams(has_side_effects=True, collective_id=0),
    )(info_row, *blocks)


def column_band(landed, m, size_r, size_c, cols):
    row_low, row_high, col_low, col_high, c_ll, c_lh, c_hl, c_hh = landed
    depth = col_low.shape[0]
    width = size_c - cols
    span = -(-size_r // 128) * 128

    def edge(column, high_corner, low_corner):
        fill = jnp.zeros((depth, m, span - size_r), jnp.float32)
        return jnp.concatenate(
            [column, high_corner, low_corner, fill],
            axis=2,
        )

    fill = jnp.zeros((depth, width - 2 * m, span), jnp.float32)
    return jnp.concatenate([edge(col_high, c_hh, c_lh), fill, edge(col_low, c_hl, c_ll)], axis=1)


def stencil_kernel(n_gx, n_gy, levels, steps, n_block, *refs):
    blocks = refs[:n_block]
    (
        high_ref, low_ref, band_ref, drag_ref, row_ref, col_ref, thrust_ref, gain_ref,
        lam_out, grad_out,
        ext_ref, states, lams, sens_all, sending, slots, roots, send_sem, recv_sem, local_sem,
    ) = refs[n_block:]
    n_dev = n_gx * n_gy
    me = lax.axis_index("gx") * n_gy + lax.axis_index("gy")
    barrier = greet(n_gy, n_dev, me)
    size_r, size_c = ext_ref.shape[1:]
    rows, cols = blocks[0].shape[1:]
    m = high_ref.shape[1]
    for depth in range(ext_ref.shape[0]):
        ext_ref[depth, :rows, :cols] = blocks[depth // levels][depth % levels]
        ext_ref[depth, rows : rows + m, :cols] = high_ref[depth]
        ext_ref[depth, size_r - m :, :cols] = low_ref[depth]
        ext_ref[depth, :, cols:] = band_ref[depth].T[:size_r]

    def west(x):
        return pltpu.roll(x, 1, 0)

    def east(x):
        return pltpu.roll(x, size_r - 1, 0)

    def south(x):
        return pltpu.roll(x, 1, 1)

    def north(x):
        return pltpu.roll(x, size_c - 1, 1)

    def vertical(plane, level, center):
        mix = None
        if level + 1 < levels:
            mix = plane(level + 1) - center
        if level > 0:
            below = plane(level - 1) - center
            mix = below if mix is None else mix + below
        return mix

    for level in range(levels):
        states[0, level] = ext_ref[level]

    def forward(n, carry):
        for level in range(levels):
            center = states[n, level]
            root = jnp.sqrt(center * center + 1.0)
            roots[n, level] = root
            upwind = west(center)
            advect = ext_ref[levels + level]
            diffuse = ext_ref[2 * levels + level]
            states[n + 1, level] = (
                center
                + advect * (upwind - center)
                + diffuse * (east(center) + upwind + north(center) + south(center) - 4.0 * center)
                + VERTICAL_MIX * vertical(lambda l: states[n, l], level, center)
                - drag_ref[level] * (center * root)
            )
        return carry

    lax.fori_loop(0, steps - 1, forward, 0, unroll=True)
    for level in range(levels):
        last = states[steps - 1, level]
        roots[steps - 1, level] = jnp.sqrt(last * last + 1.0)
    for level in range(levels):
        lams[0, level] = ext_ref[3 * levels + level]
        sens_all[level] = jnp.zeros(sens_all.shape[1:], jnp.float32)

    def backward(i, carry):
        n = steps - 1 - i
        now = i % 2
        for level in range(levels):
            adjoint = lams[now, level]
            state = states[n, level]
            root = roots[n, level]
            sens_all[level] = sens_all[level] - adjoint * (state * root)
            flux_adv = ext_ref[levels + level] * adjoint
            flux_dif = ext_ref[2 * levels + level] * adjoint
            square = state * state
            slope = ((square + 1.0) + square) * lax.rsqrt(square + 1.0)
            lams[1 - now, level] = (
                adjoint
                - flux_adv
                - 4.0 * flux_dif
                + (east(flux_adv + flux_dif) + west(flux_dif) + north(flux_dif) + south(flux_dif))
                + VERTICAL_MIX * vertical(lambda l: lams[now, l], level, adjoint)
                - drag_ref[level] * slope * adjoint
            )
        return carry

    lax.fori_loop(0, steps, backward, 0, unroll=True)
    weighted = gain_ref[0] * sens_all[0, :rows, :cols]
    for level in range(1, levels):
        weighted = weighted + gain_ref[level] * sens_all[level, :rows, :cols]
    sending[...] = jnp.zeros(sending.shape, jnp.float32)
    for slot in range(row_ref.shape[0]):
        across = jnp.dot(
            weighted, col_ref[slot], precision=HIGHEST, preferred_element_type=jnp.float32
        )
        totals = jnp.sum(row_ref[slot] * across, axis=0, keepdims=True)
        sending[slot : slot + 1, :] = thrust_ref[slot] * totals
    sending[...] = sending[...].T
    pl.semaphore_wait(barrier, n_dev - 1)
    local = pltpu.make_async_copy(sending.at[pl.ds(me, 1)], slots.at[pl.ds(me, 1)], local_sem)
    local.start()
    every = spread_rows(
        n_gy, n_dev, me, lambda target: sending.at[pl.ds(target, 1)], slots, send_sem, recv_sem
    )
    local.wait()
    every.wait_send()
    every.wait_recv()
    grad_out[...] = jnp.sum(slots[...], axis=0, keepdims=True)
    for level in range(levels):
        lam_out[level] = lams[steps % 2, level, :rows, :cols]


def stencil(blocks, landed, band, drag, levels, row_prof, col_prof, thrust_rows, gain_rows):
    size_r, size_c = drag.shape[1:]
    depth = levels * len(blocks)
    vmem = pl.BlockSpec(memory_space=pltpu.VMEM)
    plane = jax.ShapeDtypeStruct(blocks[0].shape, jnp.float32)
    n_gx = lax.axis_size("gx")
    n_gy = lax.axis_size("gy")
    n_dev = n_gx * n_gy
    width = row_prof.shape[2]
    cells = levels * size_r * size_c
    return pl.pallas_call(
        functools.partial(stencil_kernel, n_gx, n_gy, levels, STEPS, len(blocks)),
        out_shape=[plane, jax.ShapeDtypeStruct((1, width), jnp.float32)],
        in_specs=[vmem] * (len(blocks) + 8),
        out_specs=[vmem, vmem],
        scratch_shapes=[
            pltpu.VMEM((depth, size_r, size_c), jnp.float32),
            pltpu.VMEM((STEPS, levels, size_r, size_c), jnp.float32),
            pltpu.VMEM((2, levels, size_r, size_c), jnp.float32),
            pltpu.VMEM((levels, size_r, size_c), jnp.float32),
            pltpu.VMEM((width, width), jnp.float32),
            pltpu.VMEM((n_dev, width), jnp.float32),
            pltpu.VMEM((STEPS, levels, size_r, size_c), jnp.float32),
            pltpu.SemaphoreType.DMA,
            pltpu.SemaphoreType.DMA,
            pltpu.SemaphoreType.DMA,
        ],
        compiler_params=pltpu.CompilerParams(
            vmem_limit_bytes=48 * 1024 * 1024, has_side_effects=True, collective_id=1
        ),
        cost_estimate=pl.CostEstimate(
            flops=60 * STEPS * cells, transcendentals=3 * STEPS * cells, bytes_accessed=28 * cells
        ),
    )(*blocks, landed[1], landed[0], band, drag, row_prof, col_prof, thrust_rows, gain_rows)


def drag_law(state):
    return state * jnp.sqrt(state * state + 1.0)


def drag_slope(state):
    square_one = state * state + 1.0
    return (square_one + state * state) / jnp.sqrt(square_one)


def vertical(center):
    zero_row = jnp.zeros_like(center[:1])
    from_above = jnp.concatenate([center[1:] - center[:-1], zero_row], axis=0)
    from_below = jnp.concatenate([zero_row, center[:-1] - center[1:]], axis=0)
    return from_above + from_below


def advance(padded, advect, diffuse, drag_coef):
    center = padded[:, 1:-1, 1:-1]
    upwind = padded[:, :-2, 1:-1]
    downwind = padded[:, 2:, 1:-1]
    left_cell = padded[:, 1:-1, :-2]
    right_cell = padded[:, 1:-1, 2:]
    return (
        center
        + advect * (upwind - center)
        + diffuse * (downwind + upwind + right_cell + left_cell - 4.0 * center)
        + VERTICAL_MIX * vertical(center)
        - drag_coef * drag_law(center)
    )


def retreat(padded, advect_ext, diffuse_ext, drag_coef, state):
    flux_adv = advect_ext * padded
    flux_dif = diffuse_ext * padded
    center = padded[:, 1:-1, 1:-1]
    return (
        center
        - flux_adv[:, 1:-1, 1:-1]
        - 4.0 * flux_dif[:, 1:-1, 1:-1]
        + flux_adv[:, 2:, 1:-1]
        + (
            flux_dif[:, 2:, 1:-1]
            + flux_dif[:, :-2, 1:-1]
            + flux_dif[:, 1:-1, 2:]
            + flux_dif[:, 1:-1, :-2]
        )
        + VERTICAL_MIX * vertical(center)
        - drag_coef * drag_slope(state) * center
    )


def trim(array, margin, wanted):
    excess = margin - wanted
    if excess == 0:
        return array
    return array[:, excess:-excess, excess:-excess]


def profiles(first, starts, widths, period, length, inner):
    cells = jnp.arange(length, dtype=jnp.int32)
    cells = jnp.where(cells < inner, cells, cells - length)
    pos = (first + cells - starts[..., None]) % period
    cell_pos = pos.astype(jnp.float32) - (FP - 1) / 2.0
    profile = jnp.exp(-(cell_pos * cell_pos) / (2.0 * widths[..., None] * widths[..., None]))
    return jnp.where(pos < FP, profile, 0.0)


def level_gain():
    level_pos = jnp.arange(LEV, dtype=jnp.float32) - (LEV - 1) / 2.0
    return DRAG_SCALE * jnp.exp(-0.5 * level_pos * level_pos)


def shards(
    velocity, adjoint_seed, courant, viscosity, turbine_tile, turbine_offset, thrust, disk_width
):
    levels, rows, cols = velocity.shape
    n_gx = lax.axis_size("gx")
    n_gy = lax.axis_size("gy")
    m = MARGIN
    per = thrust.shape[0]
    fields = (
        turbine_tile[:, 0].astype(jnp.float32),
        turbine_offset[:, 0].astype(jnp.float32),
        turbine_offset[:, 1].astype(jnp.float32),
        thrust,
        disk_width,
    )
    spare = jnp.zeros((128 - len(fields) * per,), jnp.float32)
    info_row = jnp.concatenate(fields + (spare,))[None, :]
    blocks = (velocity, courant, viscosity, adjoint_seed)
    opened = open_exchange(info_row, blocks, m)
    info = opened[0]
    tiles = info[:, 0:per].astype(jnp.int32)
    row_start = tiles // n_gy * rows + info[:, per : 2 * per].astype(jnp.int32)
    col_start = tiles % n_gy * cols + info[:, 2 * per : 3 * per].astype(jnp.int32)
    thrusts = info[:, 3 * per : 4 * per]
    widths = info[:, 4 * per : 5 * per]
    gx = lax.axis_index("gx")
    gy = lax.axis_index("gy")
    size_r = -(-(rows + 2 * m) // 8) * 8
    size_c = -(-(cols + 2 * m) // 128) * 128
    inner_r = rows + (size_r - rows) // 2
    inner_c = cols + (size_c - cols) // 2
    prof_r = profiles(gx * rows, row_start, widths, n_gx * rows, size_r, inner_r)
    prof_c = profiles(gy * cols, col_start, widths, n_gy * cols, size_c, inner_c)
    gain = level_gain()
    plane = jnp.einsum("dkr,dkc->rc", thrusts[..., None] * prof_r, prof_c, precision=HIGHEST)
    drag = gain[:, None, None] * plane[None]
    band = column_band(opened[1:], m, size_r, size_c, cols)
    spare = ((0, 0), (0, 0), (0, -(-n_gx * n_gy // 128) * 128 - n_gx * n_gy))
    row_prof = jnp.pad(jnp.transpose(prof_r[..., :rows], (1, 2, 0)), spare)
    col_prof = jnp.pad(jnp.transpose(prof_c[..., :cols], (1, 2, 0)), spare)
    thrust_rows = jnp.pad(jnp.transpose(thrusts)[:, None, :], spare)
    gain_rows = jnp.broadcast_to(gain[:, None, None], (levels, 1, cols))
    adjoint, grad = stencil(
        blocks, opened[1:], band, drag, levels, row_prof, col_prof, thrust_rows, gain_rows
    )
    return adjoint, grad[0, :per]


def solution(mesh):
    placed = (
        P(None, "gx", "gy"),
        P(None, "gx", "gy"),
        P(None, "gx", "gy"),
        P(None, "gx", "gy"),
        P(("gx", "gy"), None),
        P(("gx", "gy"), None),
        P(("gx", "gy")),
        P(("gx", "gy")),
    )
    return jax.shard_map(
        shards,
        mesh=mesh,
        in_specs=placed,
        out_specs=(P(None, "gx", "gy"), P(("gx", "gy"))),
        check_vma=False,
    )
```

```python
import functools

import jax
import jax.numpy as jnp
from jax import lax
from jax.experimental import pallas as pl
from jax.experimental.pallas import tpu as pltpu
from jax.sharding import PartitionSpec as P

LEV = 3
STEPS = 8
FP = 64
MARGIN = 2 * STEPS

VERTICAL_MIX = 0.05
DRAG_SCALE = 0.01
HIGHEST = lax.Precision.HIGHEST


MESH_ID = pl.DeviceIdType.MESH


HALO_MOVES = ((1, 0), (-1, 0), (0, 1), (0, -1), (1, 1), (1, -1), (-1, 1), (-1, -1))


def greet(n_gy, n_dev, me):
    barrier = pltpu.get_barrier_semaphore()
    for step in range(1, n_dev):
        target = lax.rem(me + step, n_dev)
        pl.semaphore_signal(
            barrier, inc=1, device_id=(target // n_gy, target % n_gy), device_id_type=MESH_ID
        )
    return barrier


def spread_rows(n_gy, n_dev, me, src_of, slots, send_sem, recv_sem):
    for step in range(1, n_dev):
        target = lax.rem(me + step, n_dev)
        pltpu.make_async_remote_copy(
            src_of(target),
            slots.at[pl.ds(me, 1)],
            send_sem,
            recv_sem,
            device_id=(target // n_gy, target % n_gy),
            device_id_type=MESH_ID,
        ).start()
    first = lax.rem(me + 1, n_dev)
    rest = pl.ds(0, n_dev - 1)
    return pltpu.make_async_remote_copy(
        slots.at[rest],
        slots.at[rest],
        send_sem,
        recv_sem,
        device_id=(first // n_gy, first % n_gy),
        device_id_type=MESH_ID,
    )


def open_kernel(n_gx, n_gy, m, n_block, info_ref, *refs):
    n_dev = n_gx * n_gy
    n_corner = 0
    blocks = refs[:n_block]
    gathered = refs[n_block + n_corner]
    landed = refs[n_block + n_corner + 1 : n_block + n_corner + 1 + len(HALO_MOVES)]
    columns, corners, slots, send_sem, recv_sem, local_sem, halo_send, halo_recv = refs[
        n_block + n_corner + 1 + len(HALO_MOVES) :
    ]
    levels, rows, cols = blocks[0].shape
    gx = lax.axis_index("gx")
    gy = lax.axis_index("gy")
    me = gx * n_gy + gy
    barrier = greet(n_gy, n_dev, me)
    for field, block_ref in enumerate(blocks):
        for level in range(levels):
            turned = block_ref[level].T
            depth = field * levels + level
            columns[0, depth] = turned[cols - m :]
            columns[1, depth] = turned[:m]
            for index, (side, window) in enumerate(
                ((cols - m, rows - m), (0, rows - m), (cols - m, 0), (0, 0))
            ):
                corners[index, depth] = turned[side : side + m, window : window + m]
    pl.semaphore_wait(barrier, n_dev - 1)
    local = pltpu.make_async_copy(info_ref, slots.at[pl.ds(me, 1)], local_sem)
    local.start()
    parts = lambda window: [
        (block_ref.at[:, window, :], pl.ds(field * levels, levels))
        for field, block_ref in enumerate(blocks)
    ]
    whole = pl.ds(0, n_block * levels)
    sources = (
        parts(pl.ds(rows - m, m)),
        parts(pl.ds(0, m)),
        [(columns.at[0], whole)],
        [(columns.at[1], whole)],
    ) + tuple([(corners.at[index], whole)] for index in range(len(HALO_MOVES) - 4))
    waits = []
    for index in (2, 3, 4, 5, 6, 7, 0, 1):
        dx, dy = HALO_MOVES[index]
        target = (lax.rem(gx + dx + n_gx, n_gx), lax.rem(gy + dy + n_gy, n_gy))
        for source, depth in sources[index]:
            pltpu.make_async_remote_copy(
                source,
                landed[index].at[depth],
                halo_send.at[index],
                halo_recv.at[index],
                device_id=target,
                device_id_type=MESH_ID,
            ).start()
        waits.append(
            pltpu.make_async_remote_copy(
                landed[index],
                landed[index],
                halo_send.at[index],
                halo_recv.at[index],
                device_id=target,
                device_id_type=MESH_ID,
            )
        )
    every = spread_rows(n_gy, n_dev, me, lambda target: info_ref, slots, send_sem, recv_sem)
    local.wait()
    for copy in waits:
        copy.wait_send()
        copy.wait_recv()
    every.wait_send()
    every.wait_recv()
    gathered[...] = slots[...]


def open_exchange(info_row, blocks, m):
    n_gx = lax.axis_size("gx")
    n_gy = lax.axis_size("gy")
    n_dev = n_gx * n_gy
    levels, rows, cols = blocks[0].shape
    depth = levels * len(blocks)
    vmem = pl.BlockSpec(memory_space=pltpu.VMEM)
    piece_shapes = [(depth, m, cols), (depth, m, cols), (depth, m, rows), (depth, m, rows)]
    piece_shapes += [(depth, m, m)] * (len(HALO_MOVES) - 4)
    out_shape = [jax.ShapeDtypeStruct((n_dev, info_row.shape[1]), jnp.float32)] + [
        jax.ShapeDtypeStruct(shape, jnp.float32) for shape in piece_shapes
    ]
    return pl.pallas_call(
        functools.partial(open_kernel, n_gx, n_gy, m, len(blocks)),
        out_shape=out_shape,
        in_specs=[vmem] * (1 + len(blocks)),
        out_specs=[vmem] * len(out_shape),
        scratch_shapes=[
            pltpu.VMEM((2, depth, m, rows), jnp.float32),
            pltpu.VMEM((len(HALO_MOVES) - 4, depth, m, m), jnp.float32),
            pltpu.VMEM((n_dev, info_row.shape[1]), jnp.float32),
            pltpu.SemaphoreType.DMA,
            pltpu.SemaphoreType.DMA,
            pltpu.SemaphoreType.DMA,
            pltpu.SemaphoreType.DMA((len(piece_shapes),)),
            pltpu.SemaphoreType.DMA((len(piece_shapes),)),
        ],
        compiler_params=pltpu.CompilerParams(has_side_effects=True, collective_id=0),
    )(info_row, *blocks)


def column_band(landed, m, size_r, size_c, cols):
    row_low, row_high, col_low, col_high, c_ll, c_lh, c_hl, c_hh = landed
    depth = col_low.shape[0]
    width = size_c - cols
    span = -(-size_r // 128) * 128

    def edge(column, high_corner, low_corner):
        fill = jnp.zeros((depth, m, span - size_r), jnp.float32)
        return jnp.concatenate(
            [column, high_corner, low_corner, fill],
            axis=2,
        )

    fill = jnp.zeros((depth, width - 2 * m, span), jnp.float32)
    return jnp.concatenate([edge(col_high, c_hh, c_lh), fill, edge(col_low, c_hl, c_ll)], axis=1)


def stencil_kernel(n_gx, n_gy, levels, steps, n_block, *refs):
    blocks = refs[:n_block]
    (
        high_ref, low_ref, band_ref, drag_ref, row_ref, col_ref, thrust_ref, gain_ref,
        lam_out, grad_out,
        ext_ref, states, lams, sens_all, sending, slots, roots, send_sem, recv_sem, local_sem,
    ) = refs[n_block:]
    n_dev = n_gx * n_gy
    me = lax.axis_index("gx") * n_gy + lax.axis_index("gy")
    barrier = greet(n_gy, n_dev, me)
    size_r, size_c = ext_ref.shape[1:]
    rows, cols = blocks[0].shape[1:]
    m = high_ref.shape[1]
    for depth in range(ext_ref.shape[0]):
        ext_ref[depth, :rows, :cols] = blocks[depth // levels][depth % levels]
        ext_ref[depth, rows : rows + m, :cols] = high_ref[depth]
        ext_ref[depth, size_r - m :, :cols] = low_ref[depth]
        ext_ref[depth, :, cols:] = band_ref[depth].T[:size_r]

    def west(x):
        return pltpu.roll(x, 1, 0)

    def east(x):
        return pltpu.roll(x, size_r - 1, 0)

    def south(x):
        return pltpu.roll(x, 1, 1)

    def north(x):
        return pltpu.roll(x, size_c - 1, 1)

    def vertical(plane, level, center):
        mix = None
        if level + 1 < levels:
            mix = plane(level + 1) - center
        if level > 0:
            below = plane(level - 1) - center
            mix = below if mix is None else mix + below
        return mix

    for level in range(levels):
        states[0, level] = ext_ref[level]

    def forward(n, carry):
        for level in range(levels):
            center = states[n, level]
            root = jnp.sqrt(center * center + 1.0)
            roots[n, level] = root
            upwind = west(center)
            advect = ext_ref[levels + level]
            diffuse = ext_ref[2 * levels + level]
            states[n + 1, level] = (
                center
                + advect * (upwind - center)
                + diffuse * (east(center) + upwind + north(center) + south(center) - 4.0 * center)
                + VERTICAL_MIX * vertical(lambda l: states[n, l], level, center)
                - drag_ref[level] * (center * root)
            )
        return carry

    lax.fori_loop(0, steps - 1, forward, 0, unroll=True)
    for level in range(levels):
        last = states[steps - 1, level]
        roots[steps - 1, level] = jnp.sqrt(last * last + 1.0)
    for level in range(levels):
        lams[0, level] = ext_ref[3 * levels + level]
        sens_all[level] = jnp.zeros(sens_all.shape[1:], jnp.float32)

    def backward(i, carry):
        n = steps - 1 - i
        now = i % 2
        for level in range(levels):
            adjoint = lams[now, level]
            state = states[n, level]
            root = roots[n, level]
            sens_all[level] = sens_all[level] - adjoint * (state * root)
            flux_adv = ext_ref[levels + level] * adjoint
            flux_dif = ext_ref[2 * levels + level] * adjoint
            square = state * state
            slope = ((square + 1.0) + square) / root
            lams[1 - now, level] = (
                adjoint
                - flux_adv
                - 4.0 * flux_dif
                + (east(flux_adv + flux_dif) + west(flux_dif) + north(flux_dif) + south(flux_dif))
                + VERTICAL_MIX * vertical(lambda l: lams[now, l], level, adjoint)
                - drag_ref[level] * slope * adjoint
            )
        return carry

    lax.fori_loop(0, steps, backward, 0, unroll=True)
    weighted = gain_ref[0] * sens_all[0, :rows, :cols]
    for level in range(1, levels):
        weighted = weighted + gain_ref[level] * sens_all[level, :rows, :cols]
    sending[...] = jnp.zeros(sending.shape, jnp.float32)
    for slot in range(row_ref.shape[0]):
        across = jnp.dot(
            weighted, col_ref[slot], precision=HIGHEST, preferred_element_type=jnp.float32
        )
        totals = jnp.sum(row_ref[slot] * across, axis=0, keepdims=True)
        sending[slot : slot + 1, :] = thrust_ref[slot] * totals
    sending[...] = sending[...].T
    pl.semaphore_wait(barrier, n_dev - 1)
    local = pltpu.make_async_copy(sending.at[pl.ds(me, 1)], slots.at[pl.ds(me, 1)], local_sem)
    local.start()
    every = spread_rows(
        n_gy, n_dev, me, lambda target: sending.at[pl.ds(target, 1)], slots, send_sem, recv_sem
    )
    local.wait()
    every.wait_send()
    every.wait_recv()
    grad_out[...] = jnp.sum(slots[...], axis=0, keepdims=True)
    for level in range(levels):
        lam_out[level] = lams[steps % 2, level, :rows, :cols]


def stencil(blocks, landed, band, drag, levels, row_prof, col_prof, thrust_rows, gain_rows):
    size_r, size_c = drag.shape[1:]
    depth = levels * len(blocks)
    vmem = pl.BlockSpec(memory_space=pltpu.VMEM)
    plane = jax.ShapeDtypeStruct(blocks[0].shape, jnp.float32)
    n_gx = lax.axis_size("gx")
    n_gy = lax.axis_size("gy")
    n_dev = n_gx * n_gy
    width = row_prof.shape[2]
    cells = levels * size_r * size_c
    return pl.pallas_call(
        functools.partial(stencil_kernel, n_gx, n_gy, levels, STEPS, len(blocks)),
        out_shape=[plane, jax.ShapeDtypeStruct((1, width), jnp.float32)],
        in_specs=[vmem] * (len(blocks) + 8),
        out_specs=[vmem, vmem],
        scratch_shapes=[
            pltpu.VMEM((depth, size_r, size_c), jnp.float32),
            pltpu.VMEM((STEPS, levels, size_r, size_c), jnp.float32),
            pltpu.VMEM((2, levels, size_r, size_c), jnp.float32),
            pltpu.VMEM((levels, size_r, size_c), jnp.float32),
            pltpu.VMEM((width, width), jnp.float32),
            pltpu.VMEM((n_dev, width), jnp.float32),
            pltpu.VMEM((STEPS, levels, size_r, size_c), jnp.float32),
            pltpu.SemaphoreType.DMA,
            pltpu.SemaphoreType.DMA,
            pltpu.SemaphoreType.DMA,
        ],
        compiler_params=pltpu.CompilerParams(
            vmem_limit_bytes=48 * 1024 * 1024, has_side_effects=True, collective_id=1
        ),
        cost_estimate=pl.CostEstimate(
            flops=60 * STEPS * cells, transcendentals=3 * STEPS * cells, bytes_accessed=28 * cells
        ),
    )(*blocks, landed[1], landed[0], band, drag, row_prof, col_prof, thrust_rows, gain_rows)


def drag_law(state):
    return state * jnp.sqrt(state * state + 1.0)


def drag_slope(state):
    square_one = state * state + 1.0
    return (square_one + state * state) / jnp.sqrt(square_one)


def vertical(center):
    zero_row = jnp.zeros_like(center[:1])
    from_above = jnp.concatenate([center[1:] - center[:-1], zero_row], axis=0)
    from_below = jnp.concatenate([zero_row, center[:-1] - center[1:]], axis=0)
    return from_above + from_below


def advance(padded, advect, diffuse, drag_coef):
    center = padded[:, 1:-1, 1:-1]
    upwind = padded[:, :-2, 1:-1]
    downwind = padded[:, 2:, 1:-1]
    left_cell = padded[:, 1:-1, :-2]
    right_cell = padded[:, 1:-1, 2:]
    return (
        center
        + advect * (upwind - center)
        + diffuse * (downwind + upwind + right_cell + left_cell - 4.0 * center)
        + VERTICAL_MIX * vertical(center)
        - drag_coef * drag_law(center)
    )


def retreat(padded, advect_ext, diffuse_ext, drag_coef, state):
    flux_adv = advect_ext * padded
    flux_dif = diffuse_ext * padded
    center = padded[:, 1:-1, 1:-1]
    return (
        center
        - flux_adv[:, 1:-1, 1:-1]
        - 4.0 * flux_dif[:, 1:-1, 1:-1]
        + flux_adv[:, 2:, 1:-1]
        + (
            flux_dif[:, 2:, 1:-1]
            + flux_dif[:, :-2, 1:-1]
            + flux_dif[:, 1:-1, 2:]
            + flux_dif[:, 1:-1, :-2]
        )
        + VERTICAL_MIX * vertical(center)
        - drag_coef * drag_slope(state) * center
    )


def trim(array, margin, wanted):
    excess = margin - wanted
    if excess == 0:
        return array
    return array[:, excess:-excess, excess:-excess]


def profiles(first, starts, widths, period, length, inner):
    cells = jnp.arange(length, dtype=jnp.int32)
    cells = jnp.where(cells < inner, cells, cells - length)
    pos = (first + cells - starts[..., None]) % period
    cell_pos = pos.astype(jnp.float32) - (FP - 1) / 2.0
    profile = jnp.exp(-(cell_pos * cell_pos) / (2.0 * widths[..., None] * widths[..., None]))
    return jnp.where(pos < FP, profile, 0.0)


def level_gain():
    level_pos = jnp.arange(LEV, dtype=jnp.float32) - (LEV - 1) / 2.0
    return DRAG_SCALE * jnp.exp(-0.5 * level_pos * level_pos)


def shards(
    velocity, adjoint_seed, courant, viscosity, turbine_tile, turbine_offset, thrust, disk_width
):
    levels, rows, cols = velocity.shape
    n_gx = lax.axis_size("gx")
    n_gy = lax.axis_size("gy")
    m = MARGIN
    per = thrust.shape[0]
    fields = (
        turbine_tile[:, 0].astype(jnp.float32),
        turbine_offset[:, 0].astype(jnp.float32),
        turbine_offset[:, 1].astype(jnp.float32),
        thrust,
        disk_width,
    )
    spare = jnp.zeros((128 - len(fields) * per,), jnp.float32)
    info_row = jnp.concatenate(fields + (spare,))[None, :]
    blocks = (velocity, courant, viscosity, adjoint_seed)
    opened = open_exchange(info_row, blocks, m)
    info = opened[0]
    tiles = info[:, 0:per].astype(jnp.int32)
    row_start = tiles // n_gy * rows + info[:, per : 2 * per].astype(jnp.int32)
    col_start = tiles % n_gy * cols + info[:, 2 * per : 3 * per].astype(jnp.int32)
    thrusts = info[:, 3 * per : 4 * per]
    widths = info[:, 4 * per : 5 * per]
    gx = lax.axis_index("gx")
    gy = lax.axis_index("gy")
    size_r = -(-(rows + 2 * m) // 8) * 8
    size_c = -(-(cols + 2 * m) // 128) * 128
    inner_r = rows + (size_r - rows) // 2
    inner_c = cols + (size_c - cols) // 2
    prof_r = profiles(gx * rows, row_start, widths, n_gx * rows, size_r, inner_r)
    prof_c = profiles(gy * cols, col_start, widths, n_gy * cols, size_c, inner_c)
    gain = level_gain()
    plane = jnp.einsum("dkr,dkc->rc", thrusts[..., None] * prof_r, prof_c, precision=HIGHEST)
    drag = gain[:, None, None] * plane[None]
    band = column_band(opened[1:], m, size_r, size_c, cols)
    spare = ((0, 0), (0, 0), (0, -(-n_gx * n_gy // 128) * 128 - n_gx * n_gy))
    row_prof = jnp.pad(jnp.transpose(prof_r[..., :rows], (1, 2, 0)), spare)
    col_prof = jnp.pad(jnp.transpose(prof_c[..., :cols], (1, 2, 0)), spare)
    thrust_rows = jnp.pad(jnp.transpose(thrusts)[:, None, :], spare)
    gain_rows = jnp.broadcast_to(gain[:, None, None], (levels, 1, cols))
    adjoint, grad = stencil(
        blocks, opened[1:], band, drag, levels, row_prof, col_prof, thrust_rows, gain_rows
    )
    return adjoint, grad[0, :per]


def solution(mesh):
    placed = (
        P(None, "gx", "gy"),
        P(None, "gx", "gy"),
        P(None, "gx", "gy"),
        P(None, "gx", "gy"),
        P(("gx", "gy"), None),
        P(("gx", "gy"), None),
        P(("gx", "gy")),
        P(("gx", "gy")),
    )
    return jax.shard_map(
        shards,
        mesh=mesh,
        in_specs=placed,
        out_specs=(P(None, "gx", "gy"), P(("gx", "gy"))),
        check_vma=False,
    )
```
